32 devices in a mesh: group: 2 (over y), scan: 4 (over z), tensor: 2 (over x), band: 2 (over core).
Axes of the slice: x: 2, y: 2, z: 4, core: 2. Of those that a mesh axis runs over, the one named last changes fastest.
Arguments:
- signal: bfloat16 [4096, 5120], P(('group', 'scan', 'band'), 'tensor'), parts along dimension 0, may hold values from -140 to 140
- gate_branch: bfloat16 [4096, 5120], P(('group', 'scan', 'band'), 'tensor'), parts along dimension 0, may hold values from -6 to 6
- write_proj: bfloat16 [4096, 128], P(('group', 'scan', 'band')), parts along dimension 0, may hold values from -1.796875 to 1.796875
- read_proj: bfloat16 [4096, 128], P(('group', 'scan', 'band')), parts along dimension 0, may hold values from -1.796875 to 1.796875
- step_logits: float32 [80, 4096], P('tensor', ('group', 'scan', 'band')), parts along dimension 1
- valid_mask: int32 [4096], P(('group', 'scan', 'band')), parts along dimension 0, may hold values from 0 to 1
- stretch_band: int32 [16], P(('group', 'scan', 'band')), parts along dimension 0, may hold values from 0 to 11
- band_offset: float32 [12, 80], P(None, 'tensor'), may hold values from -0.35 to 0.35
- decay_log: float32 [80], P('tensor'), may hold values from -8 to 0
- step_offset: float32 [80], P('tensor'), may hold values from -7 to -1
- skip_gain: float32 [80], P('tensor'), may hold values from 0.5 to 2
- norm_gain: float32 [5120], P('tensor'), may hold values from 0.1 to 1.9
- out_weight: bfloat16 [5120, 2560], P('tensor'), may hold values from -0.078125 to 0.078125
Outputs:
- layer_output: bfloat16 [4096, 2560], P(('group', 'scan', 'band'), 'tensor'), parts along dimension 0
The draws below stay inside these ranges and needn't reach their ends.
There are 2 independent parts, one for each index of `group`. The reference program is written for one: setup_inputs(seed, part) draws one part's arguments, and reference() takes and returns one part's arrays. A program takes and returns all parts, laid end to end along the dimension named above; an argument that names none is the same for every part. Nothing has to cross between parts.
All inputs are finite; a program needn't handle non-finite values.
Results may differ from the reference program's by a relative error of at most 0.015.
Values may be sent and summed in bfloat16 or wider, within the bound.
A program may use at most 64 MiB of HBM per device.

```python
import math
import jax
import jax.numpy as jnp
from jax import lax

WIDTH = 2560
HEADS = 80
HEAD_DIM = 64
STATE = 128
STRETCH = 256
BANDS = 12
SEQUENCE_LENGTH = 2048
STRETCHES = 8
INNER = 5120
N_TENSOR = 2


def head_params(key):
    slow_share = 0.5
    chooser = jax.random.uniform(jax.random.fold_in(key, 101), (HEADS,))
    initial_sample = jax.random.uniform(jax.random.fold_in(key, 102), (HEADS,))
    second_draw = jax.random.uniform(jax.random.fold_in(key, 103), (HEADS,))
    root_length = jnp.sqrt(jnp.float32(SEQUENCE_LENGTH))
    slow_step = 0.5 * jnp.exp(initial_sample * jnp.log(4.0)) / root_length
    slow_rate = 0.3 * jnp.exp(second_draw * jnp.log(2.0)) / root_length
    fast_step = 0.1 * jnp.exp(initial_sample * jnp.log(2.0))
    fast_rate = jnp.exp(jnp.log(1.0 / 50.0) + second_draw * jnp.log(50.0 / 30.0)) / fast_step
    is_slow = chooser < slow_share
    return (jnp.where(is_slow, slow_step, fast_step), jnp.where(is_slow, slow_rate, fast_rate))


def spike_indices(key):
    return jax.random.randint(jax.random.fold_in(key, 211), (2,), 0, SEQUENCE_LENGTH)


def draw_decay_log(key, part):
    return jnp.log(head_params(key)[1])


def draw_step_offset(key, part):
    return jnp.log(jnp.expm1(head_params(key)[0]))


def draw_valid_mask(key, part):
    coin_outcome = jax.random.randint(jax.random.fold_in(key, 212), (SEQUENCE_LENGTH,), 0, 4)
    sample_places = spike_indices(key)
    spike_indicator = jnp.any(jnp.arange(SEQUENCE_LENGTH, dtype=jnp.int32)[:, None] == sample_places[None, :], axis=1)
    return jnp.where(spike_indicator | (coin_outcome == 0), 0, 1).astype(jnp.int32)


def draw_step_logits(key, part):
    rough_part = jax.random.uniform(jax.random.fold_in(key, 213), (HEADS, SEQUENCE_LENGTH), minval=-0.7, maxval=0.7)
    intensity = jax.random.uniform(jax.random.fold_in(key, 214), (2,), minval=0.8, maxval=1.1) * jnp.sqrt(jnp.float32(SEQUENCE_LENGTH))
    sample_places = spike_indices(key)
    boost = jnp.sum(jnp.where(jnp.arange(SEQUENCE_LENGTH, dtype=jnp.int32)[:, None] == sample_places[None, :], intensity[None, :], 0.0), axis=1)
    return rough_part + boost[None, :]


def draw_signal(key, part):
    row_scale = jnp.exp(jax.random.uniform(jax.random.fold_in(key, 301), (SEQUENCE_LENGTH, 1)) * jnp.log(10.0))
    column_scale = jnp.exp(jax.random.uniform(jax.random.fold_in(key, 302), (1, INNER)) * jnp.log(10.0))
    ramp_power = 0.5
    slope_scale = jnp.exp(ramp_power * jnp.log(3.0) * jnp.arange(INNER, dtype=jnp.float32)[None, :] / (INNER - 1))
    noise_part = jnp.clip(jax.random.normal(jax.random.fold_in(key, 303), (SEQUENCE_LENGTH, INNER)), -4.0, 4.0)
    return (0.2 * noise_part * row_scale * column_scale * slope_scale).astype(jnp.bfloat16)


def plant(values, rng, least, largest):
    longest = values.shape.index(max(values.shape))
    spots = []
    for shift in (0, 1):
        where = [jax.random.randint(jax.random.fold_in(rng, axis), (), 0, length) for axis, length in enumerate(values.shape)]
        where[longest] = (where[longest] + shift) % values.shape[longest]
        spots.append(tuple(where))
    return values.at[spots[0]].set(least).at[spots[1]].set(largest)


def level_of(key, extent, split, low, high):
    loudness, own = 1.0, jax.random.fold_in(key, 6)
    for dim, shards_of in split:
        draws = jnp.exp(jax.random.uniform(jax.random.fold_in(own, dim), (shards_of,), jnp.float32, low / len(split), high / len(split)))
        loudness = loudness * jnp.repeat(draws, extent[dim] // shards_of).reshape([-1 if axis == dim else 1 for axis in range(len(extent))])
    return loudness


def noise(stream_key, shape, scale, most, cuts=(), kind=jnp.bfloat16):
    values = scale * jax.random.normal(stream_key, shape, jnp.float32)
    if cuts:
        values = values * level_of(stream_key, shape, cuts, -0.22, 0.18)
    return jnp.clip(values, -most, most).astype(kind)


def setup_inputs(seed: int = 0, part: int = 0) -> dict:
    arg_keys = jax.random.split(jax.random.key(seed), 14)
    part_keys = jax.random.split(jax.random.fold_in(arg_keys[13], part), 14)
    return {
        "signal": draw_signal(jax.random.fold_in(jax.random.fold_in(arg_keys[13], part), 71), part),
        "gate_branch": noise(part_keys[1], (SEQUENCE_LENGTH, INNER), 1.0, 6.0, ((0, 8), (1, 2))),
        "write_proj": noise(part_keys[2], (SEQUENCE_LENGTH, STATE), 0.3, 1.796875, ((0, 8),)),
        "read_proj": noise(part_keys[3], (SEQUENCE_LENGTH, STATE), 0.3, 1.796875, ((0, 8),)),
        "step_logits": draw_step_logits(jax.random.fold_in(jax.random.fold_in(arg_keys[13], part), 71), part),
        "valid_mask": draw_valid_mask(jax.random.fold_in(jax.random.fold_in(arg_keys[13], part), 71), part),
        "stretch_band": plant(jax.random.randint(part_keys[6], (STRETCHES,), 0, BANDS), jax.random.fold_in(part_keys[6], 1), 0, BANDS - 1).astype(jnp.int32),
        "band_offset": jnp.clip(jax.random.uniform(arg_keys[7], (BANDS, HEADS), jnp.float32, -0.35, 0.35) * level_of(arg_keys[7], (BANDS, HEADS), ((1, 2),), -0.4, 0.0), -0.35, 0.35),
        "decay_log": draw_decay_log(jax.random.fold_in(arg_keys[13], 71), part),
        "step_offset": draw_step_offset(jax.random.fold_in(arg_keys[13], 71), part),
        "skip_gain": jnp.clip(jnp.exp(math.log(2.0) - 1.3862944 * jax.random.uniform(arg_keys[10], (HEADS,), jnp.float32) ** level_of(arg_keys[10], (HEADS,), ((0, 2),), -0.2, 0.2)), 0.5, 2.0),
        "norm_gain": jnp.clip(1.0 + 0.18 * jax.random.normal(arg_keys[11], (INNER,), jnp.float32), 0.1, 1.9),
        "out_weight": noise(arg_keys[12], (INNER, WIDTH), INNER ** -0.5, 0.078125, ((0, 2),)),
    }


EPSILON = 1e-05

def step_sizes(step_logits, stretch_band, band_offset, step_offset):
    one_hot = (stretch_band[:, None] == jnp.arange(BANDS, dtype=jnp.int32)[None, :]).astype(jnp.float32)
    stretch_offset = jnp.dot(one_hot, band_offset, precision=lax.Precision.HIGHEST)
    token_offset = jnp.repeat(stretch_offset, STRETCH, axis=0).T
    return jax.nn.softplus(step_logits + step_offset[:, None] + token_offset)

def split_state(state):
    state_high = state.astype(jnp.bfloat16)
    widened = lax.optimization_barrier(state_high).astype(jnp.float32)
    state_low = (state - widened).astype(jnp.bfloat16)
    return (state_high, state_low)

def stretch_pass(carry_state, pieces):
    signal_block, write_block, read_block, segment_damping, weight_block = pieces
    running = jnp.cumsum(segment_damping, axis=1)
    scores = jnp.dot(read_block, write_block.T, preferred_element_type=jnp.float32)
    lower_mask = jnp.arange(STRETCH)[:, None] >= jnp.arange(STRETCH)[None, :]
    span_logs = jnp.where(lower_mask[None], running[:, :, None] - running[:, None, :], -1e+30)
    mixing = (jnp.exp(span_logs) * scores[None] * weight_block[:, None, :]).astype(jnp.bfloat16)
    local_out = jnp.einsum('hij,jhp->ihp', mixing.astype(jnp.float32), signal_block.astype(jnp.float32), precision=lax.Precision.HIGHEST)
    state_high, state_low = split_state(carry_state)
    read_wide = read_block.astype(jnp.float32)
    high_part = jnp.einsum('in,hpn->ihp', read_wide, state_high.astype(jnp.float32), precision=lax.Precision.HIGHEST)
    low_part = jnp.einsum('in,hpn->ihp', read_wide, state_low.astype(jnp.float32), precision=lax.Precision.HIGHEST)
    carried_out = jnp.exp(running).T[:, :, None] * (high_part + low_part)
    tail_weight = jnp.exp(running[:, -1:] - running) * weight_block
    scaled = (signal_block.astype(jnp.float32) * tail_weight.T[:, :, None]).astype(jnp.bfloat16)
    stretch_state = jnp.einsum('jhp,jn->hpn', scaled.astype(jnp.float32), write_block.astype(jnp.float32), precision=lax.Precision.HIGHEST)
    next_state = jnp.exp(running[:, -1])[:, None, None] * carry_state + stretch_state
    return (next_state, local_out + carried_out)

def reference(signal, gate_branch, write_proj, read_proj, step_logits, valid_mask, stretch_band, band_offset, decay_log, step_offset, skip_gain, norm_gain, out_weight):
    step_size = step_sizes(step_logits, stretch_band, band_offset, step_offset)
    log_decay = step_size * (-jnp.exp(decay_log))[:, None]
    input_weight = step_size * valid_mask.astype(jnp.float32)[None, :]
    stretch_count = SEQUENCE_LENGTH // STRETCH
    signal_blocks = signal.reshape(stretch_count, STRETCH, HEADS, HEAD_DIM)
    write_blocks = write_proj.reshape(stretch_count, STRETCH, STATE)
    read_blocks = read_proj.reshape(stretch_count, STRETCH, STATE)
    decay_blocks = log_decay.reshape(HEADS, stretch_count, STRETCH).transpose(1, 0, 2)
    weight_blocks = input_weight.reshape(HEADS, stretch_count, STRETCH).transpose(1, 0, 2)
    start_state = jnp.zeros((HEADS, HEAD_DIM, STATE), jnp.float32)
    final_state, outputs = lax.scan(stretch_pass, start_state, (signal_blocks, write_blocks, read_blocks, decay_blocks, weight_blocks))
    ssm_out = outputs.reshape(SEQUENCE_LENGTH, HEADS, HEAD_DIM) + skip_gain[None, :, None] * signal.reshape(SEQUENCE_LENGTH, HEADS, HEAD_DIM).astype(jnp.float32)
    gated_out = ssm_out.reshape(SEQUENCE_LENGTH, INNER) * jax.nn.silu(gate_branch.astype(jnp.float32))
    mean_square = lax.optimization_barrier(jnp.mean(gated_out * gated_out, axis=1, keepdims=True))
    normed = (gated_out * lax.rsqrt(mean_square + EPSILON) * norm_gain[None, :]).astype(jnp.bfloat16)
    slice_width = INNER // N_TENSOR
    summed = jnp.zeros((SEQUENCE_LENGTH, WIDTH), jnp.float32)
    for member in range(N_TENSOR):
        partial_sum = jnp.dot(normed[:, member * slice_width:(member + 1) * slice_width], out_weight[member * slice_width:(member + 1) * slice_width], preferred_element_type=jnp.float32).astype(jnp.bfloat16)
        partial_sum = lax.optimization_barrier(partial_sum)
        summed = summed + partial_sum.astype(jnp.float32)
    return summed.astype(jnp.bfloat16)
```

```python
import functools

import jax
import jax.numpy as jnp
from jax import lax
from jax.experimental import pallas as pl
from jax.experimental.pallas import tpu as pltpu
from jax.sharding import PartitionSpec as P

HEAD_DIM = 64
STATE = 128
STRETCH = 256
BANDS = 12
INNER = 5120


EPSILON = 1e-05
HIGHEST = lax.Precision.HIGHEST


def step_sizes(step_logits, stretch_band, band_offset, step_offset):
    one_hot = (stretch_band[:, None] == jnp.arange(BANDS, dtype=jnp.int32)[None, :]).astype(
        jnp.float32
    )
    stretch_offset = jnp.dot(one_hot, band_offset, precision=HIGHEST)
    token_offset = jnp.repeat(stretch_offset, STRETCH, axis=0).T
    return jax.nn.softplus(step_logits + step_offset[:, None] + token_offset)


def combine(earlier, later_pair):
    return (
        earlier[0] + later_pair[0],
        jnp.exp(later_pair[0])[:, None, None] * earlier[1] + later_pair[1],
    )


def local_step(running_pair, member):
    return (combine(running_pair, member), running_pair)


def on_device(
    signal,
    gate_branch,
    write_proj,
    read_proj,
    step_logits,
    valid_mask,
    stretch_band,
    band_offset,
    decay_log,
    step_offset,
    skip_gain,
    norm_gain,
    out_weight,
):
    row_count = signal.shape[0]
    head_count = decay_log.shape[0]
    block_count = row_count // STRETCH
    step_size = step_sizes(step_logits, stretch_band, band_offset, step_offset)
    log_decay = step_size * (-jnp.exp(decay_log))[:, None]
    input_weight = step_size * valid_mask.astype(jnp.float32)[None, :]
    running = lax.associative_scan(
        jnp.add, log_decay.reshape(head_count, block_count, STRETCH), axis=2
    )
    weight_blocks = input_weight.reshape(head_count, block_count, STRETCH)
    signal_blocks = signal.reshape(block_count, STRETCH, head_count, HEAD_DIM)
    write_blocks = write_proj.reshape(block_count, STRETCH, STATE)
    read_blocks = read_proj.reshape(block_count, STRETCH, STATE)
    scores = jnp.einsum(
        "cin,cjn->cij", read_blocks, write_blocks, preferred_element_type=jnp.float32
    )
    lower_mask = jnp.arange(STRETCH)[:, None] >= jnp.arange(STRETCH)[None, :]
    span_logs = jnp.where(
        lower_mask[None, None], running[:, :, :, None] - running[:, :, None, :], -1e30
    )
    mixing = (jnp.exp(span_logs) * scores[None] * weight_blocks[:, :, None, :]).astype(jnp.bfloat16)
    local_out = jnp.einsum(
        "hcij,cjhp->cihp", mixing, signal_blocks, preferred_element_type=jnp.float32
    )
    tail_weight = jnp.exp(running[:, :, -1:] - running) * weight_blocks
    scaled = (
        signal_blocks.astype(jnp.float32) * jnp.transpose(tail_weight, (1, 2, 0))[:, :, :, None]
    ).astype(jnp.bfloat16)
    block_states = jnp.einsum(
        "cjhp,cjn->chpn", scaled, write_blocks, preferred_element_type=jnp.float32
    )
    block_decay = running[:, :, -1].T
    zero_state = jnp.zeros((head_count, HEAD_DIM, STATE), jnp.float32)
    zero_log = jnp.zeros((head_count,), jnp.float32)
    identity = (zero_log, zero_state)
    device_pair, segment_cumulative = lax.scan(local_step, identity, (block_decay, block_states))
    all_logs = lax.all_gather(device_pair[0][None], ("scan", "band"), axis=0, tiled=True)
    inclusive = lax.associative_scan(jnp.add, all_logs, axis=0)
    exclusive = inclusive - all_logs
    position = lax.axis_index(("scan", "band"))
    own_exclusive = lax.dynamic_index_in_dim(exclusive, position, 0, keepdims=False)
    shard_block = lax.all_gather(
        device_pair[1][None].astype(jnp.bfloat16), ("scan", "band"), axis=0, tiled=True
    ).astype(jnp.float32)
    how_many = shard_block.shape[0]
    sources = jnp.arange(how_many, dtype=jnp.int32)
    gap_logs = jnp.where((sources < position)[:, None], own_exclusive[None, :] - inclusive, -1e30)
    carry_state = zero_state + jnp.einsum(
        "kh,khpn->hpn", jnp.exp(gap_logs), shard_block, precision=HIGHEST
    )
    enter_state = (
        jnp.exp(segment_cumulative[0])[:, :, None, None] * carry_state[None] + segment_cumulative[1]
    )
    state_high = enter_state.astype(jnp.bfloat16)
    widened = lax.optimization_barrier(state_high).astype(jnp.float32)
    state_low = (enter_state - widened).astype(jnp.bfloat16)
    high_part = jnp.einsum(
        "cin,chpn->cihp", read_blocks, state_high, preferred_element_type=jnp.float32
    )
    low_part = jnp.einsum(
        "cin,chpn->cihp", read_blocks, state_low, preferred_element_type=jnp.float32
    )
    carried_out = jnp.transpose(jnp.exp(running), (1, 2, 0))[:, :, :, None] * (high_part + low_part)
    ssm_out = (local_out + carried_out).reshape(row_count, head_count, HEAD_DIM) + skip_gain[
        None, :, None
    ] * signal.reshape(row_count, head_count, HEAD_DIM).astype(jnp.float32)
    gated_out = ssm_out.reshape(row_count, head_count * HEAD_DIM) * jax.nn.silu(
        gate_branch.astype(jnp.float32)
    )
    square_total = lax.psum(jnp.sum(gated_out * gated_out, axis=1), "tensor")
    normed = (
        gated_out * lax.rsqrt(square_total / INNER + EPSILON)[:, None] * norm_gain[None, :]
    ).astype(jnp.bfloat16)
    own_columns = lax.psum_scatter(
        lax.dot_general(
            out_weight, normed, (((0,), (1,)), ((), ())), preferred_element_type=jnp.float32
        ).astype(jnp.bfloat16),
        "tensor",
        scatter_dimension=0,
        tiled=True,
    ).astype(jnp.float32)
    return own_columns.T.astype(jnp.bfloat16)


LOG2E = 1.4426950408889634
LANES = 128
STATE_PAIRS = 4
MIX_PAIRS = 4
GATE_PAIRS = 2
TILE = 256
MESH = pl.DeviceIdType.MESH


def fused_kernel(
    heads,
    span_count,
    signal_hbm,
    gate_hbm,
    write_ref,
    read_ref,
    logits_ref,
    valid_ref,
    band_ref,
    offset_ref,
    decay_ref,
    bias_ref,
    skip_ref,
    gain_ref,
    weight_hbm,
    out_ref,
    weight_ref,
    signal_ref,
    gate_ref,
    padded_ref,
    params_ref,
    row_ref,
    spread_ref,
    skip_rows_ref,
    scores_ref,
    read_by_token_ref,
    lead_ref,
    fed_ref,
    state_ref,
    totals_ref,
    core_totals_ref,
    local_ref,
    normed_ref,
    square_ref,
    carry_ref,
    pass_ref,
    core_state_ref,
    entry_ref,
    sent_ref,
    landed_ref,
    square_out_ref,
    square_in_ref,
    load_sem,
    totals_send,
    totals_recv,
    core_send,
    core_recv,
    onward_send,
    onward_recv,
    entry_send,
    entry_recv,
    tile_send,
    tile_recv,
    square_send,
    square_recv,
):
    pair_count = heads // 2
    scan_index = lax.axis_index("scan")
    band_index = lax.axis_index("band")
    tensor_index = lax.axis_index("tensor")
    first_core = band_index == 0
    second_core = band_index == 1
    first_chip = scan_index == 0
    has_previous = second_core & (scan_index > 0)
    has_next = second_core & (scan_index < span_count - 1)
    gets_entry = first_core & (scan_index > 0)
    peer = 1 - tensor_index
    other_core = {"band": 1 - band_index}
    following = {"scan": lax.rem(scan_index + 1, span_count)}
    previous = {"scan": lax.rem(scan_index + span_count - 1, span_count)}

    barrier = pltpu.get_barrier_semaphore()
    for target in (other_core, {"tensor": peer}):
        pl.semaphore_signal(barrier, inc=1, device_id=target, device_id_type=MESH)

    @pl.when(has_next)
    def _():
        pl.semaphore_signal(barrier, inc=1, device_id=following, device_id_type=MESH)

    @pl.when(has_previous)
    def _():
        pl.semaphore_signal(barrier, inc=1, device_id=previous, device_id_type=MESH)

    signal_load = pltpu.make_async_copy(signal_hbm, signal_ref, load_sem.at[2])
    gate_load = pltpu.make_async_copy(gate_hbm, gate_ref, load_sem.at[0])
    weight_load = pltpu.make_async_copy(weight_hbm, weight_ref, load_sem.at[1])
    signal_load.start()
    gate_load.start()
    weight_load.start()

    padded_ref[...] = jnp.zeros_like(padded_ref)
    padded_ref[0:heads, :] = logits_ref[...]
    params_ref[...] = jnp.zeros_like(params_ref)
    chosen = lax.broadcasted_iota(jnp.int32, (BANDS, heads), 0) == band_ref[0]
    params_ref[0:1, 0:heads] = bias_ref[...] + jnp.sum(
        jnp.where(chosen, offset_ref[...], 0.0), axis=0, keepdims=True
    )
    params_ref[1:2, 0:heads] = jnp.exp(decay_ref[...])
    params_ref[2:3, 0:heads] = skip_ref[...]
    shifted = padded_ref[...].T + params_ref[0:1, :]
    step_size = jnp.maximum(shifted, 0.0) + jnp.log1p(jnp.exp(-jnp.abs(shifted)))
    lanes = lax.broadcasted_iota(jnp.int32, (STRETCH, LANES), 1)
    tokens = lax.broadcasted_iota(jnp.int32, (STRETCH, LANES), 0)
    real = lanes < heads
    running = jnp.where(real, step_size * -params_ref[1:2, :], 0.0)
    shift = 1
    while shift < STRETCH:
        running = running + jnp.where(tokens >= shift, pltpu.roll(running, shift, 0), 0.0)
        shift *= 2
    running = running * LOG2E
    row_ref[...] = running.T
    valid = jnp.broadcast_to(valid_ref[...].astype(jnp.float32), (LANES, STRETCH)).T
    in_weight = jnp.where(real, step_size * valid, 0.0)

    def three_parts(value):
        high = value.astype(jnp.bfloat16).astype(jnp.float32)
        rest = value - high
        middle = rest.astype(jnp.bfloat16).astype(jnp.float32)
        low = rest - middle
        packed = high + pltpu.roll(middle, heads, 1) + pltpu.roll(low, 2 * heads, 1)
        return packed.astype(jnp.bfloat16)

    running_parts = three_parts(running)
    spread_ref[:, 0:LANES] = running_parts
    spread_ref[:, LANES : 2 * LANES] = three_parts(in_weight)
    skip_rows_ref[...] = three_parts(jnp.broadcast_to(params_ref[2:3, :], (16, LANES)))
    part = lax.broadcasted_iota(jnp.int32, (LANES, 2 * LANES), 0)
    part = (
        part
        - jnp.where(part >= heads, heads, 0)
        - jnp.where(part >= 2 * heads, heads, 0)
    )
    head_of = lax.broadcasted_iota(jnp.int32, totals_ref.shape, 1)
    head_of = (
        head_of
        - jnp.where(head_of >= heads, heads, 0)
        - jnp.where(head_of >= 2 * heads, heads, 0)
    )
    own_pair = head_of // 2 == lax.broadcasted_iota(jnp.int32, totals_ref.shape, 0)
    last_parts = running_parts[STRETCH - 16 : STRETCH].astype(jnp.float32)[15:16, :]
    totals_ref[...] = jnp.exp2(
        jnp.dot(
            jnp.where(own_pair, last_parts, 0.0).astype(jnp.bfloat16),
            jnp.where(
                part[:, 0:LANES] % 2
                == lax.broadcasted_iota(jnp.int32, (LANES, LANES), 1) // HEAD_DIM,
                1.0,
                0.0,
            ).astype(jnp.bfloat16),
            preferred_element_type=jnp.float32,
        )
    )
    write_turned = write_ref[...].astype(jnp.float32).T.astype(jnp.bfloat16)
    read_by_token_ref[...] = write_turned
    scores = jnp.dot(read_ref[...], write_turned, preferred_element_type=jnp.float32)
    square_rows = lax.broadcasted_iota(jnp.int32, (STRETCH, STRETCH), 0)
    square_columns = lax.broadcasted_iota(jnp.int32, (STRETCH, STRETCH), 1)
    scores_ref[...] = jnp.where(square_columns <= square_rows, scores, 0.0)
    square_ref[...] = jnp.zeros_like(square_ref)

    @pl.when(first_core & first_chip)
    def _():
        carry_ref[...] = jnp.zeros_like(carry_ref)

    totals_copy = pltpu.make_async_remote_copy(
        src_ref=totals_ref,
        dst_ref=core_totals_ref,
        send_sem=totals_send,
        recv_sem=totals_recv,
        device_id=other_core,
        device_id_type=MESH,
    )

    def core_copy(pair):
        return pltpu.make_async_remote_copy(
            src_ref=pass_ref.at[pair],
            dst_ref=core_state_ref.at[pair],
            send_sem=core_send.at[pair],
            recv_sem=core_recv.at[pair],
            device_id=other_core,
            device_id_type=MESH,
        )

    def onward_copy(pair):
        return pltpu.make_async_remote_copy(
            src_ref=pass_ref.at[pair],
            dst_ref=entry_ref.at[pair],
            send_sem=onward_send.at[pair],
            recv_sem=onward_recv.at[pair],
            device_id=following,
            device_id_type=MESH,
        )

    def entry_copy(pair):
        return pltpu.make_async_remote_copy(
            src_ref=entry_ref.at[pair],
            dst_ref=carry_ref.at[pair],
            send_sem=entry_send.at[pair],
            recv_sem=entry_recv.at[pair],
            device_id=other_core,
            device_id_type=MESH,
        )

    def give_onward(pair, carry):
        onward = totals_ref[pl.ds(pair, 1), :] * carry + state_ref[pair]
        pass_ref[pair] = onward.astype(jnp.bfloat16)
        onward_copy(pair).start()

    def first_chain_step(pair):
        core_copy(pair).wait_recv()
        own = core_state_ref[pair]
        carry_ref[pair] = own

        @pl.when(has_next)
        def _():
            give_onward(pair, own.astype(jnp.float32))

    def chain_step(pair):
        core_copy(pair).wait_recv()
        onward_copy(pair).wait_recv()
        entry_copy(pair).start()
        carry = core_totals_ref[pl.ds(pair, 1), :] * entry_ref[pair].astype(
            jnp.float32
        ) + core_state_ref[pair].astype(jnp.float32)
        carry_ref[pair] = carry.astype(jnp.bfloat16)

        @pl.when(has_next)
        def _():
            give_onward(pair, carry)

    def columns_of(pair):
        return pl.ds(pl.multiple_of(pair * LANES, LANES), LANES)

    wide_side = lax.broadcasted_iota(jnp.int32, (LANES, 2 * LANES), 1) // LANES
    wide_index = part - wide_side
    narrow_side = lax.broadcasted_iota(jnp.int32, (LANES, LANES), 1) // HEAD_DIM
    narrow_index = part[:, 0:LANES] - narrow_side
    outside = jnp.full((LANES, LANES), -1, jnp.int32)
    block_index = jnp.concatenate(
        [
            jnp.concatenate([narrow_index, outside], axis=1),
            jnp.concatenate([outside, narrow_index], axis=1),
        ],
        axis=0,
    )
    first_half = lanes < HEAD_DIM

    def picker(index, pair):
        return jnp.where(index == 2 * pair, 1.0, 0.0).astype(jnp.bfloat16)

    def state_pair(pair):
        columns = columns_of(pair)
        both = jnp.dot(
            spread_ref[...], picker(block_index, pair), preferred_element_type=jnp.float32
        )
        own_run = both[:, 0:LANES]
        weight = both[:, LANES : 2 * LANES]
        last_run = own_run[STRETCH - 1 : STRETCH, :]
        fed = signal_ref[:, columns].astype(jnp.float32) * weight
        fed_ref[:, columns] = fed.astype(jnp.bfloat16)
        lead_ref[:, columns] = jnp.exp2(own_run)
        scaled = (fed * jnp.exp2(last_run - own_run)).astype(jnp.bfloat16)
        state = jnp.dot(read_by_token_ref[...], scaled, preferred_element_type=jnp.float32)
        state_ref[pair] = state
        pass_ref[pair] = state.astype(jnp.bfloat16)


    def mix_pair(pair):
        columns = columns_of(pair)
        half = STRETCH // 2
        tops, bottoms = [], []
        fed = fed_ref[:, columns]
        runs = jnp.dot(
            spread_ref[:, 0:LANES], picker(wide_index, pair), preferred_element_type=jnp.float32
        )
        for side in range(2):
            row = row_ref[pl.ds(2 * pair + side, 1), :]
            run = runs[:, side * LANES : (side + 1) * LANES]
            near = jnp.exp2(jnp.minimum(run[0:half] - row[:, 0:half], 0.0))
            far = jnp.exp2(jnp.minimum(run[half:] - row[:, 0:half], 0.0))
            late = jnp.exp2(jnp.minimum(run[half:] - row[:, half:], 0.0))
            near = (near * scores_ref[0:half, 0:half]).astype(jnp.bfloat16)
            far = (far * scores_ref[half:, 0:half]).astype(jnp.bfloat16)
            late = (late * scores_ref[half:, half:]).astype(jnp.bfloat16)
            tops.append(jnp.dot(near, fed[0:half], preferred_element_type=jnp.float32))
            bottoms.append(
                jnp.dot(
                    jnp.concatenate([far, late], axis=1), fed, preferred_element_type=jnp.float32
                )
            )
        local_ref[0:half, columns] = jnp.where(first_half[0:half], tops[0], tops[1])
        local_ref[half:, columns] = jnp.where(first_half[half:], bottoms[0], bottoms[1])

    def gate_pair(pair):
        columns = columns_of(pair)
        carried = jnp.dot(read_ref[...], carry_ref[pair], preferred_element_type=jnp.float32)
        skip = jnp.dot(
            skip_rows_ref[...], picker(narrow_index, pair), preferred_element_type=jnp.float32
        )
        ssm_out = (
            local_ref[:, columns]
            + lead_ref[:, columns] * carried
            + skip[0:1, :] * signal_ref[:, columns].astype(jnp.float32)
        )
        gate = gate_ref[:, columns].astype(jnp.float32)
        gated = ssm_out * (gate / (1.0 + jnp.exp(-gate)))
        normed_ref[:, columns] = (gated * gain_ref[pl.ds(pair, 1), :]).astype(jnp.bfloat16)
        return gated * gated

    signal_load.wait()

    @pl.loop(0, pair_count // STATE_PAIRS)
    def _(group):
        for member in range(STATE_PAIRS):
            state_pair(group * STATE_PAIRS + member)

        @pl.when(group == 0)
        def _():
            pl.semaphore_wait(
                barrier, 2 + jnp.where(has_next, 1, 0) + jnp.where(has_previous, 1, 0)
            )

            @pl.when(first_core)
            def _():
                totals_copy.start()

        @pl.when(first_core)
        def _():
            for member in range(STATE_PAIRS):
                core_copy(group * STATE_PAIRS + member).start()

        @pl.when(second_core & first_chip & (group > 0))
        def _():
            for member in range(STATE_PAIRS):
                first_chain_step((group - 1) * STATE_PAIRS + member)

    @pl.when(second_core)
    def _():
        totals_copy.wait_recv()

    @pl.when(second_core & first_chip)
    def _():
        for member in range(STATE_PAIRS):
            first_chain_step(pair_count - STATE_PAIRS + member)

    @pl.loop(0, pair_count // MIX_PAIRS)
    def _(group):
        @pl.when(has_previous & has_next)
        def _():
            for member in range(MIX_PAIRS):
                chain_step(group * MIX_PAIRS + member)

        for member in range(MIX_PAIRS):
            mix_pair(group * MIX_PAIRS + member)

    gate_load.wait()
    last_step = has_previous & (scan_index == span_count - 1)

    @pl.loop(0, pair_count // GATE_PAIRS)
    def _(group):
        @pl.when(last_step)
        def _():
            for member in range(GATE_PAIRS):
                chain_step(group * GATE_PAIRS + member)

        @pl.when(gets_entry)
        def _():
            for member in range(GATE_PAIRS):
                entry_copy(group * GATE_PAIRS + member).wait_recv()

        squares = square_ref[...]
        for member in range(GATE_PAIRS):
            squares = squares + gate_pair(group * GATE_PAIRS + member)
        square_ref[...] = squares

    square_sum = jnp.sum(square_ref[...].T, axis=0, keepdims=True)
    square_out_ref[...] = jnp.broadcast_to(square_sum, square_out_ref.shape)
    square_copy = pltpu.make_async_remote_copy(
        src_ref=square_out_ref,
        dst_ref=square_in_ref,
        send_sem=square_send,
        recv_sem=square_recv,
        device_id={"tensor": peer},
        device_id_type=MESH,
    )
    square_copy.start()
    weight_load.wait()
    own_width = out_ref.shape[1]
    tile_count = own_width // TILE

    def tile_copy(tile):
        return pltpu.make_async_remote_copy(
            src_ref=sent_ref.at[tile],
            dst_ref=landed_ref.at[tile],
            send_sem=tile_send.at[tile],
            recv_sem=tile_recv.at[tile],
            device_id={"tensor": peer},
            device_id_type=MESH,
        )

    def project(owner, tile):
        start = pl.multiple_of(owner * own_width + tile * TILE, LANES)
        return jnp.dot(
            normed_ref[...], weight_ref[:, pl.ds(start, TILE)], preferred_element_type=jnp.float32
        )

    @pl.loop(0, tile_count)
    def _(tile):
        sent_ref[tile] = project(peer, tile).astype(jnp.bfloat16)
        tile_copy(tile).start()

    square_copy.wait()
    inner = 2 * heads * HEAD_DIM
    scale = lax.rsqrt((square_out_ref[0:1, :] + square_in_ref[0:1, :]) / inner + EPSILON)
    square_ref[...] = jnp.broadcast_to(scale, (LANES, STRETCH)).T

    @pl.loop(0, tile_count)
    def _(tile):
        own = project(tensor_index, tile)
        tile_copy(tile).wait_recv()
        both = own + landed_ref[tile].astype(jnp.float32)
        scales = square_ref[...]
        for side in range(TILE // LANES):
            start = pl.multiple_of(tile * TILE + side * LANES, LANES)
            out_ref[:, pl.ds(start, LANES)] = (
                both[:, side * LANES : (side + 1) * LANES] * scales
            ).astype(jnp.bfloat16)

    @pl.loop(0, tile_count)
    def _(tile):
        tile_copy(tile).wait_send()

    @pl.when(first_core)
    def _():
        totals_copy.wait_send()

        @pl.loop(0, pair_count)
        def _(pair):
            core_copy(pair).wait_send()

    @pl.when(has_next)
    def _():
        @pl.loop(0, pair_count)
        def _(pair):
            onward_copy(pair).wait_send()

    @pl.when(has_previous)
    def _():
        @pl.loop(0, pair_count)
        def _(pair):
            entry_copy(pair).wait_send()


def fused_on_device(
    span_count,
    signal,
    gate_branch,
    write_proj,
    read_proj,
    step_logits,
    valid_mask,
    stretch_band,
    band_offset,
    decay_log,
    step_offset,
    skip_gain,
    norm_gain,
    out_weight,
):
    heads = decay_log.shape[0]
    inner = heads * HEAD_DIM
    width = out_weight.shape[1]
    pair_count = heads // 2
    tile_count = width // 2 // TILE
    vmem = pl.BlockSpec(memory_space=pltpu.VMEM)
    hbm = pl.BlockSpec(memory_space=pl.ANY)
    smem = pl.BlockSpec(memory_space=pltpu.SMEM)
    f32, bf16 = jnp.float32, jnp.bfloat16
    return pl.pallas_call(
        functools.partial(fused_kernel, heads, span_count),
        out_shape=pltpu.VMEM((STRETCH, width // 2), bf16),
        in_specs=[hbm, hbm] + [vmem] * 4 + [smem] + [vmem] * 5 + [hbm],
        out_specs=vmem,
        scratch_shapes=[
            pltpu.VMEM((inner, width), bf16),
            pltpu.VMEM((STRETCH, inner), bf16),
            pltpu.VMEM((STRETCH, inner), bf16),
            pltpu.VMEM((LANES, STRETCH), f32),
            pltpu.VMEM((8, LANES), f32),
            pltpu.VMEM((LANES, STRETCH), f32),
            pltpu.VMEM((STRETCH, 2 * LANES), bf16),
            pltpu.VMEM((16, LANES), bf16),
            pltpu.VMEM((STRETCH, STRETCH), f32),
            pltpu.VMEM((STATE, STRETCH), bf16),
            pltpu.VMEM((STRETCH, inner), f32),
            pltpu.VMEM((STRETCH, inner), bf16),
            pltpu.VMEM((pair_count, STATE, LANES), f32),
            pltpu.VMEM((-(-pair_count // 16) * 16, LANES), f32),
            pltpu.VMEM((-(-pair_count // 16) * 16, LANES), f32),
            pltpu.VMEM((STRETCH, inner), f32),
            pltpu.VMEM((STRETCH, inner), bf16),
            pltpu.VMEM((STRETCH, LANES), f32),
            pltpu.VMEM((pair_count, STATE, LANES), bf16),
            pltpu.VMEM((pair_count, STATE, LANES), bf16),
            pltpu.VMEM((pair_count, STATE, LANES), bf16),
            pltpu.VMEM((pair_count, STATE, LANES), bf16),
            pltpu.VMEM((tile_count, STRETCH, TILE), bf16),
            pltpu.VMEM((tile_count, STRETCH, TILE), bf16),
            pltpu.VMEM((8, STRETCH), f32),
            pltpu.VMEM((8, STRETCH), f32),
            pltpu.SemaphoreType.DMA((3,)),
            pltpu.SemaphoreType.DMA,
            pltpu.SemaphoreType.DMA,
            pltpu.SemaphoreType.DMA((pair_count,)),
            pltpu.SemaphoreType.DMA((pair_count,)),
            pltpu.SemaphoreType.DMA((pair_count,)),
            pltpu.SemaphoreType.DMA((pair_count,)),
            pltpu.SemaphoreType.DMA((pair_count,)),
            pltpu.SemaphoreType.DMA((pair_count,)),
            pltpu.SemaphoreType.DMA((tile_count,)),
            pltpu.SemaphoreType.DMA((tile_count,)),
            pltpu.SemaphoreType.DMA,
            pltpu.SemaphoreType.DMA,
        ],
        compiler_params=pltpu.CompilerParams(
            collective_id=0, has_side_effects=True, vmem_limit_bytes=60 * 1024 * 1024
        ),
    )(
        signal,
        gate_branch,
        write_proj,
        read_proj,
        step_logits,
        valid_mask[None, :],
        stretch_band,
        band_offset,
        decay_log[None, :],
        step_offset[None, :],
        skip_gain[None, :],
        norm_gain.reshape(pair_count, LANES),
        out_weight,
    )


def solution(mesh):
    placed = (
        P(("group", "scan", "band"), "tensor"),
        P(("group", "scan", "band"), "tensor"),
        P(("group", "scan", "band"), None),
        P(("group", "scan", "band"), None),
        P("tensor", ("group", "scan", "band")),
        P(("group", "scan", "band")),
        P(("group", "scan", "band")),
        P(None, "tensor"),
        P("tensor"),
        P("tensor"),
        P("tensor"),
        P("tensor"),
        P("tensor", None),
    )
    shape = dict(mesh.shape)
    places = shape["scan"] * shape["band"]

    def layer(*arrays):
        rows = arrays[0].shape[0] // (shape["group"] * places)
        heads = arrays[8].shape[0] // shape["tensor"]
        width = arrays[12].shape[1]
        fits = (
            shape["tensor"] == 2
            and shape["band"] == 2
            and shape["scan"] >= 2
            and rows == STRETCH
            and heads % (2 * STATE_PAIRS) == 0
            and heads % (2 * MIX_PAIRS) == 0
            and heads % (2 * GATE_PAIRS) == 0
            and 3 * heads <= LANES
            and width % (2 * TILE) == 0
        )
        member = on_device
        if fits:
            member = functools.partial(fused_on_device, shape["scan"])
        return mapped(member)(*arrays)

    def mapped(member):
        return jax.shard_map(
            member,
            mesh=mesh,
            in_specs=placed,
            out_specs=P(("group", "scan", "band"), "tensor"),
            check_vma=False,
        )

    return layer
```

```python
import functools

import jax
import jax.numpy as jnp
from jax import lax
from jax.experimental import pallas as pl
from jax.experimental.pallas import tpu as pltpu
from jax.sharding import PartitionSpec as P

HEAD_DIM = 64
STATE = 128
STRETCH = 256
BANDS = 12
INNER = 5120


EPSILON = 1e-05
HIGHEST = lax.Precision.HIGHEST


def step_sizes(step_logits, stretch_band, band_offset, step_offset):
    one_hot = (stretch_band[:, None] == jnp.arange(BANDS, dtype=jnp.int32)[None, :]).astype(
        jnp.float32
    )
    stretch_offset = jnp.dot(one_hot, band_offset, precision=HIGHEST)
    token_offset = jnp.repeat(stretch_offset, STRETCH, axis=0).T
    return jax.nn.softplus(step_logits + step_offset[:, None] + token_offset)


def combine(earlier, later_pair):
    return (
        earlier[0] + later_pair[0],
        jnp.exp(later_pair[0])[:, None, None] * earlier[1] + later_pair[1],
    )


def local_step(running_pair, member):
    return (combine(running_pair, member), running_pair)


def on_device(
    signal,
    gate_branch,
    write_proj,
    read_proj,
    step_logits,
    valid_mask,
    stretch_band,
    band_offset,
    decay_log,
    step_offset,
    skip_gain,
    norm_gain,
    out_weight,
):
    row_count = signal.shape[0]
    head_count = decay_log.shape[0]
    block_count = row_count // STRETCH
    step_size = step_sizes(step_logits, stretch_band, band_offset, step_offset)
    log_decay = step_size * (-jnp.exp(decay_log))[:, None]
    input_weight = step_size * valid_mask.astype(jnp.float32)[None, :]
    running = lax.associative_scan(
        jnp.add, log_decay.reshape(head_count, block_count, STRETCH), axis=2
    )
    weight_blocks = input_weight.reshape(head_count, block_count, STRETCH)
    signal_blocks = signal.reshape(block_count, STRETCH, head_count, HEAD_DIM)
    write_blocks = write_proj.reshape(block_count, STRETCH, STATE)
    read_blocks = read_proj.reshape(block_count, STRETCH, STATE)
    scores = jnp.einsum(
        "cin,cjn->cij", read_blocks, write_blocks, preferred_element_type=jnp.float32
    )
    lower_mask = jnp.arange(STRETCH)[:, None] >= jnp.arange(STRETCH)[None, :]
    span_logs = jnp.where(
        lower_mask[None, None], running[:, :, :, None] - running[:, :, None, :], -1e30
    )
    mixing = (jnp.exp(span_logs) * scores[None] * weight_blocks[:, :, None, :]).astype(jnp.bfloat16)
    local_out = jnp.einsum(
        "hcij,cjhp->cihp", mixing, signal_blocks, preferred_element_type=jnp.float32
    )
    tail_weight = jnp.exp(running[:, :, -1:] - running) * weight_blocks
    scaled = (
        signal_blocks.astype(jnp.float32) * jnp.transpose(tail_weight, (1, 2, 0))[:, :, :, None]
    ).astype(jnp.bfloat16)
    block_states = jnp.einsum(
        "cjhp,cjn->chpn", scaled, write_blocks, preferred_element_type=jnp.float32
    )
    block_decay = running[:, :, -1].T
    zero_state = jnp.zeros((head_count, HEAD_DIM, STATE), jnp.float32)
    zero_log = jnp.zeros((head_count,), jnp.float32)
    identity = (zero_log, zero_state)
    device_pair, segment_cumulative = lax.scan(local_step, identity, (block_decay, block_states))
    all_logs = lax.all_gather(device_pair[0][None], ("scan", "band"), axis=0, tiled=True)
    inclusive = lax.associative_scan(jnp.add, all_logs, axis=0)
    exclusive = inclusive - all_logs
    position = lax.axis_index(("scan", "band"))
    own_exclusive = lax.dynamic_index_in_dim(exclusive, position, 0, keepdims=False)
    shard_block = lax.all_gather(
        device_pair[1][None].astype(jnp.bfloat16), ("scan", "band"), axis=0, tiled=True
    ).astype(jnp.float32)
    how_many = shard_block.shape[0]
    sources = jnp.arange(how_many, dtype=jnp.int32)
    gap_logs = jnp.where((sources < position)[:, None], own_exclusive[None, :] - inclusive, -1e30)
    carry_state = zero_state + jnp.einsum(
        "kh,khpn->hpn", jnp.exp(gap_logs), shard_block, precision=HIGHEST
    )
    enter_state = (
        jnp.exp(segment_cumulative[0])[:, :, None, None] * carry_state[None] + segment_cumulative[1]
    )
    state_high = enter_state.astype(jnp.bfloat16)
    widened = lax.optimization_barrier(state_high).astype(jnp.float32)
    state_low = (enter_state - widened).astype(jnp.bfloat16)
    high_part = jnp.einsum(
        "cin,chpn->cihp", read_blocks, state_high, preferred_element_type=jnp.float32
    )
    low_part = jnp.einsum(
        "cin,chpn->cihp", read_blocks, state_low, preferred_element_type=jnp.float32
    )
    carried_out = jnp.transpose(jnp.exp(running), (1, 2, 0))[:, :, :, None] * (high_part + low_part)
    ssm_out = (local_out + carried_out).reshape(row_count, head_count, HEAD_DIM) + skip_gain[
        None, :, None
    ] * signal.reshape(row_count, head_count, HEAD_DIM).astype(jnp.float32)
    gated_out = ssm_out.reshape(row_count, head_count * HEAD_DIM) * jax.nn.silu(
        gate_branch.astype(jnp.float32)
    )
    square_total = lax.psum(jnp.sum(gated_out * gated_out, axis=1), "tensor")
    normed = (
        gated_out * lax.rsqrt(square_total / INNER + EPSILON)[:, None] * norm_gain[None, :]
    ).astype(jnp.bfloat16)
    own_columns = lax.psum_scatter(
        lax.dot_general(
            out_weight, normed, (((0,), (1,)), ((), ())), preferred_element_type=jnp.float32
        ).astype(jnp.bfloat16),
        "tensor",
        scatter_dimension=0,
        tiled=True,
    ).astype(jnp.float32)
    return own_columns.T.astype(jnp.bfloat16)


LOG2E = 1.4426950408889634
LANES = 128
STATE_PAIRS = 4
MIX_PAIRS = 4
GATE_PAIRS = 2
TILE = 256
MESH = pl.DeviceIdType.MESH


def fused_kernel(
    heads,
    span_count,
    signal_hbm,
    gate_hbm,
    write_ref,
    read_ref,
    logits_ref,
    valid_ref,
    band_ref,
    offset_ref,
    decay_ref,
    bias_ref,
    skip_ref,
    gain_ref,
    weight_hbm,
    out_ref,
    weight_ref,
    signal_ref,
    gate_ref,
    padded_ref,
    params_ref,
    row_ref,
    run_ref,
    in_weight_ref,
    last_ref,
    skip_rows_ref,
    scores_ref,
    read_by_token_ref,
    lead_ref,
    fed_ref,
    state_ref,
    totals_ref,
    core_totals_ref,
    local_ref,
    normed_ref,
    square_ref,
    carry_ref,
    pass_ref,
    core_state_ref,
    entry_ref,
    sent_ref,
    landed_ref,
    square_out_ref,
    square_in_ref,
    load_sem,
    totals_send,
    totals_recv,
    core_send,
    core_recv,
    onward_send,
    onward_recv,
    entry_send,
    entry_recv,
    tile_send,
    tile_recv,
    square_send,
    square_recv,
):
    pair_count = heads // 2
    scan_index = lax.axis_index("scan")
    band_index = lax.axis_index("band")
    tensor_index = lax.axis_index("tensor")
    first_core = band_index == 0
    second_core = band_index == 1
    first_chip = scan_index == 0
    has_previous = second_core & (scan_index > 0)
    has_next = second_core & (scan_index < span_count - 1)
    gets_entry = first_core & (scan_index > 0)
    peer = 1 - tensor_index
    other_core = {"band": 1 - band_index}
    following = {"scan": lax.rem(scan_index + 1, span_count)}
    previous = {"scan": lax.rem(scan_index + span_count - 1, span_count)}

    barrier = pltpu.get_barrier_semaphore()
    for target in (other_core, {"tensor": peer}):
        pl.semaphore_signal(barrier, inc=1, device_id=target, device_id_type=MESH)

    @pl.when(has_next)
    def _():
        pl.semaphore_signal(barrier, inc=1, device_id=following, device_id_type=MESH)

    @pl.when(has_previous)
    def _():
        pl.semaphore_signal(barrier, inc=1, device_id=previous, device_id_type=MESH)

    signal_load = pltpu.make_async_copy(signal_hbm, signal_ref, load_sem.at[2])
    gate_load = pltpu.make_async_copy(gate_hbm, gate_ref, load_sem.at[0])
    weight_load = pltpu.make_async_copy(weight_hbm, weight_ref, load_sem.at[1])
    signal_load.start()
    gate_load.start()
    weight_load.start()

    padded_ref[...] = jnp.zeros_like(padded_ref)
    padded_ref[0:heads, :] = logits_ref[...]
    params_ref[...] = jnp.zeros_like(params_ref)
    chosen = lax.broadcasted_iota(jnp.int32, (BANDS, heads), 0) == band_ref[0]
    params_ref[0:1, 0:heads] = bias_ref[...] + jnp.sum(
        jnp.where(chosen, offset_ref[...], 0.0), axis=0, keepdims=True
    )
    params_ref[1:2, 0:heads] = jnp.exp(decay_ref[...])
    params_ref[2:3, 0:heads] = skip_ref[...]
    shifted = padded_ref[...].T + params_ref[0:1, :]
    step_size = jnp.maximum(shifted, 0.0) + jnp.log1p(jnp.exp(-jnp.abs(shifted)))
    lanes = lax.broadcasted_iota(jnp.int32, (STRETCH, LANES), 1)
    tokens = lax.broadcasted_iota(jnp.int32, (STRETCH, LANES), 0)
    real = lanes < heads
    running = jnp.where(real, step_size * -params_ref[1:2, :], 0.0)
    shift = 1
    while shift < STRETCH:
        running = running + jnp.where(tokens >= shift, pltpu.roll(running, shift, 0), 0.0)
        shift *= 2
    running = running * LOG2E
    row_ref[...] = running.T
    valid = jnp.broadcast_to(valid_ref[...].astype(jnp.float32), (LANES, STRETCH)).T
    in_weight = jnp.where(real, step_size * valid, 0.0)

    def three_parts(value):
        high = value.astype(jnp.bfloat16).astype(jnp.float32)
        rest = value - high
        middle = rest.astype(jnp.bfloat16).astype(jnp.float32)
        low = rest - middle
        packed = high + pltpu.roll(middle, heads, 1) + pltpu.roll(low, 2 * heads, 1)
        return packed.astype(jnp.bfloat16)

    running_parts = three_parts(running)
    run_ref[...] = running
    in_weight_ref[...] = in_weight
    skip_rows_ref[...] = three_parts(jnp.broadcast_to(params_ref[2:3, :], (16, LANES)))
    part = lax.broadcasted_iota(jnp.int32, (LANES, 2 * LANES), 0)
    part = (
        part
        - jnp.where(part >= heads, heads, 0)
        - jnp.where(part >= 2 * heads, heads, 0)
    )
    head_of = lax.broadcasted_iota(jnp.int32, totals_ref.shape, 1)
    head_of = (
        head_of
        - jnp.where(head_of >= heads, heads, 0)
        - jnp.where(head_of >= 2 * heads, heads, 0)
    )
    own_pair = head_of // 2 == lax.broadcasted_iota(jnp.int32, totals_ref.shape, 0)
    last_parts = running_parts[STRETCH - 16 : STRETCH].astype(jnp.float32)[15:16, :]
    last_rows = (
        jnp.dot(
            jnp.where(own_pair, last_parts, 0.0).astype(jnp.bfloat16),
            jnp.where(
                part[:, 0:LANES] % 2
                == lax.broadcasted_iota(jnp.int32, (LANES, LANES), 1) // HEAD_DIM,
                1.0,
                0.0,
            ).astype(jnp.bfloat16),
            preferred_element_type=jnp.float32,
        )
    )
    last_ref[...] = last_rows
    totals_ref[...] = jnp.exp2(last_rows)
    write_turned = write_ref[...].astype(jnp.float32).T.astype(jnp.bfloat16)
    read_by_token_ref[...] = write_turned
    scores = jnp.dot(read_ref[...], write_turned, preferred_element_type=jnp.float32)
    square_rows = lax.broadcasted_iota(jnp.int32, (STRETCH, STRETCH), 0)
    square_columns = lax.broadcasted_iota(jnp.int32, (STRETCH, STRETCH), 1)
    scores_ref[...] = jnp.where(square_columns <= square_rows, scores, 0.0)
    square_ref[...] = jnp.zeros_like(square_ref)

    @pl.when(first_core & first_chip)
    def _():
        carry_ref[...] = jnp.zeros_like(carry_ref)

    totals_copy = pltpu.make_async_remote_copy(
        src_ref=totals_ref,
        dst_ref=core_totals_ref,
        send_sem=totals_send,
        recv_sem=totals_recv,
        device_id=other_core,
        device_id_type=MESH,
    )

    def core_copy(pair):
        return pltpu.make_async_remote_copy(
            src_ref=pass_ref.at[pair],
            dst_ref=core_state_ref.at[pair],
            send_sem=core_send.at[pair],
            recv_sem=core_recv.at[pair],
            device_id=other_core,
            device_id_type=MESH,
        )

    def onward_copy(pair):
        return pltpu.make_async_remote_copy(
            src_ref=pass_ref.at[pair],
            dst_ref=entry_ref.at[pair],
            send_sem=onward_send.at[pair],
            recv_sem=onward_recv.at[pair],
            device_id=following,
            device_id_type=MESH,
        )

    def entry_copy(pair):
        return pltpu.make_async_remote_copy(
            src_ref=entry_ref.at[pair],
            dst_ref=carry_ref.at[pair],
            send_sem=entry_send.at[pair],
            recv_sem=entry_recv.at[pair],
            device_id=other_core,
            device_id_type=MESH,
        )

    def give_onward(pair, carry):
        onward = totals_ref[pl.ds(pair, 1), :] * carry + state_ref[pair]
        pass_ref[pair] = onward.astype(jnp.bfloat16)
        onward_copy(pair).start()

    def first_chain_step(pair):
        core_copy(pair).wait_recv()
        own = core_state_ref[pair]
        carry_ref[pair] = own

        @pl.when(has_next)
        def _():
            give_onward(pair, own.astype(jnp.float32))

    def chain_step(pair):
        core_copy(pair).wait_recv()
        onward_copy(pair).wait_recv()
        entry_copy(pair).start()
        carry = core_totals_ref[pl.ds(pair, 1), :] * entry_ref[pair].astype(
            jnp.float32
        ) + core_state_ref[pair].astype(jnp.float32)
        carry_ref[pair] = carry.astype(jnp.bfloat16)

        @pl.when(has_next)
        def _():
            give_onward(pair, carry)

    def columns_of(pair):
        return pl.ds(pl.multiple_of(pair * LANES, LANES), LANES)

    narrow_side = lax.broadcasted_iota(jnp.int32, (LANES, LANES), 1) // HEAD_DIM
    narrow_index = part[:, 0:LANES] - narrow_side
    first_half = lanes < HEAD_DIM

    def picker(index, pair):
        return jnp.where(index == 2 * pair, 1.0, 0.0).astype(jnp.bfloat16)

    def spread(values, index):
        return jnp.take_along_axis(values, index, axis=1, mode="promise_in_bounds")

    def state_pair(pair):
        columns = columns_of(pair)
        index = 2 * pair + lanes // HEAD_DIM
        own_run = spread(run_ref[...], index)
        weight = spread(in_weight_ref[...], index)
        last_run = last_ref[pl.ds(pair, 1), :]
        fed = signal_ref[:, columns].astype(jnp.float32) * weight
        fed_ref[:, columns] = fed.astype(jnp.bfloat16)
        lead_ref[:, columns] = jnp.exp2(own_run)
        scaled = (fed * jnp.exp2(last_run - own_run)).astype(jnp.bfloat16)
        state = jnp.dot(read_by_token_ref[...], scaled, preferred_element_type=jnp.float32)
        state_ref[pair] = state
        pass_ref[pair] = state.astype(jnp.bfloat16)


    def mix_pair(pair):
        columns = columns_of(pair)
        half = STRETCH // 2
        tops, bottoms = [], []
        fed = fed_ref[:, columns]
        for side in range(2):
            row = row_ref[pl.ds(2 * pair + side, 1), :]
            run = spread(run_ref[...], jnp.full((STRETCH, LANES), 2 * pair + side, jnp.int32))
            near = jnp.exp2(jnp.minimum(run[0:half] - row[:, 0:half], 0.0))
            far = jnp.exp2(jnp.minimum(run[half:] - row[:, 0:half], 0.0))
            late = jnp.exp2(jnp.minimum(run[half:] - row[:, half:], 0.0))
            near = (near * scores_ref[0:half, 0:half]).astype(jnp.bfloat16)
            far = (far * scores_ref[half:, 0:half]).astype(jnp.bfloat16)
            late = (late * scores_ref[half:, half:]).astype(jnp.bfloat16)
            tops.append(jnp.dot(near, fed[0:half], preferred_element_type=jnp.float32))
            bottoms.append(
                jnp.dot(
                    jnp.concatenate([far, late], axis=1), fed, preferred_element_type=jnp.float32
                )
            )
        local_ref[0:half, columns] = jnp.where(first_half[0:half], tops[0], tops[1])
        local_ref[half:, columns] = jnp.where(first_half[half:], bottoms[0], bottoms[1])

    def gate_pair(pair):
        columns = columns_of(pair)
        carried = jnp.dot(read_ref[...], carry_ref[pair], preferred_element_type=jnp.float32)
        skip = jnp.dot(
            skip_rows_ref[...], picker(narrow_index, pair), preferred_element_type=jnp.float32
        )
        ssm_out = (
            local_ref[:, columns]
            + lead_ref[:, columns] * carried
            + skip[0:1, :] * signal_ref[:, columns].astype(jnp.float32)
        )
        gate = gate_ref[:, columns].astype(jnp.float32)
        gated = ssm_out * (gate / (1.0 + jnp.exp(-gate)))
        normed_ref[:, columns] = (gated * gain_ref[pl.ds(pair, 1), :]).astype(jnp.bfloat16)
        return gated * gated

    signal_load.wait()

    @pl.loop(0, pair_count // STATE_PAIRS)
    def _(group):
        for member in range(STATE_PAIRS):
            state_pair(group * STATE_PAIRS + member)

        @pl.when(group == 0)
        def _():
            pl.semaphore_wait(
                barrier, 2 + jnp.where(has_next, 1, 0) + jnp.where(has_previous, 1, 0)
            )

            @pl.when(first_core)
            def _():
                totals_copy.start()

        @pl.when(first_core)
        def _():
            for member in range(STATE_PAIRS):
                core_copy(group * STATE_PAIRS + member).start()

        @pl.when(second_core & first_chip & (group > 0))
        def _():
            for member in range(STATE_PAIRS):
                first_chain_step((group - 1) * STATE_PAIRS + member)

    @pl.when(second_core)
    def _():
        totals_copy.wait_recv()

    @pl.when(second_core & first_chip)
    def _():
        for member in range(STATE_PAIRS):
            first_chain_step(pair_count - STATE_PAIRS + member)

    @pl.loop(0, pair_count // MIX_PAIRS)
    def _(group):
        @pl.when(has_previous & has_next)
        def _():
            for member in range(MIX_PAIRS):
                chain_step(group * MIX_PAIRS + member)

        for member in range(MIX_PAIRS):
            mix_pair(group * MIX_PAIRS + member)

    gate_load.wait()
    last_step = has_previous & (scan_index == span_count - 1)

    @pl.loop(0, pair_count // GATE_PAIRS)
    def _(group):
        @pl.when(last_step)
        def _():
            for member in range(GATE_PAIRS):
                chain_step(group * GATE_PAIRS + member)

        @pl.when(gets_entry)
        def _():
            for member in range(GATE_PAIRS):
                entry_copy(group * GATE_PAIRS + member).wait_recv()

        squares = square_ref[...]
        for member in range(GATE_PAIRS):
            squares = squares + gate_pair(group * GATE_PAIRS + member)
        square_ref[...] = squares

    square_sum = jnp.sum(square_ref[...].T, axis=0, keepdims=True)
    square_out_ref[...] = jnp.broadcast_to(square_sum, square_out_ref.shape)
    square_copy = pltpu.make_async_remote_copy(
        src_ref=square_out_ref,
        dst_ref=square_in_ref,
        send_sem=square_send,
        recv_sem=square_recv,
        device_id={"tensor": peer},
        device_id_type=MESH,
    )
    square_copy.start()
    weight_load.wait()
    own_width = out_ref.shape[1]
    tile_count = own_width // TILE

    def tile_copy(tile):
        return pltpu.make_async_remote_copy(
            src_ref=sent_ref.at[tile],
            dst_ref=landed_ref.at[tile],
            send_sem=tile_send.at[tile],
            recv_sem=tile_recv.at[tile],
            device_id={"tensor": peer},
            device_id_type=MESH,
        )

    def project(owner, tile):
        start = pl.multiple_of(owner * own_width + tile * TILE, LANES)
        return jnp.dot(
            normed_ref[...], weight_ref[:, pl.ds(start, TILE)], preferred_element_type=jnp.float32
        )

    @pl.loop(0, tile_count)
    def _(tile):
        sent_ref[tile] = project(peer, tile).astype(jnp.bfloat16)
        tile_copy(tile).start()

    square_copy.wait()
    inner = 2 * heads * HEAD_DIM
    scale = lax.rsqrt((square_out_ref[0:1, :] + square_in_ref[0:1, :]) / inner + EPSILON)
    square_ref[...] = jnp.broadcast_to(scale, (LANES, STRETCH)).T

    @pl.loop(0, tile_count)
    def _(tile):
        own = project(tensor_index, tile)
        tile_copy(tile).wait_recv()
        both = own + landed_ref[tile].astype(jnp.float32)
        scales = square_ref[...]
        for side in range(TILE // LANES):
            start = pl.multiple_of(tile * TILE + side * LANES, LANES)
            out_ref[:, pl.ds(start, LANES)] = (
                both[:, side * LANES : (side + 1) * LANES] * scales
            ).astype(jnp.bfloat16)

    @pl.loop(0, tile_count)
    def _(tile):
        tile_copy(tile).wait_send()

    @pl.when(first_core)
    def _():
        totals_copy.wait_send()

        @pl.loop(0, pair_count)
        def _(pair):
            core_copy(pair).wait_send()

    @pl.when(has_next)
    def _():
        @pl.loop(0, pair_count)
        def _(pair):
            onward_copy(pair).wait_send()

    @pl.when(has_previous)
    def _():
        @pl.loop(0, pair_count)
        def _(pair):
            entry_copy(pair).wait_send()


def fused_on_device(
    span_count,
    signal,
    gate_branch,
    write_proj,
    read_proj,
    step_logits,
    valid_mask,
    stretch_band,
    band_offset,
    decay_log,
    step_offset,
    skip_gain,
    norm_gain,
    out_weight,
):
    heads = decay_log.shape[0]
    inner = heads * HEAD_DIM
    width = out_weight.shape[1]
    pair_count = heads // 2
    tile_count = width // 2 // TILE
    vmem = pl.BlockSpec(memory_space=pltpu.VMEM)
    hbm = pl.BlockSpec(memory_space=pl.ANY)
    smem = pl.BlockSpec(memory_space=pltpu.SMEM)
    f32, bf16 = jnp.float32, jnp.bfloat16
    return pl.pallas_call(
        functools.partial(fused_kernel, heads, span_count),
        out_shape=pltpu.VMEM((STRETCH, width // 2), bf16),
        in_specs=[hbm, hbm] + [vmem] * 4 + [smem] + [vmem] * 5 + [hbm],
        out_specs=vmem,
        scratch_shapes=[
            pltpu.VMEM((inner, width), bf16),
            pltpu.VMEM((STRETCH, inner), bf16),
            pltpu.VMEM((STRETCH, inner), bf16),
            pltpu.VMEM((LANES, STRETCH), f32),
            pltpu.VMEM((8, LANES), f32),
            pltpu.VMEM((LANES, STRETCH), f32),
            pltpu.VMEM((STRETCH, LANES), f32),
            pltpu.VMEM((STRETCH, LANES), f32),
            pltpu.VMEM((-(-pair_count // 16) * 16, LANES), f32),
            pltpu.VMEM((16, LANES), bf16),
            pltpu.VMEM((STRETCH, STRETCH), f32),
            pltpu.VMEM((STATE, STRETCH), bf16),
            pltpu.VMEM((STRETCH, inner), f32),
            pltpu.VMEM((STRETCH, inner), bf16),
            pltpu.VMEM((pair_count, STATE, LANES), f32),
            pltpu.VMEM((-(-pair_count // 16) * 16, LANES), f32),
            pltpu.VMEM((-(-pair_count // 16) * 16, LANES), f32),
            pltpu.VMEM((STRETCH, inner), f32),
            pltpu.VMEM((STRETCH, inner), bf16),
            pltpu.VMEM((STRETCH, LANES), f32),
            pltpu.VMEM((pair_count, STATE, LANES), bf16),
            pltpu.VMEM((pair_count, STATE, LANES), bf16),
            pltpu.VMEM((pair_count, STATE, LANES), bf16),
            pltpu.VMEM((pair_count, STATE, LANES), bf16),
            pltpu.VMEM((tile_count, STRETCH, TILE), bf16),
            pltpu.VMEM((tile_count, STRETCH, TILE), bf16),
            pltpu.VMEM((8, STRETCH), f32),
            pltpu.VMEM((8, STRETCH), f32),
            pltpu.SemaphoreType.DMA((3,)),
            pltpu.SemaphoreType.DMA,
            pltpu.SemaphoreType.DMA,
            pltpu.SemaphoreType.DMA((pair_count,)),
            pltpu.SemaphoreType.DMA((pair_count,)),
            pltpu.SemaphoreType.DMA((pair_count,)),
            pltpu.SemaphoreType.DMA((pair_count,)),
            pltpu.SemaphoreType.DMA((pair_count,)),
            pltpu.SemaphoreType.DMA((pair_count,)),
            pltpu.SemaphoreType.DMA((tile_count,)),
            pltpu.SemaphoreType.DMA((tile_count,)),
            pltpu.SemaphoreType.DMA,
            pltpu.SemaphoreType.DMA,
        ],
        compiler_params=pltpu.CompilerParams(
            collective_id=0, has_side_effects=True, vmem_limit_bytes=60 * 1024 * 1024
        ),
    )(
        signal,
        gate_branch,
        write_proj,
        read_proj,
        step_logits,
        valid_mask[None, :],
        stretch_band,
        band_offset,
        decay_log[None, :],
        step_offset[None, :],
        skip_gain[None, :],
        norm_gain.reshape(pair_count, LANES),
        out_weight,
    )


def solution(mesh):
    placed = (
        P(("group", "scan", "band"), "tensor"),
        P(("group", "scan", "band"), "tensor"),
        P(("group", "scan", "band"), None),
        P(("group", "scan", "band"), None),
        P("tensor", ("group", "scan", "band")),
        P(("group", "scan", "band")),
        P(("group", "scan", "band")),
        P(None, "tensor"),
        P("tensor"),
        P("tensor"),
        P("tensor"),
        P("tensor"),
        P("tensor", None),
    )
    shape = dict(mesh.shape)
    places = shape["scan"] * shape["band"]

    def layer(*arrays):
        rows = arrays[0].shape[0] // (shape["group"] * places)
        heads = arrays[8].shape[0] // shape["tensor"]
        width = arrays[12].shape[1]
        fits = (
            shape["tensor"] == 2
            and shape["band"] == 2
            and shape["scan"] >= 2
            and rows == STRETCH
            and heads % (2 * STATE_PAIRS) == 0
            and heads % (2 * MIX_PAIRS) == 0
            and heads % (2 * GATE_PAIRS) == 0
            and 3 * heads <= LANES
            and width % (2 * TILE) == 0
        )
        member = on_device
        if fits:
            member = functools.partial(fused_on_device, shape["scan"])
        return mapped(member)(*arrays)

    def mapped(member):
        return jax.shard_map(
            member,
            mesh=mesh,
            in_specs=placed,
            out_specs=P(("group", "scan", "band"), "tensor"),
            check_vma=False,
        )

    return layer
```

```python
import functools

import jax
import jax.numpy as jnp
from jax import lax
from jax.experimental import pallas as pl
from jax.experimental.pallas import tpu as pltpu
from jax.sharding import PartitionSpec as P

HEAD_DIM = 64
STATE = 128
STRETCH = 256
BANDS = 12
INNER = 5120


EPSILON = 1e-05
HIGHEST = lax.Precision.HIGHEST


def step_sizes(step_logits, stretch_band, band_offset, step_offset):
    one_hot = (stretch_band[:, None] == jnp.arange(BANDS, dtype=jnp.int32)[None, :]).astype(
        jnp.float32
    )
    stretch_offset = jnp.dot(one_hot, band_offset, precision=HIGHEST)
    token_offset = jnp.repeat(stretch_offset, STRETCH, axis=0).T
    return jax.nn.softplus(step_logits + step_offset[:, None] + token_offset)


def combine(earlier, later_pair):
    return (
        earlier[0] + later_pair[0],
        jnp.exp(later_pair[0])[:, None, None] * earlier[1] + later_pair[1],
    )


def local_step(running_pair, member):
    return (combine(running_pair, member), running_pair)


def on_device(
    signal,
    gate_branch,
    write_proj,
    read_proj,
    step_logits,
    valid_mask,
    stretch_band,
    band_offset,
    decay_log,
    step_offset,
    skip_gain,
    norm_gain,
    out_weight,
):
    row_count = signal.shape[0]
    head_count = decay_log.shape[0]
    block_count = row_count // STRETCH
    step_size = step_sizes(step_logits, stretch_band, band_offset, step_offset)
    log_decay = step_size * (-jnp.exp(decay_log))[:, None]
    input_weight = step_size * valid_mask.astype(jnp.float32)[None, :]
    running = lax.associative_scan(
        jnp.add, log_decay.reshape(head_count, block_count, STRETCH), axis=2
    )
    weight_blocks = input_weight.reshape(head_count, block_count, STRETCH)
    signal_blocks = signal.reshape(block_count, STRETCH, head_count, HEAD_DIM)
    write_blocks = write_proj.reshape(block_count, STRETCH, STATE)
    read_blocks = read_proj.reshape(block_count, STRETCH, STATE)
    scores = jnp.einsum(
        "cin,cjn->cij", read_blocks, write_blocks, preferred_element_type=jnp.float32
    )
    lower_mask = jnp.arange(STRETCH)[:, None] >= jnp.arange(STRETCH)[None, :]
    span_logs = jnp.where(
        lower_mask[None, None], running[:, :, :, None] - running[:, :, None, :], -1e30
    )
    mixing = (jnp.exp(span_logs) * scores[None] * weight_blocks[:, :, None, :]).astype(jnp.bfloat16)
    local_out = jnp.einsum(
        "hcij,cjhp->cihp", mixing, signal_blocks, preferred_element_type=jnp.float32
    )
    tail_weight = jnp.exp(running[:, :, -1:] - running) * weight_blocks
    scaled = (
        signal_blocks.astype(jnp.float32) * jnp.transpose(tail_weight, (1, 2, 0))[:, :, :, None]
    ).astype(jnp.bfloat16)
    block_states = jnp.einsum(
        "cjhp,cjn->chpn", scaled, write_blocks, preferred_element_type=jnp.float32
    )
    block_decay = running[:, :, -1].T
    zero_state = jnp.zeros((head_count, HEAD_DIM, STATE), jnp.float32)
    zero_log = jnp.zeros((head_count,), jnp.float32)
    identity = (zero_log, zero_state)
    device_pair, segment_cumulative = lax.scan(local_step, identity, (block_decay, block_states))
    all_logs = lax.all_gather(device_pair[0][None], ("scan", "band"), axis=0, tiled=True)
    inclusive = lax.associative_scan(jnp.add, all_logs, axis=0)
    exclusive = inclusive - all_logs
    position = lax.axis_index(("scan", "band"))
    own_exclusive = lax.dynamic_index_in_dim(exclusive, position, 0, keepdims=False)
    shard_block = lax.all_gather(
        device_pair[1][None].astype(jnp.bfloat16), ("scan", "band"), axis=0, tiled=True
    ).astype(jnp.float32)
    how_many = shard_block.shape[0]
    sources = jnp.arange(how_many, dtype=jnp.int32)
    gap_logs = jnp.where((sources < position)[:, None], own_exclusive[None, :] - inclusive, -1e30)
    carry_state = zero_state + jnp.einsum(
        "kh,khpn->hpn", jnp.exp(gap_logs), shard_block, precision=HIGHEST
    )
    enter_state = (
        jnp.exp(segment_cumulative[0])[:, :, None, None] * carry_state[None] + segment_cumulative[1]
    )
    state_high = enter_state.astype(jnp.bfloat16)
    widened = lax.optimization_barrier(state_high).astype(jnp.float32)
    state_low = (enter_state - widened).astype(jnp.bfloat16)
    high_part = jnp.einsum(
        "cin,chpn->cihp", read_blocks, state_high, preferred_element_type=jnp.float32
    )
    low_part = jnp.einsum(
        "cin,chpn->cihp", read_blocks, state_low, preferred_element_type=jnp.float32
    )
    carried_out = jnp.transpose(jnp.exp(running), (1, 2, 0))[:, :, :, None] * (high_part + low_part)
    ssm_out = (local_out + carried_out).reshape(row_count, head_count, HEAD_DIM) + skip_gain[
        None, :, None
    ] * signal.reshape(row_count, head_count, HEAD_DIM).astype(jnp.float32)
    gated_out = ssm_out.reshape(row_count, head_count * HEAD_DIM) * jax.nn.silu(
        gate_branch.astype(jnp.float32)
    )
    square_total = lax.psum(jnp.sum(gated_out * gated_out, axis=1), "tensor")
    normed = (
        gated_out * lax.rsqrt(square_total / INNER + EPSILON)[:, None] * norm_gain[None, :]
    ).astype(jnp.bfloat16)
    own_columns = lax.psum_scatter(
        lax.dot_general(
            out_weight, normed, (((0,), (1,)), ((), ())), preferred_element_type=jnp.float32
        ).astype(jnp.bfloat16),
        "tensor",
        scatter_dimension=0,
        tiled=True,
    ).astype(jnp.float32)
    return own_columns.T.astype(jnp.bfloat16)


LOG2E = 1.4426950408889634
LANES = 128
STATE_PAIRS = 4
MIX_PAIRS = 2
EARLY_GROUP = 3
GATE_PAIRS = 2
TILE = 256
MESH = pl.DeviceIdType.MESH


def fused_kernel(
    heads,
    span_count,
    signal_hbm,
    gate_hbm,
    write_ref,
    read_ref,
    logits_ref,
    valid_ref,
    band_ref,
    offset_ref,
    decay_ref,
    bias_ref,
    skip_ref,
    gain_ref,
    weight_hbm,
    out_ref,
    weight_ref,
    signal_ref,
    gate_ref,
    padded_ref,
    params_ref,
    row_ref,
    run_ref,
    in_weight_ref,
    last_ref,
    skip_rows_ref,
    scores_ref,
    read_by_token_ref,
    lead_ref,
    fed_ref,
    state_ref,
    totals_ref,
    core_totals_ref,
    local_ref,
    normed_ref,
    square_ref,
    carry_ref,
    pass_ref,
    core_state_ref,
    entry_ref,
    sent_ref,
    own_ref,
    landed_ref,
    square_out_ref,
    square_in_ref,
    load_sem,
    totals_send,
    totals_recv,
    core_send,
    core_recv,
    onward_send,
    onward_recv,
    tile_send,
    tile_recv,
    square_send,
    square_recv,
):
    pair_count = heads // 2
    scan_index = lax.axis_index("scan")
    band_index = lax.axis_index("band")
    tensor_index = lax.axis_index("tensor")
    first_core = band_index == 0
    second_core = band_index == 1
    first_chip = scan_index == 0
    has_previous = second_core & (scan_index > 0)
    has_next = second_core & (scan_index < span_count - 1)
    gets_entry = first_core & (scan_index > 0)
    peer = 1 - tensor_index
    other_core = {"band": 1 - band_index}
    following = {"scan": lax.rem(scan_index + 1, span_count)}
    previous = {"scan": lax.rem(scan_index + span_count - 1, span_count)}

    barrier = pltpu.get_barrier_semaphore()
    for target in (other_core, {"tensor": peer}):
        pl.semaphore_signal(barrier, inc=1, device_id=target, device_id_type=MESH)

    @pl.when(has_next)
    def _():
        pl.semaphore_signal(barrier, inc=1, device_id=following, device_id_type=MESH)

    @pl.when(has_previous)
    def _():
        pl.semaphore_signal(barrier, inc=1, device_id=previous, device_id_type=MESH)

    signal_load = pltpu.make_async_copy(signal_hbm, signal_ref, load_sem.at[2])
    gate_load = pltpu.make_async_copy(gate_hbm, gate_ref, load_sem.at[0])
    weight_load = pltpu.make_async_copy(weight_hbm, weight_ref, load_sem.at[1])
    signal_load.start()
    gate_load.start()
    weight_load.start()

    padded_ref[...] = jnp.zeros_like(padded_ref)
    padded_ref[0:heads, :] = logits_ref[...]
    params_ref[...] = jnp.zeros_like(params_ref)
    chosen = lax.broadcasted_iota(jnp.int32, (BANDS, heads), 0) == band_ref[0]
    params_ref[0:1, 0:heads] = bias_ref[...] + jnp.sum(
        jnp.where(chosen, offset_ref[...], 0.0), axis=0, keepdims=True
    )
    params_ref[1:2, 0:heads] = jnp.exp(decay_ref[...])
    params_ref[2:3, 0:heads] = skip_ref[...]
    shifted = padded_ref[...].T + params_ref[0:1, :]
    step_size = jnp.maximum(shifted, 0.0) + jnp.log1p(jnp.exp(-jnp.abs(shifted)))
    lanes = lax.broadcasted_iota(jnp.int32, (STRETCH, LANES), 1)
    tokens = lax.broadcasted_iota(jnp.int32, (STRETCH, LANES), 0)
    real = lanes < heads
    running = jnp.where(real, step_size * -params_ref[1:2, :], 0.0)
    shift = 1
    while shift < STRETCH:
        running = running + jnp.where(tokens >= shift, pltpu.roll(running, shift, 0), 0.0)
        shift *= 2
    running = running * LOG2E
    row_ref[...] = running.T
    valid = jnp.broadcast_to(valid_ref[...].astype(jnp.float32), (LANES, STRETCH)).T
    in_weight = jnp.where(real, step_size * valid, 0.0)

    def three_parts(value):
        high = value.astype(jnp.bfloat16).astype(jnp.float32)
        rest = value - high
        middle = rest.astype(jnp.bfloat16).astype(jnp.float32)
        low = rest - middle
        packed = high + pltpu.roll(middle, heads, 1) + pltpu.roll(low, 2 * heads, 1)
        return packed.astype(jnp.bfloat16)

    running_parts = three_parts(running)
    run_ref[...] = running
    in_weight_ref[...] = in_weight
    skip_rows_ref[...] = three_parts(jnp.broadcast_to(params_ref[2:3, :], (16, LANES)))
    part = lax.broadcasted_iota(jnp.int32, (LANES, 2 * LANES), 0)
    part = (
        part
        - jnp.where(part >= heads, heads, 0)
        - jnp.where(part >= 2 * heads, heads, 0)
    )
    head_of = lax.broadcasted_iota(jnp.int32, totals_ref.shape, 1)
    head_of = (
        head_of
        - jnp.where(head_of >= heads, heads, 0)
        - jnp.where(head_of >= 2 * heads, heads, 0)
    )
    own_pair = head_of // 2 == lax.broadcasted_iota(jnp.int32, totals_ref.shape, 0)
    last_parts = running_parts[STRETCH - 16 : STRETCH].astype(jnp.float32)[15:16, :]
    last_rows = (
        jnp.dot(
            jnp.where(own_pair, last_parts, 0.0).astype(jnp.bfloat16),
            jnp.where(
                part[:, 0:LANES] % 2
                == lax.broadcasted_iota(jnp.int32, (LANES, LANES), 1) // HEAD_DIM,
                1.0,
                0.0,
            ).astype(jnp.bfloat16),
            preferred_element_type=jnp.float32,
        )
    )
    last_ref[...] = last_rows
    totals_ref[...] = jnp.exp2(last_rows)
    write_turned = write_ref[...].astype(jnp.float32).T.astype(jnp.bfloat16)
    read_by_token_ref[...] = write_turned
    scores = jnp.dot(read_ref[...], write_turned, preferred_element_type=jnp.float32)
    square_rows = lax.broadcasted_iota(jnp.int32, (STRETCH, STRETCH), 0)
    square_columns = lax.broadcasted_iota(jnp.int32, (STRETCH, STRETCH), 1)
    scores_ref[...] = jnp.where(square_columns <= square_rows, scores, 0.0)
    square_ref[...] = jnp.zeros_like(square_ref)

    @pl.when(first_core & first_chip)
    def _():
        carry_ref[...] = jnp.zeros_like(carry_ref)

    totals_copy = pltpu.make_async_remote_copy(
        src_ref=totals_ref,
        dst_ref=core_totals_ref,
        send_sem=totals_send,
        recv_sem=totals_recv,
        device_id=other_core,
        device_id_type=MESH,
    )

    def core_copy(pair):
        return pltpu.make_async_remote_copy(
            src_ref=pass_ref.at[pair],
            dst_ref=core_state_ref.at[pair],
            send_sem=core_send,
            recv_sem=core_recv.at[pair],
            device_id=other_core,
            device_id_type=MESH,
        )

    def onward_copy(pair):
        return pltpu.make_async_remote_copy(
            src_ref=pass_ref.at[pair],
            dst_ref=entry_ref.at[pair],
            send_sem=onward_send,
            recv_sem=onward_recv.at[pair],
            device_id=following,
            device_id_type=MESH,
        )

    def entry_copy(pair):
        return pltpu.make_async_remote_copy(
            src_ref=entry_ref.at[pair],
            dst_ref=carry_ref.at[pair],
            send_sem=core_send,
            recv_sem=core_recv.at[pair],
            device_id=other_core,
            device_id_type=MESH,
        )

    def give_onward(pair, carry):
        onward = totals_ref[pl.ds(pair, 1), :] * carry + state_ref[pair]
        pass_ref[pair] = onward.astype(jnp.bfloat16)
        onward_copy(pair).start()

    def first_chain_step(pair):
        core_copy(pair).wait_recv()
        own = core_state_ref[pair]
        carry_ref[pair] = own

        @pl.when(has_next)
        def _():
            give_onward(pair, own.astype(jnp.float32))

    def chain_step(pair):
        core_copy(pair).wait_recv()
        onward_copy(pair).wait_recv()
        carry = core_totals_ref[pl.ds(pair, 1), :] * entry_ref[pair].astype(
            jnp.float32
        ) + core_state_ref[pair].astype(jnp.float32)

        @pl.when(has_next)
        def _():
            give_onward(pair, carry)

        entry_copy(pair).start()
        carry_ref[pair] = carry.astype(jnp.bfloat16)

    def columns_of(pair):
        return pl.ds(pl.multiple_of(pair * LANES, LANES), LANES)

    narrow_side = lax.broadcasted_iota(jnp.int32, (LANES, LANES), 1) // HEAD_DIM
    narrow_index = part[:, 0:LANES] - narrow_side
    first_half = lanes < HEAD_DIM

    def picker(index, pair):
        return jnp.where(index == 2 * pair, 1.0, 0.0).astype(jnp.bfloat16)

    def spread(values, index):
        return jnp.take_along_axis(values, index, axis=1, mode="promise_in_bounds")

    def state_pair(pair):
        columns = columns_of(pair)
        index = 2 * pair + lanes // HEAD_DIM
        own_run = spread(run_ref[...], index)
        weight = spread(in_weight_ref[...], index)
        last_run = last_ref[pl.ds(pair, 1), :]
        fed = signal_ref[:, columns].astype(jnp.float32) * weight
        fed_ref[:, columns] = fed.astype(jnp.bfloat16)
        lead_ref[:, columns] = jnp.exp2(own_run)
        scaled = (fed * jnp.exp2(last_run - own_run)).astype(jnp.bfloat16)
        state = jnp.dot(read_by_token_ref[...], scaled, preferred_element_type=jnp.float32)
        state_ref[pair] = state
        pass_ref[pair] = state.astype(jnp.bfloat16)


    def mix_pair(pair):
        columns = columns_of(pair)
        half = STRETCH // 2
        tops, bottoms = [], []
        fed = fed_ref[:, columns]
        for side in range(2):
            row = row_ref[pl.ds(2 * pair + side, 1), :]
            run = spread(run_ref[...], jnp.full((STRETCH, LANES), 2 * pair + side, jnp.int32))
            near = jnp.exp2(jnp.minimum(run[0:half] - row[:, 0:half], 0.0))
            far = jnp.exp2(jnp.minimum(run[half:] - row[:, 0:half], 0.0))
            late = jnp.exp2(jnp.minimum(run[half:] - row[:, half:], 0.0))
            near = (near * scores_ref[0:half, 0:half]).astype(jnp.bfloat16)
            far = (far * scores_ref[half:, 0:half]).astype(jnp.bfloat16)
            late = (late * scores_ref[half:, half:]).astype(jnp.bfloat16)
            tops.append(jnp.dot(near, fed[0:half], preferred_element_type=jnp.float32))
            bottoms.append(
                jnp.dot(
                    jnp.concatenate([far, late], axis=1), fed, preferred_element_type=jnp.float32
                )
            )
        local_ref[0:half, columns] = jnp.where(first_half[0:half], tops[0], tops[1])
        local_ref[half:, columns] = jnp.where(first_half[half:], bottoms[0], bottoms[1])

    def gate_pair(pair):
        columns = columns_of(pair)
        carried = jnp.dot(read_ref[...], carry_ref[pair], preferred_element_type=jnp.float32)
        skip = jnp.dot(
            skip_rows_ref[...], picker(narrow_index, pair), preferred_element_type=jnp.float32
        )
        ssm_out = (
            local_ref[:, columns]
            + lead_ref[:, columns] * carried
            + skip[0:1, :] * signal_ref[:, columns].astype(jnp.float32)
        )
        gate = gate_ref[:, columns].astype(jnp.float32)
        gated = ssm_out * (gate / (1.0 + jnp.exp(-gate)))
        normed_ref[:, columns] = (gated * gain_ref[pl.ds(pair, 1), :]).astype(jnp.bfloat16)
        return gated * gated

    signal_load.wait()

    @pl.loop(0, pair_count // STATE_PAIRS)
    def _(group):
        for member in range(STATE_PAIRS):
            state_pair(group * STATE_PAIRS + member)

        @pl.when(group == 0)
        def _():
            pl.semaphore_wait(
                barrier, 2 + jnp.where(has_next, 1, 0) + jnp.where(has_previous, 1, 0)
            )

            @pl.when(first_core)
            def _():
                totals_copy.start()

        @pl.when(first_core)
        def _():
            for member in range(STATE_PAIRS):
                core_copy(group * STATE_PAIRS + member).start()

        @pl.when(second_core & first_chip & (group > 0))
        def _():
            for member in range(STATE_PAIRS):
                first_chain_step((group - 1) * STATE_PAIRS + member)

        @pl.when(second_core & (group == EARLY_GROUP))
        def _():
            totals_copy.wait_recv()

        @pl.when(has_previous & has_next & (scan_index == 1) & (group >= EARLY_GROUP))
        def _():
            for member in range(2):
                chain_step((group - EARLY_GROUP) * 2 + member)

    @pl.when(second_core & first_chip)
    def _():
        for member in range(STATE_PAIRS):
            first_chain_step(pair_count - STATE_PAIRS + member)

    early_count = 2 * (pair_count // STATE_PAIRS - EARLY_GROUP)

    @pl.loop(0, pair_count // MIX_PAIRS)
    def _(group):
        chunk = group * MIX_PAIRS + jnp.where(scan_index == 1, early_count, 0)

        @pl.when(has_previous & has_next & (chunk < pair_count))
        def _():
            for member in range(MIX_PAIRS):
                chain_step(chunk + member)

        for member in range(MIX_PAIRS):
            mix_pair(group * MIX_PAIRS + member)

    gate_load.wait()
    last_step = has_previous & (scan_index == span_count - 1)

    @pl.loop(0, pair_count // GATE_PAIRS)
    def _(group):
        @pl.when(last_step)
        def _():
            for member in range(GATE_PAIRS):
                chain_step(group * GATE_PAIRS + member)

        @pl.when(gets_entry)
        def _():
            for member in range(GATE_PAIRS):
                entry_copy(group * GATE_PAIRS + member).wait_recv()

        squares = square_ref[...]
        for member in range(GATE_PAIRS):
            squares = squares + gate_pair(group * GATE_PAIRS + member)
        square_ref[...] = squares

    weight_load.wait()
    own_width = out_ref.shape[1]
    tile_count = own_width // TILE

    def tile_copy(tile):
        return pltpu.make_async_remote_copy(
            src_ref=sent_ref.at[tile],
            dst_ref=landed_ref.at[tile],
            send_sem=tile_send,
            recv_sem=tile_recv.at[tile],
            device_id={"tensor": peer},
            device_id_type=MESH,
        )

    def project(owner, tile):
        start = pl.multiple_of(owner * own_width + tile * TILE, LANES)
        return jnp.dot(
            normed_ref[...], weight_ref[:, pl.ds(start, TILE)], preferred_element_type=jnp.float32
        )

    sent_ref[0] = project(peer, 0).astype(jnp.bfloat16)
    tile_copy(0).start()
    square_sum = jnp.sum(square_ref[...].T, axis=0, keepdims=True)
    square_out_ref[...] = jnp.broadcast_to(square_sum, square_out_ref.shape)
    square_copy = pltpu.make_async_remote_copy(
        src_ref=square_out_ref,
        dst_ref=square_in_ref,
        send_sem=square_send,
        recv_sem=square_recv,
        device_id={"tensor": peer},
        device_id_type=MESH,
    )
    square_copy.start()

    @pl.loop(1, tile_count)
    def _(tile):
        sent_ref[tile] = project(peer, tile).astype(jnp.bfloat16)
        tile_copy(tile).start()

    @pl.loop(0, tile_count)
    def _(tile):
        own_ref[tile] = project(tensor_index, tile)

    @pl.when(first_core)
    def _():
        totals_copy.wait_send()

    @pl.when(first_core | has_previous)
    def _():
        pltpu.make_async_copy(pass_ref, pass_ref, core_send).wait()

    @pl.when(has_next)
    def _():
        pltpu.make_async_copy(pass_ref, pass_ref, onward_send).wait()

    square_copy.wait()
    inner = 2 * heads * HEAD_DIM
    scale = lax.rsqrt((square_out_ref[0:1, :] + square_in_ref[0:1, :]) / inner + EPSILON)
    square_ref[...] = jnp.broadcast_to(scale, (LANES, STRETCH)).T

    @pl.loop(0, tile_count)
    def _(tile):
        tile_copy(tile).wait_recv()
        scales = square_ref[...]
        for side in range(TILE // LANES):
            start = pl.multiple_of(tile * TILE + side * LANES, LANES)
            columns = slice(side * LANES, (side + 1) * LANES)
            both = own_ref[tile, :, columns] + landed_ref[tile, :, columns].astype(jnp.float32)
            out_ref[:, pl.ds(start, LANES)] = (both * scales).astype(jnp.bfloat16)

    pltpu.make_async_copy(sent_ref, sent_ref, tile_send).wait()


def fused_on_device(
    span_count,
    signal,
    gate_branch,
    write_proj,
    read_proj,
    step_logits,
    valid_mask,
    stretch_band,
    band_offset,
    decay_log,
    step_offset,
    skip_gain,
    norm_gain,
    out_weight,
):
    heads = decay_log.shape[0]
    inner = heads * HEAD_DIM
    width = out_weight.shape[1]
    pair_count = heads // 2
    tile_count = width // 2 // TILE
    vmem = pl.BlockSpec(memory_space=pltpu.VMEM)
    hbm = pl.BlockSpec(memory_space=pl.ANY)
    smem = pl.BlockSpec(memory_space=pltpu.SMEM)
    f32, bf16 = jnp.float32, jnp.bfloat16
    return pl.pallas_call(
        functools.partial(fused_kernel, heads, span_count),
        out_shape=pltpu.VMEM((STRETCH, width // 2), bf16),
        in_specs=[hbm, hbm] + [vmem] * 4 + [smem] + [vmem] * 5 + [hbm],
        out_specs=vmem,
        scratch_shapes=[
            pltpu.VMEM((inner, width), bf16),
            pltpu.VMEM((STRETCH, inner), bf16),
            pltpu.VMEM((STRETCH, inner), bf16),
            pltpu.VMEM((LANES, STRETCH), f32),
            pltpu.VMEM((8, LANES), f32),
            pltpu.VMEM((LANES, STRETCH), f32),
            pltpu.VMEM((STRETCH, LANES), f32),
            pltpu.VMEM((STRETCH, LANES), f32),
            pltpu.VMEM((-(-pair_count // 16) * 16, LANES), f32),
            pltpu.VMEM((16, LANES), bf16),
            pltpu.VMEM((STRETCH, STRETCH), f32),
            pltpu.VMEM((STATE, STRETCH), bf16),
            pltpu.VMEM((STRETCH, inner), f32),
            pltpu.VMEM((STRETCH, inner), bf16),
            pltpu.VMEM((pair_count, STATE, LANES), f32),
            pltpu.VMEM((-(-pair_count // 16) * 16, LANES), f32),
            pltpu.VMEM((-(-pair_count // 16) * 16, LANES), f32),
            pltpu.VMEM((STRETCH, inner), f32),
            pltpu.VMEM((STRETCH, inner), bf16),
            pltpu.VMEM((STRETCH, LANES), f32),
            pltpu.VMEM((pair_count, STATE, LANES), bf16),
            pltpu.VMEM((pair_count, STATE, LANES), bf16),
            pltpu.VMEM((pair_count, STATE, LANES), bf16),
            pltpu.VMEM((pair_count, STATE, LANES), bf16),
            pltpu.VMEM((tile_count, STRETCH, TILE), bf16),
            pltpu.VMEM((tile_count, STRETCH, TILE), f32),
            pltpu.VMEM((tile_count, STRETCH, TILE), bf16),
            pltpu.VMEM((8, STRETCH), f32),
            pltpu.VMEM((8, STRETCH), f32),
            pltpu.SemaphoreType.DMA((3,)),
            pltpu.SemaphoreType.DMA,
            pltpu.SemaphoreType.DMA,
            pltpu.SemaphoreType.DMA,
            pltpu.SemaphoreType.DMA((pair_count,)),
            pltpu.SemaphoreType.DMA,
            pltpu.SemaphoreType.DMA((pair_count,)),
            pltpu.SemaphoreType.DMA,
            pltpu.SemaphoreType.DMA((tile_count,)),
            pltpu.SemaphoreType.DMA,
            pltpu.SemaphoreType.DMA,
        ],
        compiler_params=pltpu.CompilerParams(
            collective_id=0, has_side_effects=True, vmem_limit_bytes=60 * 1024 * 1024
        ),
    )(
        signal,
        gate_branch,
        write_proj,
        read_proj,
        step_logits,
        valid_mask[None, :],
        stretch_band,
        band_offset,
        decay_log[None, :],
        step_offset[None, :],
        skip_gain[None, :],
        norm_gain.reshape(pair_count, LANES),
        out_weight,
    )


def solution(mesh):
    placed = (
        P(("group", "scan", "band"), "tensor"),
        P(("group", "scan", "band"), "tensor"),
        P(("group", "scan", "band"), None),
        P(("group", "scan", "band"), None),
        P("tensor", ("group", "scan", "band")),
        P(("group", "scan", "band")),
        P(("group", "scan", "band")),
        P(None, "tensor"),
        P("tensor"),
        P("tensor"),
        P("tensor"),
        P("tensor"),
        P("tensor", None),
    )
    shape = dict(mesh.shape)
    places = shape["scan"] * shape["band"]

    def layer(*arrays):
        rows = arrays[0].shape[0] // (shape["group"] * places)
        heads = arrays[8].shape[0] // shape["tensor"]
        width = arrays[12].shape[1]
        fits = (
            shape["tensor"] == 2
            and shape["band"] == 2
            and shape["scan"] >= 2
            and rows == STRETCH
            and heads % (2 * STATE_PAIRS) == 0
            and heads % (2 * MIX_PAIRS) == 0
            and heads % (2 * GATE_PAIRS) == 0
            and heads > 2 * STATE_PAIRS * EARLY_GROUP
            and 3 * heads <= LANES
            and width % (2 * TILE) == 0
        )
        member = on_device
        if fits:
            member = functools.partial(fused_on_device, shape["scan"])
        return mapped(member)(*arrays)

    def mapped(member):
        return jax.shard_map(
            member,
            mesh=mesh,
            in_specs=placed,
            out_specs=P(("group", "scan", "band"), "tensor"),
            check_vma=False,
        )

    return layer
```

```python
import functools

import jax
import jax.numpy as jnp
from jax import lax
from jax.experimental import pallas as pl
from jax.experimental.pallas import tpu as pltpu
from jax.sharding import PartitionSpec as P

HEAD_DIM = 64
STATE = 128
STRETCH = 256
BANDS = 12
INNER = 5120


EPSILON = 1e-05
HIGHEST = lax.Precision.HIGHEST


def step_sizes(step_logits, stretch_band, band_offset, step_offset):
    one_hot = (stretch_band[:, None] == jnp.arange(BANDS, dtype=jnp.int32)[None, :]).astype(
        jnp.float32
    )
    stretch_offset = jnp.dot(one_hot, band_offset, precision=HIGHEST)
    token_offset = jnp.repeat(stretch_offset, STRETCH, axis=0).T
    return jax.nn.softplus(step_logits + step_offset[:, None] + token_offset)


def combine(earlier, later_pair):
    return (
        earlier[0] + later_pair[0],
        jnp.exp(later_pair[0])[:, None, None] * earlier[1] + later_pair[1],
    )


def local_step(running_pair, member):
    return (combine(running_pair, member), running_pair)


def on_device(
    signal,
    gate_branch,
    write_proj,
    read_proj,
    step_logits,
    valid_mask,
    stretch_band,
    band_offset,
    decay_log,
    step_offset,
    skip_gain,
    norm_gain,
    out_weight,
):
    row_count = signal.shape[0]
    head_count = decay_log.shape[0]
    block_count = row_count // STRETCH
    step_size = step_sizes(step_logits, stretch_band, band_offset, step_offset)
    log_decay = step_size * (-jnp.exp(decay_log))[:, None]
    input_weight = step_size * valid_mask.astype(jnp.float32)[None, :]
    running = lax.associative_scan(
        jnp.add, log_decay.reshape(head_count, block_count, STRETCH), axis=2
    )
    weight_blocks = input_weight.reshape(head_count, block_count, STRETCH)
    signal_blocks = signal.reshape(block_count, STRETCH, head_count, HEAD_DIM)
    write_blocks = write_proj.reshape(block_count, STRETCH, STATE)
    read_blocks = read_proj.reshape(block_count, STRETCH, STATE)
    scores = jnp.einsum(
        "cin,cjn->cij", read_blocks, write_blocks, preferred_element_type=jnp.float32
    )
    lower_mask = jnp.arange(STRETCH)[:, None] >= jnp.arange(STRETCH)[None, :]
    span_logs = jnp.where(
        lower_mask[None, None], running[:, :, :, None] - running[:, :, None, :], -1e30
    )
    mixing = (jnp.exp(span_logs) * scores[None] * weight_blocks[:, :, None, :]).astype(jnp.bfloat16)
    local_out = jnp.einsum(
        "hcij,cjhp->cihp", mixing, signal_blocks, preferred_element_type=jnp.float32
    )
    tail_weight = jnp.exp(running[:, :, -1:] - running) * weight_blocks
    scaled = (
        signal_blocks.astype(jnp.float32) * jnp.transpose(tail_weight, (1, 2, 0))[:, :, :, None]
    ).astype(jnp.bfloat16)
    block_states = jnp.einsum(
        "cjhp,cjn->chpn", scaled, write_blocks, preferred_element_type=jnp.float32
    )
    block_decay = running[:, :, -1].T
    zero_state = jnp.zeros((head_count, HEAD_DIM, STATE), jnp.float32)
    zero_log = jnp.zeros((head_count,), jnp.float32)
    identity = (zero_log, zero_state)
    device_pair, segment_cumulative = lax.scan(local_step, identity, (block_decay, block_states))
    all_logs = lax.all_gather(device_pair[0][None], ("scan", "band"), axis=0, tiled=True)
    inclusive = lax.associative_scan(jnp.add, all_logs, axis=0)
    exclusive = inclusive - all_logs
    position = lax.axis_index(("scan", "band"))
    own_exclusive = lax.dynamic_index_in_dim(exclusive, position, 0, keepdims=False)
    shard_block = lax.all_gather(
        device_pair[1][None].astype(jnp.bfloat16), ("scan", "band"), axis=0, tiled=True
    ).astype(jnp.float32)
    how_many = shard_block.shape[0]
    sources = jnp.arange(how_many, dtype=jnp.int32)
    gap_logs = jnp.where((sources < position)[:, None], own_exclusive[None, :] - inclusive, -1e30)
    carry_state = zero_state + jnp.einsum(
        "kh,khpn->hpn", jnp.exp(gap_logs), shard_block, precision=HIGHEST
    )
    enter_state = (
        jnp.exp(segment_cumulative[0])[:, :, None, None] * carry_state[None] + segment_cumulative[1]
    )
    state_high = enter_state.astype(jnp.bfloat16)
    widened = lax.optimization_barrier(state_high).astype(jnp.float32)
    state_low = (enter_state - widened).astype(jnp.bfloat16)
    high_part = jnp.einsum(
        "cin,chpn->cihp", read_blocks, state_high, preferred_element_type=jnp.float32
    )
    low_part = jnp.einsum(
        "cin,chpn->cihp", read_blocks, state_low, preferred_element_type=jnp.float32
    )
    carried_out = jnp.transpose(jnp.exp(running), (1, 2, 0))[:, :, :, None] * (high_part + low_part)
    ssm_out = (local_out + carried_out).reshape(row_count, head_count, HEAD_DIM) + skip_gain[
        None, :, None
    ] * signal.reshape(row_count, head_count, HEAD_DIM).astype(jnp.float32)
    gated_out = ssm_out.reshape(row_count, head_count * HEAD_DIM) * jax.nn.silu(
        gate_branch.astype(jnp.float32)
    )
    square_total = lax.psum(jnp.sum(gated_out * gated_out, axis=1), "tensor")
    normed = (
        gated_out * lax.rsqrt(square_total / INNER + EPSILON)[:, None] * norm_gain[None, :]
    ).astype(jnp.bfloat16)
    own_columns = lax.psum_scatter(
        lax.dot_general(
            out_weight, normed, (((0,), (1,)), ((), ())), preferred_element_type=jnp.float32
        ).astype(jnp.bfloat16),
        "tensor",
        scatter_dimension=0,
        tiled=True,
    ).astype(jnp.float32)
    return own_columns.T.astype(jnp.bfloat16)


LOG2E = 1.4426950408889634
LANES = 128
STATE_PAIRS = 4
MIX_PAIRS = 2
EARLY_GROUP = 3
GATE_PAIRS = 2
TILE = 256
MESH = pl.DeviceIdType.MESH


def fused_kernel(
    heads,
    span_count,
    signal_hbm,
    gate_hbm,
    write_hbm,
    read_hbm,
    logits_hbm,
    valid_hbm,
    band_hbm,
    offset_hbm,
    decay_hbm,
    bias_hbm,
    skip_hbm,
    gain_hbm,
    weight_hbm,
    out_ref,
    weight_ref,
    signal_ref,
    gate_ref,
    write_ref,
    read_ref,
    logits_ref,
    valid_ref,
    band_ref,
    offset_ref,
    decay_ref,
    bias_ref,
    skip_ref,
    gain_ref,
    padded_ref,
    params_ref,
    row_ref,
    run_ref,
    tail_ref,
    lead_ref,
    row_log_ref,
    skip_rows_ref,
    scores_ref,
    read_by_token_ref,
    state_ref,
    totals_ref,
    core_totals_ref,
    local_ref,
    normed_ref,
    square_ref,
    carry_ref,
    pass_ref,
    core_state_ref,
    entry_ref,
    sent_ref,
    own_ref,
    landed_ref,
    square_out_ref,
    square_in_ref,
    load_sem,
    small_sem,
    totals_send,
    totals_recv,
    core_send,
    core_recv,
    onward_send,
    onward_recv,
    tile_send,
    tile_recv,
    square_send,
    square_recv,
):
    pair_count = heads // 2
    scan_index = lax.axis_index("scan")
    band_index = lax.axis_index("band")
    tensor_index = lax.axis_index("tensor")
    first_core = band_index == 0
    second_core = band_index == 1
    first_chip = scan_index == 0
    has_previous = second_core & (scan_index > 0)
    has_next = second_core & (scan_index < span_count - 1)
    gets_entry = first_core & (scan_index > 0)
    peer = 1 - tensor_index
    other_core = {"band": 1 - band_index}
    following = {"scan": lax.rem(scan_index + 1, span_count)}
    previous = {"scan": lax.rem(scan_index + span_count - 1, span_count)}

    barrier = pltpu.get_barrier_semaphore()
    for target in (other_core, {"tensor": peer}):
        pl.semaphore_signal(barrier, inc=1, device_id=target, device_id_type=MESH)

    @pl.when(has_next)
    def _():
        pl.semaphore_signal(barrier, inc=1, device_id=following, device_id_type=MESH)

    @pl.when(has_previous)
    def _():
        pl.semaphore_signal(barrier, inc=1, device_id=previous, device_id_type=MESH)

    signal_load = pltpu.make_async_copy(signal_hbm, signal_ref, load_sem.at[2])
    gate_load = pltpu.make_async_copy(gate_hbm, gate_ref, load_sem.at[0])
    weight_load = pltpu.make_async_copy(weight_hbm, weight_ref, load_sem.at[1])
    small_loads = [
        pltpu.make_async_copy(source, target, small_sem.at[spot])
        for spot, (source, target) in enumerate(
            (
                (logits_hbm, logits_ref),
                (band_hbm, band_ref),
                (offset_hbm, offset_ref),
                (decay_hbm, decay_ref),
                (bias_hbm, bias_ref),
                (valid_hbm, valid_ref),
                (skip_hbm, skip_ref),
                (write_hbm, write_ref),
                (read_hbm, read_ref),
                (gain_hbm, gain_ref),
            )
        )
    ]
    for load in small_loads:
        load.start()
    signal_load.start()
    gate_load.start()
    weight_load.start()
    for load in small_loads:
        load.wait()

    padded_ref[...] = jnp.zeros_like(padded_ref)
    padded_ref[0:heads, :] = logits_ref[...]
    params_ref[...] = jnp.zeros_like(params_ref)
    chosen = lax.broadcasted_iota(jnp.int32, (BANDS, heads), 0) == band_ref[...]
    params_ref[0:1, 0:heads] = bias_ref[...] + jnp.sum(
        jnp.where(chosen, offset_ref[...], 0.0), axis=0, keepdims=True
    )
    params_ref[1:2, 0:heads] = jnp.exp(decay_ref[...])
    params_ref[2:3, 0:heads] = skip_ref[...]
    shifted = padded_ref[...].T + params_ref[0:1, :]
    step_size = jnp.maximum(shifted, 0.0) + jnp.log1p(jnp.exp(-jnp.abs(shifted)))
    lanes = lax.broadcasted_iota(jnp.int32, (STRETCH, LANES), 1)
    tokens = lax.broadcasted_iota(jnp.int32, (STRETCH, LANES), 0)
    real = lanes < heads
    running = jnp.where(real, step_size * -params_ref[1:2, :], 0.0)
    shift = 1
    while shift < STRETCH:
        running = running + jnp.where(tokens >= shift, pltpu.roll(running, shift, 0), 0.0)
        shift *= 2
    running = running * LOG2E
    running_rows = running.T
    valid = jnp.broadcast_to(valid_ref[...].astype(jnp.float32), (LANES, STRETCH)).T
    in_weight = jnp.where(real, step_size * valid, 0.0)

    def three_parts(value):
        high = value.astype(jnp.bfloat16).astype(jnp.float32)
        rest = value - high
        middle = rest.astype(jnp.bfloat16).astype(jnp.float32)
        low = rest - middle
        packed = high + pltpu.roll(middle, heads, 1) + pltpu.roll(low, 2 * heads, 1)
        return packed.astype(jnp.bfloat16)

    running_parts = three_parts(running)
    run_ref[...] = running
    weight_rows = in_weight.T
    weight_log = jnp.where(weight_rows > 0.0, jnp.log(weight_rows) * LOG2E, -1e30)
    row_log_ref[...] = weight_log
    row_ref[...] = running_rows - weight_log
    tail_ref[...] = jnp.exp2(running[STRETCH - 1 : STRETCH, :] - running) * in_weight
    lead_ref[...] = jnp.exp2(running)
    skip_rows_ref[...] = three_parts(jnp.broadcast_to(params_ref[2:3, :], (16, LANES)))
    part = lax.broadcasted_iota(jnp.int32, (LANES, 2 * LANES), 0)
    part = (
        part
        - jnp.where(part >= heads, heads, 0)
        - jnp.where(part >= 2 * heads, heads, 0)
    )
    head_of = lax.broadcasted_iota(jnp.int32, totals_ref.shape, 1)
    head_of = (
        head_of
        - jnp.where(head_of >= heads, heads, 0)
        - jnp.where(head_of >= 2 * heads, heads, 0)
    )
    own_pair = head_of // 2 == lax.broadcasted_iota(jnp.int32, totals_ref.shape, 0)
    last_parts = running_parts[STRETCH - 16 : STRETCH].astype(jnp.float32)[15:16, :]
    last_rows = (
        jnp.dot(
            jnp.where(own_pair, last_parts, 0.0).astype(jnp.bfloat16),
            jnp.where(
                part[:, 0:LANES] % 2
                == lax.broadcasted_iota(jnp.int32, (LANES, LANES), 1) // HEAD_DIM,
                1.0,
                0.0,
            ).astype(jnp.bfloat16),
            preferred_element_type=jnp.float32,
        )
    )
    totals_ref[...] = jnp.exp2(last_rows)
    write_turned = write_ref[...].astype(jnp.float32).T.astype(jnp.bfloat16)
    read_by_token_ref[...] = write_turned
    scores = jnp.dot(read_ref[...], write_turned, preferred_element_type=jnp.float32)
    square_rows = lax.broadcasted_iota(jnp.int32, (STRETCH, STRETCH), 0)
    square_columns = lax.broadcasted_iota(jnp.int32, (STRETCH, STRETCH), 1)
    scores_ref[...] = jnp.where(square_columns <= square_rows, scores, 0.0)
    square_ref[...] = jnp.zeros_like(square_ref)

    @pl.when(first_core & first_chip)
    def _():
        carry_ref[...] = jnp.zeros_like(carry_ref)

    totals_copy = pltpu.make_async_remote_copy(
        src_ref=totals_ref,
        dst_ref=core_totals_ref,
        send_sem=totals_send,
        recv_sem=totals_recv,
        device_id=other_core,
        device_id_type=MESH,
    )

    def core_copy(pair):
        return pltpu.make_async_remote_copy(
            src_ref=pass_ref.at[pair],
            dst_ref=core_state_ref.at[pair],
            send_sem=core_send,
            recv_sem=core_recv.at[pair],
            device_id=other_core,
            device_id_type=MESH,
        )

    def onward_copy(pair):
        return pltpu.make_async_remote_copy(
            src_ref=pass_ref.at[pair],
            dst_ref=entry_ref.at[pair],
            send_sem=onward_send,
            recv_sem=onward_recv.at[pair],
            device_id=following,
            device_id_type=MESH,
        )

    def entry_copy(pair):
        return pltpu.make_async_remote_copy(
            src_ref=entry_ref.at[pair],
            dst_ref=carry_ref.at[pair],
            send_sem=core_send,
            recv_sem=core_recv.at[pair],
            device_id=other_core,
            device_id_type=MESH,
        )

    def give_onward(pair, carry):
        onward = totals_ref[pl.ds(pair, 1), :] * carry + state_ref[pair]
        pass_ref[pair] = onward.astype(jnp.bfloat16)
        onward_copy(pair).start()

    def first_chain_step(pair):
        core_copy(pair).wait_recv()
        own = core_state_ref[pair]
        carry_ref[pair] = own

        @pl.when(has_next)
        def _():
            give_onward(pair, own.astype(jnp.float32))

    def chain_step(pair):
        core_copy(pair).wait_recv()
        onward_copy(pair).wait_recv()

        @pl.when(jnp.logical_not(has_next))
        def _():
            entry_copy(pair).start()

        carry = core_totals_ref[pl.ds(pair, 1), :] * entry_ref[pair].astype(
            jnp.float32
        ) + core_state_ref[pair].astype(jnp.float32)

        @pl.when(has_next)
        def _():
            give_onward(pair, carry)
            entry_copy(pair).start()

        carry_ref[pair] = carry.astype(jnp.bfloat16)

    def columns_of(pair):
        return pl.ds(pl.multiple_of(pair * LANES, LANES), LANES)

    narrow_side = lax.broadcasted_iota(jnp.int32, (LANES, LANES), 1) // HEAD_DIM
    narrow_index = part[:, 0:LANES] - narrow_side
    first_half = lanes < HEAD_DIM

    def picker(index, pair):
        return jnp.where(index == 2 * pair, 1.0, 0.0).astype(jnp.bfloat16)

    def spread(values, index):
        return jnp.take_along_axis(values, index, axis=1, mode="promise_in_bounds")

    def pair_heads(pair):
        return 2 * pair + lanes // HEAD_DIM

    def state_pair(pair):
        columns = columns_of(pair)
        tail = spread(tail_ref[...], pair_heads(pair))
        scaled = (signal_ref[:, columns].astype(jnp.float32) * tail).astype(jnp.bfloat16)
        state = jnp.dot(read_by_token_ref[...], scaled, preferred_element_type=jnp.float32)
        state_ref[pair] = state
        pass_ref[pair] = state.astype(jnp.bfloat16)


    def mix_pair(pair):
        columns = columns_of(pair)
        half = STRETCH // 2
        tops, bottoms = [], []
        fed = signal_ref[:, columns]
        for side in range(2):
            row = row_ref[pl.ds(2 * pair + side, 1), :]
            most = row_log_ref[pl.ds(2 * pair + side, 1), :]
            run = spread(run_ref[...], jnp.full((STRETCH, LANES), 2 * pair + side, jnp.int32))
            near = jnp.exp2(jnp.minimum(run[0:half] - row[:, 0:half], most[:, 0:half]))
            far = jnp.exp2(run[half:] - row[:, 0:half])
            late = jnp.exp2(jnp.minimum(run[half:] - row[:, half:], most[:, half:]))
            near = (near * scores_ref[0:half, 0:half]).astype(jnp.bfloat16)
            far = (far * scores_ref[half:, 0:half]).astype(jnp.bfloat16)
            late = (late * scores_ref[half:, half:]).astype(jnp.bfloat16)
            tops.append(jnp.dot(near, fed[0:half], preferred_element_type=jnp.float32))
            bottoms.append(
                jnp.dot(
                    jnp.concatenate([far, late], axis=1), fed, preferred_element_type=jnp.float32
                )
            )
        local_ref[0:half, columns] = jnp.where(first_half[0:half], tops[0], tops[1])
        local_ref[half:, columns] = jnp.where(first_half[half:], bottoms[0], bottoms[1])

    def gate_pair(pair):
        columns = columns_of(pair)
        carried = jnp.dot(read_ref[...], carry_ref[pair], preferred_element_type=jnp.float32)
        skip = jnp.dot(
            skip_rows_ref[...], picker(narrow_index, pair), preferred_element_type=jnp.float32
        )
        ssm_out = (
            local_ref[:, columns]
            + spread(lead_ref[...], pair_heads(pair)) * carried
            + skip[0:1, :] * signal_ref[:, columns].astype(jnp.float32)
        )
        gate = gate_ref[:, columns].astype(jnp.float32)
        gated = ssm_out * (gate / (1.0 + jnp.exp(-gate)))
        normed_ref[:, columns] = (gated * gain_ref[pl.ds(pair, 1), :]).astype(jnp.bfloat16)
        return gated * gated

    signal_load.wait()

    @pl.loop(0, pair_count // STATE_PAIRS)
    def _(group):
        for member in range(STATE_PAIRS):
            state_pair(group * STATE_PAIRS + member)

        @pl.when(group == 0)
        def _():
            pl.semaphore_wait(
                barrier, 2 + jnp.where(has_next, 1, 0) + jnp.where(has_previous, 1, 0)
            )

            @pl.when(first_core)
            def _():
                totals_copy.start()

        @pl.when(first_core)
        def _():
            for member in range(STATE_PAIRS):
                core_copy(group * STATE_PAIRS + member).start()

        @pl.when(second_core & first_chip & (group > 0))
        def _():
            for member in range(STATE_PAIRS):
                first_chain_step((group - 1) * STATE_PAIRS + member)

        @pl.when(second_core & (group == EARLY_GROUP))
        def _():
            totals_copy.wait_recv()

        @pl.when(has_previous & has_next & (scan_index == 1) & (group >= EARLY_GROUP))
        def _():
            for member in range(2):
                chain_step((group - EARLY_GROUP) * 2 + member)

    @pl.when(second_core & first_chip)
    def _():
        for member in range(STATE_PAIRS):
            first_chain_step(pair_count - STATE_PAIRS + member)

    early_count = 2 * (pair_count // STATE_PAIRS - EARLY_GROUP)

    @pl.loop(0, pair_count // MIX_PAIRS)
    def _(group):
        chunk = group * MIX_PAIRS + jnp.where(scan_index == 1, early_count, 0)

        @pl.when(has_previous & has_next & (chunk < pair_count))
        def _():
            for member in range(MIX_PAIRS):
                chain_step(chunk + member)

        for member in range(MIX_PAIRS):
            mix_pair(group * MIX_PAIRS + member)

    gate_load.wait()
    last_step = has_previous & (scan_index == span_count - 1)

    def gate_pairs(start, count):
        @pl.when(last_step)
        def _():
            for member in range(count):
                chain_step(start + member)

        @pl.when(gets_entry)
        def _():
            for member in range(count):
                entry_copy(start + member).wait_recv()

        squares = square_ref[...]
        for member in range(count):
            squares = squares + gate_pair(start + member)
        square_ref[...] = squares

    @pl.loop(0, pair_count // GATE_PAIRS - 1)
    def _(group):
        gate_pairs(group * GATE_PAIRS, GATE_PAIRS)

    weight_load.wait()
    own_width = out_ref.shape[1]
    tile_count = own_width // TILE

    def tile_copy(tile):
        return pltpu.make_async_remote_copy(
            src_ref=sent_ref.at[tile],
            dst_ref=landed_ref.at[tile],
            send_sem=tile_send,
            recv_sem=tile_recv.at[tile],
            device_id={"tensor": peer},
            device_id_type=MESH,
        )

    def project(owner, tile, first=0, last=pair_count):
        start = pl.multiple_of(owner * own_width + tile * TILE, LANES)
        rows = slice(first * LANES, last * LANES)
        return jnp.dot(
            normed_ref[:, rows],
            weight_ref[rows, pl.ds(start, TILE)],
            preferred_element_type=jnp.float32,
        )

    early = pair_count - GATE_PAIRS
    own_ref[0] = project(peer, 0, 0, early)
    for pair in range(early, pair_count):
        gate_pairs(pair, 1)
    sent_ref[0] = (own_ref[0] + project(peer, 0, early)).astype(jnp.bfloat16)
    tile_copy(0).start()
    square_sum = jnp.sum(square_ref[...].T, axis=0, keepdims=True)
    square_out_ref[...] = jnp.broadcast_to(square_sum, square_out_ref.shape)
    square_copy = pltpu.make_async_remote_copy(
        src_ref=square_out_ref,
        dst_ref=square_in_ref,
        send_sem=square_send,
        recv_sem=square_recv,
        device_id={"tensor": peer},
        device_id_type=MESH,
    )
    square_copy.start()

    @pl.loop(1, tile_count)
    def _(tile):
        sent_ref[tile] = project(peer, tile).astype(jnp.bfloat16)
        tile_copy(tile).start()

    @pl.loop(0, tile_count)
    def _(tile):
        own_ref[tile] = project(tensor_index, tile)

    @pl.when(first_core)
    def _():
        totals_copy.wait_send()

    @pl.when(first_core | has_previous)
    def _():
        pltpu.make_async_copy(pass_ref, pass_ref, core_send).wait()

    @pl.when(has_next)
    def _():
        pltpu.make_async_copy(pass_ref, pass_ref, onward_send).wait()

    square_copy.wait()
    inner = 2 * heads * HEAD_DIM
    scale = lax.rsqrt((square_out_ref[0:1, :] + square_in_ref[0:1, :]) / inner + EPSILON)
    square_ref[...] = jnp.broadcast_to(scale, (LANES, STRETCH)).T

    @pl.loop(0, tile_count)
    def _(tile):
        tile_copy(tile).wait_recv()
        scales = square_ref[...]
        for side in range(TILE // LANES):
            start = pl.multiple_of(tile * TILE + side * LANES, LANES)
            columns = slice(side * LANES, (side + 1) * LANES)
            both = own_ref[tile, :, columns] + landed_ref[tile, :, columns].astype(jnp.float32)
            out_ref[:, pl.ds(start, LANES)] = (both * scales).astype(jnp.bfloat16)

    pltpu.make_async_copy(sent_ref, sent_ref, tile_send).wait()


def fused_on_device(
    span_count,
    signal,
    gate_branch,
    write_proj,
    read_proj,
    step_logits,
    valid_mask,
    stretch_band,
    band_offset,
    decay_log,
    step_offset,
    skip_gain,
    norm_gain,
    out_weight,
):
    heads = decay_log.shape[0]
    inner = heads * HEAD_DIM
    width = out_weight.shape[1]
    pair_count = heads // 2
    tile_count = width // 2 // TILE
    vmem = pl.BlockSpec(memory_space=pltpu.VMEM)
    hbm = pl.BlockSpec(memory_space=pl.ANY)
    f32, bf16 = jnp.float32, jnp.bfloat16
    return pl.pallas_call(
        functools.partial(fused_kernel, heads, span_count),
        out_shape=pltpu.VMEM((STRETCH, width // 2), bf16),
        in_specs=[hbm] * 13,
        out_specs=vmem,
        scratch_shapes=[
            pltpu.VMEM((inner, width), bf16),
            pltpu.VMEM((STRETCH, inner), bf16),
            pltpu.VMEM((STRETCH, inner), bf16),
            pltpu.VMEM((STRETCH, STATE), bf16),
            pltpu.VMEM((STRETCH, STATE), bf16),
            pltpu.VMEM((heads, STRETCH), f32),
            pltpu.VMEM((1, STRETCH), jnp.int32),
            pltpu.VMEM((1, 1), jnp.int32),
            pltpu.VMEM((BANDS, heads), f32),
            pltpu.VMEM((1, heads), f32),
            pltpu.VMEM((1, heads), f32),
            pltpu.VMEM((1, heads), f32),
            pltpu.VMEM((pair_count, LANES), f32),
            pltpu.VMEM((LANES, STRETCH), f32),
            pltpu.VMEM((8, LANES), f32),
            pltpu.VMEM((LANES, STRETCH), f32),
            pltpu.VMEM((STRETCH, LANES), f32),
            pltpu.VMEM((STRETCH, LANES), f32),
            pltpu.VMEM((STRETCH, LANES), f32),
            pltpu.VMEM((LANES, STRETCH), f32),
            pltpu.VMEM((16, LANES), bf16),
            pltpu.VMEM((STRETCH, STRETCH), f32),
            pltpu.VMEM((STATE, STRETCH), bf16),
            pltpu.VMEM((pair_count, STATE, LANES), f32),
            pltpu.VMEM((-(-pair_count // 16) * 16, LANES), f32),
            pltpu.VMEM((-(-pair_count // 16) * 16, LANES), f32),
            pltpu.VMEM((STRETCH, inner), f32),
            pltpu.VMEM((STRETCH, inner), bf16),
            pltpu.VMEM((STRETCH, LANES), f32),
            pltpu.VMEM((pair_count, STATE, LANES), bf16),
            pltpu.VMEM((pair_count, STATE, LANES), bf16),
            pltpu.VMEM((pair_count, STATE, LANES), bf16),
            pltpu.VMEM((pair_count, STATE, LANES), bf16),
            pltpu.VMEM((tile_count, STRETCH, TILE), bf16),
            pltpu.VMEM((tile_count, STRETCH, TILE), f32),
            pltpu.VMEM((tile_count, STRETCH, TILE), bf16),
            pltpu.VMEM((8, STRETCH), f32),
            pltpu.VMEM((8, STRETCH), f32),
            pltpu.SemaphoreType.DMA((3,)),
            pltpu.SemaphoreType.DMA((10,)),
            pltpu.SemaphoreType.DMA,
            pltpu.SemaphoreType.DMA,
            pltpu.SemaphoreType.DMA,
            pltpu.SemaphoreType.DMA((pair_count,)),
            pltpu.SemaphoreType.DMA,
            pltpu.SemaphoreType.DMA((pair_count,)),
            pltpu.SemaphoreType.DMA,
            pltpu.SemaphoreType.DMA((tile_count,)),
            pltpu.SemaphoreType.DMA,
            pltpu.SemaphoreType.DMA,
        ],
        compiler_params=pltpu.CompilerParams(
            collective_id=0, has_side_effects=True, vmem_limit_bytes=60 * 1024 * 1024
        ),
    )(
        signal,
        gate_branch,
        write_proj,
        read_proj,
        step_logits,
        valid_mask[None, :],
        stretch_band[None, :],
        band_offset,
        decay_log[None, :],
        step_offset[None, :],
        skip_gain[None, :],
        norm_gain.reshape(pair_count, LANES),
        out_weight,
    )


def solution(mesh):
    placed = (
        P(("group", "scan", "band"), "tensor"),
        P(("group", "scan", "band"), "tensor"),
        P(("group", "scan", "band"), None),
        P(("group", "scan", "band"), None),
        P("tensor", ("group", "scan", "band")),
        P(("group", "scan", "band")),
        P(("group", "scan", "band")),
        P(None, "tensor"),
        P("tensor"),
        P("tensor"),
        P("tensor"),
        P("tensor"),
        P("tensor", None),
    )
    shape = dict(mesh.shape)
    places = shape["scan"] * shape["band"]

    def layer(*arrays):
        rows = arrays[0].shape[0] // (shape["group"] * places)
        heads = arrays[8].shape[0] // shape["tensor"]
        width = arrays[12].shape[1]
        fits = (
            shape["tensor"] == 2
            and shape["band"] == 2
            and shape["scan"] >= 2
            and rows == STRETCH
            and heads % (2 * STATE_PAIRS) == 0
            and heads % (2 * MIX_PAIRS) == 0
            and heads % (2 * GATE_PAIRS) == 0
            and heads > 2 * STATE_PAIRS * EARLY_GROUP
            and 3 * heads <= LANES
            and width % (2 * TILE) == 0
        )
        member = on_device
        if fits:
            member = functools.partial(fused_on_device, shape["scan"])
        return mapped(member)(*arrays)

    def mapped(member):
        return jax.shard_map(
            member,
            mesh=mesh,
            in_specs=placed,
            out_specs=P(("group", "scan", "band"), "tensor"),
            check_vma=False,
        )

    return layer
```

```python
import functools

import jax
import jax.numpy as jnp
from jax import lax
from jax.experimental import pallas as pl
from jax.experimental.pallas import tpu as pltpu
from jax.sharding import PartitionSpec as P

HEAD_DIM = 64
STATE = 128
STRETCH = 256
BANDS = 12
INNER = 5120


EPSILON = 1e-05
HIGHEST = lax.Precision.HIGHEST


def step_sizes(step_logits, stretch_band, band_offset, step_offset):
    one_hot = (stretch_band[:, None] == jnp.arange(BANDS, dtype=jnp.int32)[None, :]).astype(
        jnp.float32
    )
    stretch_offset = jnp.dot(one_hot, band_offset, precision=HIGHEST)
    token_offset = jnp.repeat(stretch_offset, STRETCH, axis=0).T
    return jax.nn.softplus(step_logits + step_offset[:, None] + token_offset)


def combine(earlier, later_pair):
    return (
        earlier[0] + later_pair[0],
        jnp.exp(later_pair[0])[:, None, None] * earlier[1] + later_pair[1],
    )


def local_step(running_pair, member):
    return (combine(running_pair, member), running_pair)


def on_device(
    signal,
    gate_branch,
    write_proj,
    read_proj,
    step_logits,
    valid_mask,
    stretch_band,
    band_offset,
    decay_log,
    step_offset,
    skip_gain,
    norm_gain,
    out_weight,
):
    row_count = signal.shape[0]
    head_count = decay_log.shape[0]
    block_count = row_count // STRETCH
    step_size = step_sizes(step_logits, stretch_band, band_offset, step_offset)
    log_decay = step_size * (-jnp.exp(decay_log))[:, None]
    input_weight = step_size * valid_mask.astype(jnp.float32)[None, :]
    running = lax.associative_scan(
        jnp.add, log_decay.reshape(head_count, block_count, STRETCH), axis=2
    )
    weight_blocks = input_weight.reshape(head_count, block_count, STRETCH)
    signal_blocks = signal.reshape(block_count, STRETCH, head_count, HEAD_DIM)
    write_blocks = write_proj.reshape(block_count, STRETCH, STATE)
    read_blocks = read_proj.reshape(block_count, STRETCH, STATE)
    scores = jnp.einsum(
        "cin,cjn->cij", read_blocks, write_blocks, preferred_element_type=jnp.float32
    )
    lower_mask = jnp.arange(STRETCH)[:, None] >= jnp.arange(STRETCH)[None, :]
    span_logs = jnp.where(
        lower_mask[None, None], running[:, :, :, None] - running[:, :, None, :], -1e30
    )
    mixing = (jnp.exp(span_logs) * scores[None] * weight_blocks[:, :, None, :]).astype(jnp.bfloat16)
    local_out = jnp.einsum(
        "hcij,cjhp->cihp", mixing, signal_blocks, preferred_element_type=jnp.float32
    )
    tail_weight = jnp.exp(running[:, :, -1:] - running) * weight_blocks
    scaled = (
        signal_blocks.astype(jnp.float32) * jnp.transpose(tail_weight, (1, 2, 0))[:, :, :, None]
    ).astype(jnp.bfloat16)
    block_states = jnp.einsum(
        "cjhp,cjn->chpn", scaled, write_blocks, preferred_element_type=jnp.float32
    )
    block_decay = running[:, :, -1].T
    zero_state = jnp.zeros((head_count, HEAD_DIM, STATE), jnp.float32)
    zero_log = jnp.zeros((head_count,), jnp.float32)
    identity = (zero_log, zero_state)
    device_pair, segment_cumulative = lax.scan(local_step, identity, (block_decay, block_states))
    all_logs = lax.all_gather(device_pair[0][None], ("scan", "band"), axis=0, tiled=True)
    inclusive = lax.associative_scan(jnp.add, all_logs, axis=0)
    exclusive = inclusive - all_logs
    position = lax.axis_index(("scan", "band"))
    own_exclusive = lax.dynamic_index_in_dim(exclusive, position, 0, keepdims=False)
    shard_block = lax.all_gather(
        device_pair[1][None].astype(jnp.bfloat16), ("scan", "band"), axis=0, tiled=True
    ).astype(jnp.float32)
    how_many = shard_block.shape[0]
    sources = jnp.arange(how_many, dtype=jnp.int32)
    gap_logs = jnp.where((sources < position)[:, None], own_exclusive[None, :] - inclusive, -1e30)
    carry_state = zero_state + jnp.einsum(
        "kh,khpn->hpn", jnp.exp(gap_logs), shard_block, precision=HIGHEST
    )
    enter_state = (
        jnp.exp(segment_cumulative[0])[:, :, None, None] * carry_state[None] + segment_cumulative[1]
    )
    state_high = enter_state.astype(jnp.bfloat16)
    widened = lax.optimization_barrier(state_high).astype(jnp.float32)
    state_low = (enter_state - widened).astype(jnp.bfloat16)
    high_part = jnp.einsum(
        "cin,chpn->cihp", read_blocks, state_high, preferred_element_type=jnp.float32
    )
    low_part = jnp.einsum(
        "cin,chpn->cihp", read_blocks, state_low, preferred_element_type=jnp.float32
    )
    carried_out = jnp.transpose(jnp.exp(running), (1, 2, 0))[:, :, :, None] * (high_part + low_part)
    ssm_out = (local_out + carried_out).reshape(row_count, head_count, HEAD_DIM) + skip_gain[
        None, :, None
    ] * signal.reshape(row_count, head_count, HEAD_DIM).astype(jnp.float32)
    gated_out = ssm_out.reshape(row_count, head_count * HEAD_DIM) * jax.nn.silu(
        gate_branch.astype(jnp.float32)
    )
    square_total = lax.psum(jnp.sum(gated_out * gated_out, axis=1), "tensor")
    normed = (
        gated_out * lax.rsqrt(square_total / INNER + EPSILON)[:, None] * norm_gain[None, :]
    ).astype(jnp.bfloat16)
    own_columns = lax.psum_scatter(
        lax.dot_general(
            out_weight, normed, (((0,), (1,)), ((), ())), preferred_element_type=jnp.float32
        ).astype(jnp.bfloat16),
        "tensor",
        scatter_dimension=0,
        tiled=True,
    ).astype(jnp.float32)
    return own_columns.T.astype(jnp.bfloat16)


LOG2E = 1.4426950408889634
LANES = 128
STATE_PAIRS = 4
HEAD_START = 2
MIX_PAIRS = 2
GATE_PAIRS = 2
TILE = 256
MESH = pl.DeviceIdType.MESH


def fused_kernel(
    heads,
    span_count,
    signal_hbm,
    gate_hbm,
    write_hbm,
    read_hbm,
    logits_hbm,
    valid_hbm,
    band_hbm,
    offset_hbm,
    decay_hbm,
    bias_hbm,
    skip_hbm,
    gain_hbm,
    weight_hbm,
    out_ref,
    weight_ref,
    signal_ref,
    gate_ref,
    write_ref,
    read_ref,
    logits_ref,
    valid_ref,
    band_ref,
    offset_ref,
    decay_ref,
    bias_ref,
    skip_ref,
    gain_ref,
    padded_ref,
    params_ref,
    row_ref,
    run_ref,
    in_weight_ref,
    tail_ref,
    lead_ref,
    row_log_ref,
    skip_rows_ref,
    scores_ref,
    read_by_token_ref,
    state_ref,
    totals_ref,
    core_totals_ref,
    local_ref,
    normed_ref,
    square_ref,
    carry_ref,
    pass_ref,
    core_state_ref,
    entry_ref,
    sent_ref,
    own_ref,
    landed_ref,
    square_out_ref,
    square_in_ref,
    load_sem,
    small_sem,
    totals_send,
    totals_recv,
    core_send,
    core_recv,
    onward_send,
    onward_recv,
    tile_send,
    tile_recv,
    square_send,
    square_recv,
):
    pair_count = heads // 2
    scan_index = lax.axis_index("scan")
    band_index = lax.axis_index("band")
    tensor_index = lax.axis_index("tensor")
    first_core = band_index == 0
    second_core = band_index == 1
    first_chip = scan_index == 0
    has_previous = second_core & (scan_index > 0)
    has_next = second_core & (scan_index < span_count - 1)
    gets_entry = first_core & (scan_index > 0)
    peer = 1 - tensor_index
    other_core = {"band": 1 - band_index}
    following = {"scan": lax.rem(scan_index + 1, span_count)}
    previous = {"scan": lax.rem(scan_index + span_count - 1, span_count)}

    barrier = pltpu.get_barrier_semaphore()
    for target in (other_core, {"tensor": peer}):
        pl.semaphore_signal(barrier, inc=1, device_id=target, device_id_type=MESH)

    @pl.when(has_next)
    def _():
        pl.semaphore_signal(barrier, inc=1, device_id=following, device_id_type=MESH)

    @pl.when(has_previous)
    def _():
        pl.semaphore_signal(barrier, inc=1, device_id=previous, device_id_type=MESH)

    signal_load = pltpu.make_async_copy(signal_hbm, signal_ref, load_sem.at[2])
    gate_load = pltpu.make_async_copy(gate_hbm, gate_ref, load_sem.at[0])
    weight_load = pltpu.make_async_copy(weight_hbm, weight_ref, load_sem.at[1])
    small_loads = [
        pltpu.make_async_copy(source, target, small_sem.at[spot])
        for spot, (source, target) in enumerate(
            (
                (logits_hbm, logits_ref),
                (band_hbm, band_ref),
                (offset_hbm, offset_ref),
                (decay_hbm, decay_ref),
                (bias_hbm, bias_ref),
                (valid_hbm, valid_ref),
                (skip_hbm, skip_ref),
                (write_hbm, write_ref),
                (read_hbm, read_ref),
                (gain_hbm, gain_ref),
            )
        )
    ]
    for load in small_loads:
        load.start()
    signal_load.start()
    gate_load.start()
    weight_load.start()
    for load in small_loads:
        load.wait()

    padded_ref[...] = jnp.zeros_like(padded_ref)
    padded_ref[0:heads, :] = logits_ref[...]
    params_ref[...] = jnp.zeros_like(params_ref)
    chosen = lax.broadcasted_iota(jnp.int32, (BANDS, heads), 0) == band_ref[...]
    params_ref[0:1, 0:heads] = bias_ref[...] + jnp.sum(
        jnp.where(chosen, offset_ref[...], 0.0), axis=0, keepdims=True
    )
    params_ref[1:2, 0:heads] = jnp.exp(decay_ref[...])
    params_ref[2:3, 0:heads] = skip_ref[...]
    shifted = padded_ref[...].T + params_ref[0:1, :]
    step_size = jnp.maximum(shifted, 0.0) + jnp.log1p(jnp.exp(-jnp.abs(shifted)))
    lanes = lax.broadcasted_iota(jnp.int32, (STRETCH, LANES), 1)
    tokens = lax.broadcasted_iota(jnp.int32, (STRETCH, LANES), 0)
    real = lanes < heads
    running = jnp.where(real, step_size * -params_ref[1:2, :], 0.0)
    shift = 1
    while shift < STRETCH:
        running = running + jnp.where(tokens >= shift, pltpu.roll(running, shift, 0), 0.0)
        shift *= 2
    running = running * LOG2E
    run_ref[...] = running
    valid = jnp.broadcast_to(valid_ref[...].astype(jnp.float32), (LANES, STRETCH)).T
    in_weight = jnp.where(real, step_size * valid, 0.0)

    def three_parts(value):
        high = value.astype(jnp.bfloat16).astype(jnp.float32)
        rest = value - high
        middle = rest.astype(jnp.bfloat16).astype(jnp.float32)
        low = rest - middle
        packed = high + pltpu.roll(middle, heads, 1) + pltpu.roll(low, 2 * heads, 1)
        return packed.astype(jnp.bfloat16)

    running_parts = three_parts(running[STRETCH - 16 : STRETCH])
    in_weight_ref[...] = in_weight
    tail_ref[...] = jnp.exp2(running[STRETCH - 1 : STRETCH, :] - running) * in_weight
    part = lax.broadcasted_iota(jnp.int32, (LANES, 2 * LANES), 0)
    part = (
        part
        - jnp.where(part >= heads, heads, 0)
        - jnp.where(part >= 2 * heads, heads, 0)
    )
    head_of = lax.broadcasted_iota(jnp.int32, totals_ref.shape, 1)
    head_of = (
        head_of
        - jnp.where(head_of >= heads, heads, 0)
        - jnp.where(head_of >= 2 * heads, heads, 0)
    )
    own_pair = head_of // 2 == lax.broadcasted_iota(jnp.int32, totals_ref.shape, 0)
    last_parts = running_parts.astype(jnp.float32)[15:16, :]
    last_rows = (
        jnp.dot(
            jnp.where(own_pair, last_parts, 0.0).astype(jnp.bfloat16),
            jnp.where(
                part[:, 0:LANES] % 2
                == lax.broadcasted_iota(jnp.int32, (LANES, LANES), 1) // HEAD_DIM,
                1.0,
                0.0,
            ).astype(jnp.bfloat16),
            preferred_element_type=jnp.float32,
        )
    )
    totals_ref[...] = jnp.exp2(last_rows)
    write_turned = write_ref[...].astype(jnp.float32).T.astype(jnp.bfloat16)
    read_by_token_ref[...] = write_turned

    totals_copy = pltpu.make_async_remote_copy(
        src_ref=totals_ref,
        dst_ref=core_totals_ref,
        send_sem=totals_send,
        recv_sem=totals_recv,
        device_id=other_core,
        device_id_type=MESH,
    )

    def core_copy(pair):
        return pltpu.make_async_remote_copy(
            src_ref=pass_ref.at[pair],
            dst_ref=core_state_ref.at[pair],
            send_sem=core_send,
            recv_sem=core_recv.at[pair],
            device_id=other_core,
            device_id_type=MESH,
        )

    def onward_copy(pair):
        return pltpu.make_async_remote_copy(
            src_ref=pass_ref.at[pair],
            dst_ref=entry_ref.at[pair],
            send_sem=onward_send,
            recv_sem=onward_recv.at[pair],
            device_id=following,
            device_id_type=MESH,
        )

    def entry_copy(pair):
        return pltpu.make_async_remote_copy(
            src_ref=entry_ref.at[pair],
            dst_ref=carry_ref.at[pair],
            send_sem=core_send,
            recv_sem=core_recv.at[pair],
            device_id=other_core,
            device_id_type=MESH,
        )

    def give_onward(pair, carry):
        onward = totals_ref[pl.ds(pair, 1), :] * carry + state_ref[pair]
        pass_ref[pair] = onward.astype(jnp.bfloat16)
        onward_copy(pair).start()

    def first_chain_step(pair):
        core_copy(pair).wait_recv()
        own = core_state_ref[pair]
        carry_ref[pair] = own

        @pl.when(has_next)
        def _():
            give_onward(pair, own.astype(jnp.float32))

    def chain_step(pair):
        core_copy(pair).wait_recv()
        onward_copy(pair).wait_recv()

        @pl.when(jnp.logical_not(has_next))
        def _():
            entry_copy(pair).start()

        carry = core_totals_ref[pl.ds(pair, 1), :] * entry_ref[pair].astype(
            jnp.float32
        ) + core_state_ref[pair].astype(jnp.float32)

        @pl.when(has_next)
        def _():
            give_onward(pair, carry)
            entry_copy(pair).start()

        carry_ref[pair] = carry.astype(jnp.bfloat16)

    def columns_of(pair):
        return pl.ds(pl.multiple_of(pair * LANES, LANES), LANES)

    narrow_side = lax.broadcasted_iota(jnp.int32, (LANES, LANES), 1) // HEAD_DIM
    narrow_index = part[:, 0:LANES] - narrow_side
    first_half = lanes < HEAD_DIM

    def picker(index, pair):
        return jnp.where(index == 2 * pair, 1.0, 0.0).astype(jnp.bfloat16)

    def spread(values, index):
        return jnp.take_along_axis(values, index, axis=1, mode="promise_in_bounds")

    def pair_heads(pair):
        return 2 * pair + lanes // HEAD_DIM

    def state_pair(pair):
        columns = columns_of(pair)
        tail = spread(tail_ref[...], pair_heads(pair))
        scaled = (signal_ref[:, columns].astype(jnp.float32) * tail).astype(jnp.bfloat16)
        state = jnp.dot(read_by_token_ref[...], scaled, preferred_element_type=jnp.float32)
        state_ref[pair] = state
        pass_ref[pair] = state.astype(jnp.bfloat16)


    def mix_pair(pair):
        columns = columns_of(pair)
        half = STRETCH // 2
        tops, bottoms = [], []
        fed = signal_ref[:, columns]
        for side in range(2):
            row = row_ref[pl.ds(2 * pair + side, 1), :]
            most = row_log_ref[pl.ds(2 * pair + side, 1), :]
            run = spread(run_ref[...], jnp.full((STRETCH, LANES), 2 * pair + side, jnp.int32))
            near = jnp.exp2(jnp.minimum(run[0:half] - row[:, 0:half], most[:, 0:half]))
            far = jnp.exp2(run[half:] - row[:, 0:half])
            late = jnp.exp2(jnp.minimum(run[half:] - row[:, half:], most[:, half:]))
            near = (near * scores_ref[0:half, 0:half]).astype(jnp.bfloat16)
            far = (far * scores_ref[half:, 0:half]).astype(jnp.bfloat16)
            late = (late * scores_ref[half:, half:]).astype(jnp.bfloat16)
            tops.append(jnp.dot(near, fed[0:half], preferred_element_type=jnp.float32))
            bottoms.append(
                jnp.dot(
                    jnp.concatenate([far, late], axis=1), fed, preferred_element_type=jnp.float32
                )
            )
        local_ref[0:half, columns] = jnp.where(first_half[0:half], tops[0], tops[1])
        local_ref[half:, columns] = jnp.where(first_half[half:], bottoms[0], bottoms[1])

    def gate_pair(pair):
        columns = columns_of(pair)
        carried = jnp.dot(read_ref[...], carry_ref[pair], preferred_element_type=jnp.float32)
        skip = jnp.dot(
            skip_rows_ref[...], picker(narrow_index, pair), preferred_element_type=jnp.float32
        )
        ssm_out = (
            local_ref[:, columns]
            + spread(lead_ref[...], pair_heads(pair)) * carried
            + skip[0:1, :] * signal_ref[:, columns].astype(jnp.float32)
        )
        gate = gate_ref[:, columns].astype(jnp.float32)
        gated = ssm_out * (gate / (1.0 + jnp.exp(-gate)))
        normed_ref[:, columns] = (gated * gain_ref[pl.ds(pair, 1), :]).astype(jnp.bfloat16)
        return gated * gated

    def state_pairs(start, count):
        for member in range(count):
            state_pair(start + member)

    def core_copies(start, count):
        @pl.when(first_core)
        def _():
            for member in range(count):
                core_copy(start + member).start()

    def first_chain_steps(start, count):
        @pl.when(second_core & first_chip)
        def _():
            for member in range(count):
                first_chain_step(start + member)

    signal_load.wait()
    state_pairs(0, HEAD_START)
    pl.semaphore_wait(barrier, 2 + jnp.where(has_next, 1, 0) + jnp.where(has_previous, 1, 0))
    core_copies(0, HEAD_START)

    @pl.when(first_core)
    def _():
        totals_copy.start()

    state_pairs(HEAD_START, STATE_PAIRS - HEAD_START)
    core_copies(HEAD_START, STATE_PAIRS - HEAD_START)
    first_chain_steps(0, HEAD_START)

    @pl.loop(1, pair_count // STATE_PAIRS)
    def _(group):
        start = group * STATE_PAIRS
        state_pairs(start, STATE_PAIRS)
        core_copies(start, STATE_PAIRS)
        first_chain_steps(start - STATE_PAIRS + HEAD_START, STATE_PAIRS)

    first_chain_steps(pair_count - STATE_PAIRS + HEAD_START, STATE_PAIRS - HEAD_START)

    @pl.when(second_core)
    def _():
        totals_copy.wait_recv()

    skip_rows_ref[...] = three_parts(jnp.broadcast_to(params_ref[2:3, :], (16, LANES)))
    lead_ref[...] = jnp.exp2(run_ref[...])
    weight_rows = in_weight_ref[...].T
    weight_log = jnp.where(weight_rows > 0.0, jnp.log(weight_rows) * LOG2E, -1e30)
    row_log_ref[...] = weight_log
    row_ref[...] = run_ref[...].T - weight_log
    scores = jnp.dot(read_ref[...], read_by_token_ref[...], preferred_element_type=jnp.float32)
    square_rows = lax.broadcasted_iota(jnp.int32, (STRETCH, STRETCH), 0)
    square_columns = lax.broadcasted_iota(jnp.int32, (STRETCH, STRETCH), 1)
    scores_ref[...] = jnp.where(square_columns <= square_rows, scores, 0.0)
    square_ref[...] = jnp.zeros_like(square_ref)
    @pl.when(first_core & first_chip)
    def _():
        carry_ref[...] = jnp.zeros_like(carry_ref)

    @pl.loop(0, pair_count // MIX_PAIRS)
    def _(group):
        @pl.when(has_previous & has_next)
        def _():
            for member in range(MIX_PAIRS):
                chain_step(group * MIX_PAIRS + member)

        for member in range(MIX_PAIRS):
            mix_pair(group * MIX_PAIRS + member)

    gate_load.wait()
    last_step = has_previous & (scan_index == span_count - 1)

    def gate_pairs(start, count):
        @pl.when(last_step)
        def _():
            for member in range(count):
                chain_step(start + member)

        @pl.when(gets_entry)
        def _():
            for member in range(count):
                entry_copy(start + member).wait_recv()

        squares = square_ref[...]
        for member in range(count):
            squares = squares + gate_pair(start + member)
        square_ref[...] = squares

    @pl.loop(0, pair_count // GATE_PAIRS - 1)
    def _(group):
        gate_pairs(group * GATE_PAIRS, GATE_PAIRS)

    weight_load.wait()
    own_width = out_ref.shape[1]
    tile_count = own_width // TILE

    def tile_copy(tile):
        return pltpu.make_async_remote_copy(
            src_ref=sent_ref.at[tile],
            dst_ref=landed_ref.at[tile],
            send_sem=tile_send,
            recv_sem=tile_recv.at[tile],
            device_id={"tensor": peer},
            device_id_type=MESH,
        )

    def project(owner, tile, first=0, last=pair_count):
        start = pl.multiple_of(owner * own_width + tile * TILE, LANES)
        rows = slice(first * LANES, last * LANES)
        return jnp.dot(
            normed_ref[:, rows],
            weight_ref[rows, pl.ds(start, TILE)],
            preferred_element_type=jnp.float32,
        )

    early = pair_count - GATE_PAIRS
    own_ref[0] = project(peer, 0, 0, early)
    for pair in range(early, pair_count):
        gate_pairs(pair, 1)
    sent_ref[0] = (own_ref[0] + project(peer, 0, early)).astype(jnp.bfloat16)
    tile_copy(0).start()
    square_sum = jnp.sum(square_ref[...].T, axis=0, keepdims=True)
    square_out_ref[...] = jnp.broadcast_to(square_sum, square_out_ref.shape)
    square_copy = pltpu.make_async_remote_copy(
        src_ref=square_out_ref,
        dst_ref=square_in_ref,
        send_sem=square_send,
        recv_sem=square_recv,
        device_id={"tensor": peer},
        device_id_type=MESH,
    )
    square_copy.start()

    @pl.loop(1, tile_count)
    def _(tile):
        sent_ref[tile] = project(peer, tile).astype(jnp.bfloat16)
        tile_copy(tile).start()

    @pl.loop(0, tile_count)
    def _(tile):
        own_ref[tile] = project(tensor_index, tile)

    @pl.when(first_core)
    def _():
        totals_copy.wait_send()

    @pl.when(first_core | has_previous)
    def _():
        pltpu.make_async_copy(pass_ref, pass_ref, core_send).wait()

    @pl.when(has_next)
    def _():
        pltpu.make_async_copy(pass_ref, pass_ref, onward_send).wait()

    square_copy.wait()
    inner = 2 * heads * HEAD_DIM
    scale = lax.rsqrt((square_out_ref[0:1, :] + square_in_ref[0:1, :]) / inner + EPSILON)
    square_ref[...] = jnp.broadcast_to(scale, (LANES, STRETCH)).T

    @pl.loop(0, tile_count)
    def _(tile):
        tile_copy(tile).wait_recv()
        scales = square_ref[...]
        for side in range(TILE // LANES):
            start = pl.multiple_of(tile * TILE + side * LANES, LANES)
            columns = slice(side * LANES, (side + 1) * LANES)
            both = own_ref[tile, :, columns] + landed_ref[tile, :, columns].astype(jnp.float32)
            out_ref[:, pl.ds(start, LANES)] = (both * scales).astype(jnp.bfloat16)

    pltpu.make_async_copy(sent_ref, sent_ref, tile_send).wait()


def fused_on_device(
    span_count,
    signal,
    gate_branch,
    write_proj,
    read_proj,
    step_logits,
    valid_mask,
    stretch_band,
    band_offset,
    decay_log,
    step_offset,
    skip_gain,
    norm_gain,
    out_weight,
):
    heads = decay_log.shape[0]
    inner = heads * HEAD_DIM
    width = out_weight.shape[1]
    pair_count = heads // 2
    tile_count = width // 2 // TILE
    vmem = pl.BlockSpec(memory_space=pltpu.VMEM)
    hbm = pl.BlockSpec(memory_space=pl.ANY)
    f32, bf16 = jnp.float32, jnp.bfloat16
    return pl.pallas_call(
        functools.partial(fused_kernel, heads, span_count),
        out_shape=pltpu.VMEM((STRETCH, width // 2), bf16),
        in_specs=[hbm] * 13,
        out_specs=vmem,
        scratch_shapes=[
            pltpu.VMEM((inner, width), bf16),
            pltpu.VMEM((STRETCH, inner), bf16),
            pltpu.VMEM((STRETCH, inner), bf16),
            pltpu.VMEM((STRETCH, STATE), bf16),
            pltpu.VMEM((STRETCH, STATE), bf16),
            pltpu.VMEM((heads, STRETCH), f32),
            pltpu.VMEM((1, STRETCH), jnp.int32),
            pltpu.VMEM((1, 1), jnp.int32),
            pltpu.VMEM((BANDS, heads), f32),
            pltpu.VMEM((1, heads), f32),
            pltpu.VMEM((1, heads), f32),
            pltpu.VMEM((1, heads), f32),
            pltpu.VMEM((pair_count, LANES), f32),
            pltpu.VMEM((LANES, STRETCH), f32),
            pltpu.VMEM((8, LANES), f32),
            pltpu.VMEM((LANES, STRETCH), f32),
            pltpu.VMEM((STRETCH, LANES), f32),
            pltpu.VMEM((STRETCH, LANES), f32),
            pltpu.VMEM((STRETCH, LANES), f32),
            pltpu.VMEM((STRETCH, LANES), f32),
            pltpu.VMEM((LANES, STRETCH), f32),
            pltpu.VMEM((16, LANES), bf16),
            pltpu.VMEM((STRETCH, STRETCH), f32),
            pltpu.VMEM((STATE, STRETCH), bf16),
            pltpu.VMEM((pair_count, STATE, LANES), f32),
            pltpu.VMEM((-(-pair_count // 16) * 16, LANES), f32),
            pltpu.VMEM((-(-pair_count // 16) * 16, LANES), f32),
            pltpu.VMEM((STRETCH, inner), f32),
            pltpu.VMEM((STRETCH, inner), bf16),
            pltpu.VMEM((STRETCH, LANES), f32),
            pltpu.VMEM((pair_count, STATE, LANES), bf16),
            pltpu.VMEM((pair_count, STATE, LANES), bf16),
            pltpu.VMEM((pair_count, STATE, LANES), bf16),
            pltpu.VMEM((pair_count, STATE, LANES), bf16),
            pltpu.VMEM((tile_count, STRETCH, TILE), bf16),
            pltpu.VMEM((tile_count, STRETCH, TILE), f32),
            pltpu.VMEM((tile_count, STRETCH, TILE), bf16),
            pltpu.VMEM((8, STRETCH), f32),
            pltpu.VMEM((8, STRETCH), f32),
            pltpu.SemaphoreType.DMA((3,)),
            pltpu.SemaphoreType.DMA((10,)),
            pltpu.SemaphoreType.DMA,
            pltpu.SemaphoreType.DMA,
            pltpu.SemaphoreType.DMA,
            pltpu.SemaphoreType.DMA((pair_count,)),
            pltpu.SemaphoreType.DMA,
            pltpu.SemaphoreType.DMA((pair_count,)),
            pltpu.SemaphoreType.DMA,
            pltpu.SemaphoreType.DMA((tile_count,)),
            pltpu.SemaphoreType.DMA,
            pltpu.SemaphoreType.DMA,
        ],
        compiler_params=pltpu.CompilerParams(
            collective_id=0, has_side_effects=True, vmem_limit_bytes=60 * 1024 * 1024
        ),
    )(
        signal,
        gate_branch,
        write_proj,
        read_proj,
        step_logits,
        valid_mask[None, :],
        stretch_band[None, :],
        band_offset,
        decay_log[None, :],
        step_offset[None, :],
        skip_gain[None, :],
        norm_gain.reshape(pair_count, LANES),
        out_weight,
    )


def solution(mesh):
    placed = (
        P(("group", "scan", "band"), "tensor"),
        P(("group", "scan", "band"), "tensor"),
        P(("group", "scan", "band"), None),
        P(("group", "scan", "band"), None),
        P("tensor", ("group", "scan", "band")),
        P(("group", "scan", "band")),
        P(("group", "scan", "band")),
        P(None, "tensor"),
        P("tensor"),
        P("tensor"),
        P("tensor"),
        P("tensor"),
        P("tensor", None),
    )
    shape = dict(mesh.shape)
    places = shape["scan"] * shape["band"]

    def layer(*arrays):
        rows = arrays[0].shape[0] // (shape["group"] * places)
        heads = arrays[8].shape[0] // shape["tensor"]
        width = arrays[12].shape[1]
        fits = (
            shape["tensor"] == 2
            and shape["band"] == 2
            and shape["scan"] >= 2
            and rows == STRETCH
            and heads % (2 * STATE_PAIRS) == 0
            and heads % (2 * MIX_PAIRS) == 0
            and heads % (2 * GATE_PAIRS) == 0
            and 3 * heads <= LANES
            and width % (2 * TILE) == 0
        )
        member = on_device
        if fits:
            member = functools.partial(fused_on_device, shape["scan"])
        return mapped(member)(*arrays)

    def mapped(member):
        return jax.shard_map(
            member,
            mesh=mesh,
            in_specs=placed,
            out_specs=P(("group", "scan", "band"), "tensor"),
            check_vma=False,
        )

    return layer
```

```python
import functools

import jax
import jax.numpy as jnp
from jax import lax
from jax.experimental import pallas as pl
from jax.experimental.pallas import tpu as pltpu
from jax.sharding import PartitionSpec as P

HEAD_DIM = 64
STATE = 128
STRETCH = 256
BANDS = 12
INNER = 5120


EPSILON = 1e-05
HIGHEST = lax.Precision.HIGHEST


def step_sizes(step_logits, stretch_band, band_offset, step_offset):
    one_hot = (stretch_band[:, None] == jnp.arange(BANDS, dtype=jnp.int32)[None, :]).astype(
        jnp.float32
    )
    stretch_offset = jnp.dot(one_hot, band_offset, precision=HIGHEST)
    token_offset = jnp.repeat(stretch_offset, STRETCH, axis=0).T
    return jax.nn.softplus(step_logits + step_offset[:, None] + token_offset)


def combine(earlier, later_pair):
    return (
        earlier[0] + later_pair[0],
        jnp.exp(later_pair[0])[:, None, None] * earlier[1] + later_pair[1],
    )


def local_step(running_pair, member):
    return (combine(running_pair, member), running_pair)


def on_device(
    signal,
    gate_branch,
    write_proj,
    read_proj,
    step_logits,
    valid_mask,
    stretch_band,
    band_offset,
    decay_log,
    step_offset,
    skip_gain,
    norm_gain,
    out_weight,
):
    row_count = signal.shape[0]
    head_count = decay_log.shape[0]
    block_count = row_count // STRETCH
    step_size = step_sizes(step_logits, stretch_band, band_offset, step_offset)
    log_decay = step_size * (-jnp.exp(decay_log))[:, None]
    input_weight = step_size * valid_mask.astype(jnp.float32)[None, :]
    running = lax.associative_scan(
        jnp.add, log_decay.reshape(head_count, block_count, STRETCH), axis=2
    )
    weight_blocks = input_weight.reshape(head_count, block_count, STRETCH)
    signal_blocks = signal.reshape(block_count, STRETCH, head_count, HEAD_DIM)
    write_blocks = write_proj.reshape(block_count, STRETCH, STATE)
    read_blocks = read_proj.reshape(block_count, STRETCH, STATE)
    scores = jnp.einsum(
        "cin,cjn->cij", read_blocks, write_blocks, preferred_element_type=jnp.float32
    )
    lower_mask = jnp.arange(STRETCH)[:, None] >= jnp.arange(STRETCH)[None, :]
    span_logs = jnp.where(
        lower_mask[None, None], running[:, :, :, None] - running[:, :, None, :], -1e30
    )
    mixing = (jnp.exp(span_logs) * scores[None] * weight_blocks[:, :, None, :]).astype(jnp.bfloat16)
    local_out = jnp.einsum(
        "hcij,cjhp->cihp", mixing, signal_blocks, preferred_element_type=jnp.float32
    )
    tail_weight = jnp.exp(running[:, :, -1:] - running) * weight_blocks
    scaled = (
        signal_blocks.astype(jnp.float32) * jnp.transpose(tail_weight, (1, 2, 0))[:, :, :, None]
    ).astype(jnp.bfloat16)
    block_states = jnp.einsum(
        "cjhp,cjn->chpn", scaled, write_blocks, preferred_element_type=jnp.float32
    )
    block_decay = running[:, :, -1].T
    zero_state = jnp.zeros((head_count, HEAD_DIM, STATE), jnp.float32)
    zero_log = jnp.zeros((head_count,), jnp.float32)
    identity = (zero_log, zero_state)
    device_pair, segment_cumulative = lax.scan(local_step, identity, (block_decay, block_states))
    all_logs = lax.all_gather(device_pair[0][None], ("scan", "band"), axis=0, tiled=True)
    inclusive = lax.associative_scan(jnp.add, all_logs, axis=0)
    exclusive = inclusive - all_logs
    position = lax.axis_index(("scan", "band"))
    own_exclusive = lax.dynamic_index_in_dim(exclusive, position, 0, keepdims=False)
    shard_block = lax.all_gather(
        device_pair[1][None].astype(jnp.bfloat16), ("scan", "band"), axis=0, tiled=True
    ).astype(jnp.float32)
    how_many = shard_block.shape[0]
    sources = jnp.arange(how_many, dtype=jnp.int32)
    gap_logs = jnp.where((sources < position)[:, None], own_exclusive[None, :] - inclusive, -1e30)
    carry_state = zero_state + jnp.einsum(
        "kh,khpn->hpn", jnp.exp(gap_logs), shard_block, precision=HIGHEST
    )
    enter_state = (
        jnp.exp(segment_cumulative[0])[:, :, None, None] * carry_state[None] + segment_cumulative[1]
    )
    state_high = enter_state.astype(jnp.bfloat16)
    widened = lax.optimization_barrier(state_high).astype(jnp.float32)
    state_low = (enter_state - widened).astype(jnp.bfloat16)
    high_part = jnp.einsum(
        "cin,chpn->cihp", read_blocks, state_high, preferred_element_type=jnp.float32
    )
    low_part = jnp.einsum(
        "cin,chpn->cihp", read_blocks, state_low, preferred_element_type=jnp.float32
    )
    carried_out = jnp.transpose(jnp.exp(running), (1, 2, 0))[:, :, :, None] * (high_part + low_part)
    ssm_out = (local_out + carried_out).reshape(row_count, head_count, HEAD_DIM) + skip_gain[
        None, :, None
    ] * signal.reshape(row_count, head_count, HEAD_DIM).astype(jnp.float32)
    gated_out = ssm_out.reshape(row_count, head_count * HEAD_DIM) * jax.nn.silu(
        gate_branch.astype(jnp.float32)
    )
    square_total = lax.psum(jnp.sum(gated_out * gated_out, axis=1), "tensor")
    normed = (
        gated_out * lax.rsqrt(square_total / INNER + EPSILON)[:, None] * norm_gain[None, :]
    ).astype(jnp.bfloat16)
    own_columns = lax.psum_scatter(
        lax.dot_general(
            out_weight, normed, (((0,), (1,)), ((), ())), preferred_element_type=jnp.float32
        ).astype(jnp.bfloat16),
        "tensor",
        scatter_dimension=0,
        tiled=True,
    ).astype(jnp.float32)
    return own_columns.T.astype(jnp.bfloat16)


LOG2E = 1.4426950408889634
LANES = 128
STATE_PAIRS = 4
HEAD_START = 2
PIECES = 1
PIECE = STATE // PIECES
MIX_PAIRS = 2
GATE_PAIRS = 2
TILE = 256
MESH = pl.DeviceIdType.MESH


def fused_kernel(
    heads,
    span_count,
    signal_hbm,
    gate_hbm,
    write_hbm,
    read_hbm,
    logits_hbm,
    valid_hbm,
    band_hbm,
    offset_hbm,
    decay_hbm,
    bias_hbm,
    skip_hbm,
    gain_hbm,
    weight_hbm,
    out_ref,
    weight_ref,
    signal_ref,
    gate_ref,
    write_ref,
    read_ref,
    logits_ref,
    valid_ref,
    band_ref,
    offset_ref,
    decay_ref,
    bias_ref,
    skip_ref,
    gain_ref,
    padded_ref,
    params_ref,
    row_ref,
    run_ref,
    lead_ref,
    row_log_ref,
    skip_rows_ref,
    scores_ref,
    read_by_token_ref,
    state_ref,
    totals_ref,
    core_totals_ref,
    local_ref,
    normed_ref,
    square_ref,
    carry_ref,
    pass_ref,
    core_state_ref,
    entry_ref,
    sent_ref,
    own_ref,
    landed_ref,
    square_out_ref,
    square_in_ref,
    load_sem,
    small_sem,
    totals_send,
    totals_recv,
    core_send,
    core_recv,
    onward_send,
    arrival,
    tile_send,
    tile_recv,
    square_send,
    square_recv,
):
    pair_count = heads // 2
    scan_index = lax.axis_index("scan")
    band_index = lax.axis_index("band")
    tensor_index = lax.axis_index("tensor")
    first_core = band_index == 0
    second_core = band_index == 1
    first_chip = scan_index == 0
    has_previous = second_core & (scan_index > 0)
    has_next = second_core & (scan_index < span_count - 1)
    gets_entry = first_core & (scan_index > 0)
    peer = 1 - tensor_index
    other_core = {"band": 1 - band_index}
    following = {"scan": lax.rem(scan_index + 1, span_count)}
    previous = {"scan": lax.rem(scan_index + span_count - 1, span_count)}

    signal_load = pltpu.make_async_copy(signal_hbm, signal_ref, load_sem.at[2])
    gate_load = pltpu.make_async_copy(gate_hbm, gate_ref, load_sem.at[0])
    weight_load = pltpu.make_async_copy(weight_hbm, weight_ref, load_sem.at[1])
    small_loads = [
        pltpu.make_async_copy(source, target, small_sem.at[spot])
        for spot, (source, target) in enumerate(
            (
                (logits_hbm, logits_ref),
                (band_hbm, band_ref),
                (offset_hbm, offset_ref),
                (decay_hbm, decay_ref),
                (bias_hbm, bias_ref),
                (valid_hbm, valid_ref),
                (skip_hbm, skip_ref),
                (write_hbm, write_ref),
                (read_hbm, read_ref),
                (gain_hbm, gain_ref),
            )
        )
    ]
    for load in small_loads:
        load.start()
    signal_load.start()

    barrier = pltpu.get_barrier_semaphore()
    for target in (other_core, {"tensor": peer}):
        pl.semaphore_signal(barrier, inc=1, device_id=target, device_id_type=MESH)

    @pl.when(has_next)
    def _():
        pl.semaphore_signal(barrier, inc=1, device_id=following, device_id_type=MESH)

    @pl.when(has_previous)
    def _():
        pl.semaphore_signal(barrier, inc=1, device_id=previous, device_id_type=MESH)

    gate_load.start()
    weight_load.start()
    for load in small_loads:
        load.wait()

    params_ref[...] = jnp.zeros_like(params_ref)
    chosen = lax.broadcasted_iota(jnp.int32, (BANDS, heads), 0) == band_ref[...]
    params_ref[0:1, 0:heads] = bias_ref[...] + jnp.sum(
        jnp.where(chosen, offset_ref[...], 0.0), axis=0, keepdims=True
    )
    params_ref[1:2, 0:heads] = jnp.exp(decay_ref[...]) * -LOG2E
    params_ref[2:3, 0:heads] = skip_ref[...]
    head_columns = params_ref[...].T[0:heads]
    shifted = logits_ref[...] + head_columns[:, 0:1]
    step_size = jnp.maximum(shifted, 0.0) + jnp.log1p(jnp.exp(-jnp.abs(shifted)))
    lanes = lax.broadcasted_iota(jnp.int32, (STRETCH, LANES), 1)
    square_rows = lax.broadcasted_iota(jnp.int32, (STRETCH, STRETCH), 0)
    square_columns = lax.broadcasted_iota(jnp.int32, (STRETCH, STRETCH), 1)
    high = step_size.astype(jnp.bfloat16).astype(jnp.float32)
    middle = (step_size - high).astype(jnp.bfloat16).astype(jnp.float32)
    low = step_size - high - middle
    sums = jnp.dot(
        jnp.concatenate([high, middle, low], axis=0).astype(jnp.bfloat16),
        jnp.where(square_rows <= square_columns, 1.0, 0.0).astype(jnp.bfloat16),
        preferred_element_type=jnp.float32,
    )
    summed = sums[0:heads] + sums[heads : 2 * heads] + sums[2 * heads : 3 * heads]
    running = summed * head_columns[:, 1:2]
    in_weight = step_size * valid_ref[...].astype(jnp.float32)
    tail = jnp.exp2(running[:, STRETCH - 1 : STRETCH] - running) * in_weight
    row_ref[...] = running
    row_log_ref[...] = in_weight
    padded_ref[...] = jnp.zeros_like(padded_ref)
    padded_ref[0:heads, :] = tail
    padded_ref[HEAD_DIM : HEAD_DIM + heads, :] = running
    factors = padded_ref[...].T
    run_ref[...] = factors

    def three_parts(value):
        high = value.astype(jnp.bfloat16).astype(jnp.float32)
        rest = value - high
        middle = rest.astype(jnp.bfloat16).astype(jnp.float32)
        low = rest - middle
        packed = high + pltpu.roll(middle, heads, 1) + pltpu.roll(low, 2 * heads, 1)
        return packed.astype(jnp.bfloat16)

    last_running = pltpu.roll(factors[STRETCH - 16 : STRETCH], LANES - HEAD_DIM, 1)
    running_parts = three_parts(jnp.where(lanes[0:16] < heads, last_running, 0.0))
    part = lax.broadcasted_iota(jnp.int32, (LANES, 2 * LANES), 0)
    part = (
        part
        - jnp.where(part >= heads, heads, 0)
        - jnp.where(part >= 2 * heads, heads, 0)
    )
    head_of = lax.broadcasted_iota(jnp.int32, totals_ref.shape, 1)
    head_of = (
        head_of
        - jnp.where(head_of >= heads, heads, 0)
        - jnp.where(head_of >= 2 * heads, heads, 0)
    )
    own_pair = head_of // 2 == lax.broadcasted_iota(jnp.int32, totals_ref.shape, 0)
    last_parts = running_parts.astype(jnp.float32)[15:16, :]
    last_rows = (
        jnp.dot(
            jnp.where(own_pair, last_parts, 0.0).astype(jnp.bfloat16),
            jnp.where(
                part[:, 0:LANES] % 2
                == lax.broadcasted_iota(jnp.int32, (LANES, LANES), 1) // HEAD_DIM,
                1.0,
                0.0,
            ).astype(jnp.bfloat16),
            preferred_element_type=jnp.float32,
        )
    )
    totals_ref[...] = jnp.exp2(last_rows)
    write_turned = write_ref[...].astype(jnp.float32).T.astype(jnp.bfloat16)
    read_by_token_ref[...] = write_turned

    totals_copy = pltpu.make_async_remote_copy(
        src_ref=totals_ref,
        dst_ref=core_totals_ref,
        send_sem=totals_send,
        recv_sem=totals_recv,
        device_id=other_core,
        device_id_type=MESH,
    )

    def core_copy(start, count, group):
        members = pl.ds(start, count)
        return pltpu.make_async_remote_copy(
            src_ref=pass_ref.at[members],
            dst_ref=core_state_ref.at[members],
            send_sem=core_send,
            recv_sem=core_recv.at[group],
            device_id=other_core,
            device_id_type=MESH,
        )

    def onward_copy(pair, piece):
        rows = pl.ds(piece * PIECE, PIECE)
        return pltpu.make_async_remote_copy(
            src_ref=pass_ref.at[pair, rows],
            dst_ref=entry_ref.at[pair, rows],
            send_sem=onward_send,
            recv_sem=arrival.at[pair * PIECES + piece],
            device_id=following,
            device_id_type=MESH,
        )

    def entry_copy(pair):
        return pltpu.make_async_remote_copy(
            src_ref=entry_ref.at[pair],
            dst_ref=carry_ref.at[pair],
            send_sem=core_send,
            recv_sem=arrival.at[pair * PIECES],
            device_id=other_core,
            device_id_type=MESH,
        )

    def give_onward(pair, piece, carry):
        rows = slice(piece * PIECE, (piece + 1) * PIECE)
        onward = totals_ref[pl.ds(pair, 1), :] * carry + state_ref[pair, rows]
        pass_ref[pair, rows] = onward.astype(jnp.bfloat16)
        onward_copy(pair, piece).start()

    def first_chain_step(pair):
        own = core_state_ref[pair]
        carry_ref[pair] = own

        @pl.when(has_next)
        def _():
            for piece in range(PIECES):
                rows = slice(piece * PIECE, (piece + 1) * PIECE)
                give_onward(pair, piece, own[rows].astype(jnp.float32))

    def chain_step(pair):
        for piece in range(PIECES):
            rows = slice(piece * PIECE, (piece + 1) * PIECE)
            onward_copy(pair, piece).wait_recv()
            if piece == PIECES - 1:

                @pl.when(jnp.logical_not(has_next))
                def _():
                    entry_copy(pair).start()

            carry = core_totals_ref[pl.ds(pair, 1), :] * entry_ref[pair, rows].astype(
                jnp.float32
            ) + core_state_ref[pair, rows].astype(jnp.float32)
            carry_ref[pair, rows] = carry.astype(jnp.bfloat16)

            @pl.when(has_next)
            def _():
                give_onward(pair, piece, carry)
                if piece == PIECES - 1:
                    entry_copy(pair).start()

    def columns_of(pair):
        return pl.ds(pl.multiple_of(pair * LANES, LANES), LANES)

    narrow_side = lax.broadcasted_iota(jnp.int32, (LANES, LANES), 1) // HEAD_DIM
    narrow_index = part[:, 0:LANES] - narrow_side
    first_half = lanes < HEAD_DIM
    second_half = lanes >= HEAD_DIM

    def picker(index, pair):
        return jnp.where(index == 2 * pair, 1.0, 0.0).astype(jnp.bfloat16)

    def spread(values, index):
        return jnp.take_along_axis(values, index, axis=1, mode="promise_in_bounds")

    def pair_heads(pair):
        return 2 * pair + lanes // HEAD_DIM

    def state_pair(pair):
        columns = columns_of(pair)
        tail = spread(run_ref[...], pair_heads(pair))
        scaled = (signal_ref[:, columns].astype(jnp.float32) * tail).astype(jnp.bfloat16)
        state = jnp.dot(read_by_token_ref[...], scaled, preferred_element_type=jnp.float32)
        state_ref[pair] = state
        pass_ref[pair] = state.astype(jnp.bfloat16)


    def mix_pair(pair):
        columns = columns_of(pair)
        half = STRETCH // 2
        fed = signal_ref[:, columns]
        tops, bottoms, sides = [], [], []
        for side in range(2):
            row = row_ref[pl.ds(2 * pair + side, 1), :]
            most = row_log_ref[pl.ds(2 * pair + side, 1), :]
            run = spread(run_ref[...], jnp.full((STRETCH, LANES), HEAD_DIM + 2 * pair + side, jnp.int32))
            near = jnp.exp2(jnp.minimum(run[0:half] - row[:, 0:half], most[:, 0:half]))
            far = jnp.exp2(run[half:] - row[:, 0:half])
            late = jnp.exp2(jnp.minimum(run[half:] - row[:, half:], most[:, half:]))
            tops.append((near * scores_ref[0:half, 0:half]).astype(jnp.bfloat16))
            bottoms.append((far * scores_ref[half:, 0:half]).astype(jnp.bfloat16))
            bottoms.append((late * scores_ref[half:, half:]).astype(jnp.bfloat16))
            sides.append(jnp.where(first_half if side == 0 else second_half, fed, jnp.zeros_like(fed)))
        local_ref[0:half, columns] = jnp.dot(
            jnp.concatenate(tops, axis=1),
            jnp.concatenate([sides[0][0:half], sides[1][0:half]], axis=0),
            preferred_element_type=jnp.float32,
        )
        local_ref[half:, columns] = jnp.dot(
            jnp.concatenate(bottoms, axis=1),
            jnp.concatenate(sides, axis=0),
            preferred_element_type=jnp.float32,
        )

    def gate_pair(pair):
        columns = columns_of(pair)
        carried = jnp.dot(read_ref[...], carry_ref[pair], preferred_element_type=jnp.float32)
        skip = jnp.dot(
            skip_rows_ref[...], picker(narrow_index, pair), preferred_element_type=jnp.float32
        )
        ssm_out = (
            local_ref[:, columns]
            + spread(lead_ref[...], HEAD_DIM + pair_heads(pair)) * carried
            + skip[0:1, :] * signal_ref[:, columns].astype(jnp.float32)
        )
        gate = gate_ref[:, columns].astype(jnp.float32)
        gated = ssm_out * (gate / (1.0 + jnp.exp(-gate)))
        normed_ref[:, columns] = (gated * gain_ref[pl.ds(pair, 1), :]).astype(jnp.bfloat16)
        return gated * gated

    def state_pairs(start, count):
        for member in range(count):
            state_pair(start + member)

    def core_copies(start, count, group):
        @pl.when(first_core)
        def _():
            core_copy(start, count, group).start()

    def first_chain_steps(start, count, group):
        core_copy(start, count, group).wait_recv()
        for member in range(count):
            first_chain_step(start + member)

    group_count = pair_count // STATE_PAIRS
    signal_load.wait()
    state_pairs(0, HEAD_START)
    pl.semaphore_wait(barrier, 2 + jnp.where(has_next, 1, 0) + jnp.where(has_previous, 1, 0))
    core_copies(0, HEAD_START, 0)

    @pl.when(first_core)
    def _():
        totals_copy.start()

    state_pairs(HEAD_START, STATE_PAIRS - HEAD_START)
    core_copies(HEAD_START, STATE_PAIRS - HEAD_START, 1)

    @pl.when(second_core & first_chip)
    def _():
        first_chain_steps(0, HEAD_START, 0)

    @pl.loop(1, group_count)
    def _(group):
        start = group * STATE_PAIRS
        state_pairs(start, STATE_PAIRS)
        core_copies(start, STATE_PAIRS, group + 1)

        @pl.when(second_core & first_chip & (group == 1))
        def _():
            first_chain_steps(HEAD_START, STATE_PAIRS - HEAD_START, 1)

        @pl.when(second_core & first_chip & (group > 1))
        def _():
            first_chain_steps(start - STATE_PAIRS, STATE_PAIRS, group)

    @pl.when(second_core & first_chip)
    def _():
        first_chain_steps(pair_count - STATE_PAIRS, STATE_PAIRS, group_count)

    @pl.when(second_core)
    def _():
        totals_copy.wait_recv()

    skip_rows_ref[...] = three_parts(jnp.broadcast_to(params_ref[2:3, :], (16, LANES)))
    lead_ref[...] = jnp.exp2(run_ref[...])
    in_weights = row_log_ref[...]
    weight_log = jnp.where(in_weights > 0.0, jnp.log(in_weights) * LOG2E, -1e30)
    row_log_ref[...] = weight_log
    row_ref[...] = row_ref[...] - weight_log
    scores = jnp.dot(read_ref[...], read_by_token_ref[...], preferred_element_type=jnp.float32)
    scores_ref[...] = jnp.where(square_columns <= square_rows, scores, 0.0)
    square_ref[...] = jnp.zeros_like(square_ref)
    @pl.when(first_core & first_chip)
    def _():
        carry_ref[...] = jnp.zeros_like(carry_ref)

    @pl.loop(0, pair_count // MIX_PAIRS)
    def _(group):
        @pl.when(has_previous & has_next)
        def _():
            @pl.when(group == 0)
            def _():
                core_copy(0, HEAD_START, 0).wait_recv()

            @pl.when(group == 1)
            def _():
                core_copy(HEAD_START, STATE_PAIRS - HEAD_START, 1).wait_recv()

            @pl.when((group > 1) & (group % 2 == 0))
            def _():
                core_copy(group * MIX_PAIRS, STATE_PAIRS, group // 2 + 1).wait_recv()

            for member in range(MIX_PAIRS):
                chain_step(group * MIX_PAIRS + member)

        for member in range(MIX_PAIRS):
            mix_pair(group * MIX_PAIRS + member)

    gate_load.wait()
    last_step = has_previous & (scan_index == span_count - 1)

    @pl.when(last_step)
    def _():
        core_copy(0, HEAD_START, 0).wait_recv()
        core_copy(HEAD_START, STATE_PAIRS - HEAD_START, 1).wait_recv()

        @pl.loop(1, group_count)
        def _(group):
            core_copy(group * STATE_PAIRS, STATE_PAIRS, group + 1).wait_recv()

    def gate_pairs(start, count):
        @pl.when(last_step)
        def _():
            for member in range(count):
                chain_step(start + member)

        @pl.when(gets_entry)
        def _():
            for member in range(count):
                entry_copy(start + member).wait_recv()

        squares = square_ref[...]
        for member in range(count):
            squares = squares + gate_pair(start + member)
        square_ref[...] = squares

    @pl.loop(0, pair_count // GATE_PAIRS - 1)
    def _(group):
        gate_pairs(group * GATE_PAIRS, GATE_PAIRS)

    weight_load.wait()
    own_width = out_ref.shape[1]
    tile_count = own_width // TILE

    def tile_copy(tile):
        return pltpu.make_async_remote_copy(
            src_ref=sent_ref.at[tile],
            dst_ref=landed_ref.at[tile],
            send_sem=tile_send,
            recv_sem=tile_recv.at[tile],
            device_id={"tensor": peer},
            device_id_type=MESH,
        )

    def project(owner, tile, first=0, last=pair_count):
        start = pl.multiple_of(owner * own_width + tile * TILE, LANES)
        rows = slice(first * LANES, last * LANES)
        return jnp.dot(
            normed_ref[:, rows],
            weight_ref[rows, pl.ds(start, TILE)],
            preferred_element_type=jnp.float32,
        )

    early = pair_count - GATE_PAIRS
    own_ref[0] = project(peer, 0, 0, early)
    for pair in range(early, pair_count):
        gate_pairs(pair, 1)
    sent_ref[0] = (own_ref[0] + project(peer, 0, early)).astype(jnp.bfloat16)
    tile_copy(0).start()
    square_sum = jnp.sum(square_ref[...].T, axis=0, keepdims=True)
    square_out_ref[...] = jnp.broadcast_to(square_sum, square_out_ref.shape)
    square_copy = pltpu.make_async_remote_copy(
        src_ref=square_out_ref,
        dst_ref=square_in_ref,
        send_sem=square_send,
        recv_sem=square_recv,
        device_id={"tensor": peer},
        device_id_type=MESH,
    )
    square_copy.start()

    @pl.loop(1, tile_count)
    def _(tile):
        sent_ref[tile] = project(peer, tile).astype(jnp.bfloat16)
        tile_copy(tile).start()

    @pl.loop(0, tile_count)
    def _(tile):
        own_ref[tile] = project(tensor_index, tile)

    @pl.when(first_core)
    def _():
        totals_copy.wait_send()

    @pl.when(first_core | has_previous)
    def _():
        pltpu.make_async_copy(pass_ref, pass_ref, core_send).wait()

    @pl.when(has_next)
    def _():
        pltpu.make_async_copy(pass_ref, pass_ref, onward_send).wait()

    square_copy.wait()
    inner = 2 * heads * HEAD_DIM
    scale = lax.rsqrt((square_out_ref[0:1, :] + square_in_ref[0:1, :]) / inner + EPSILON)
    square_ref[...] = jnp.broadcast_to(scale, (LANES, STRETCH)).T

    @pl.loop(0, tile_count)
    def _(tile):
        tile_copy(tile).wait_recv()
        scales = square_ref[...]
        for side in range(TILE // LANES):
            start = pl.multiple_of(tile * TILE + side * LANES, LANES)
            columns = slice(side * LANES, (side + 1) * LANES)
            both = own_ref[tile, :, columns] + landed_ref[tile, :, columns].astype(jnp.float32)
            out_ref[:, pl.ds(start, LANES)] = (both * scales).astype(jnp.bfloat16)

    pltpu.make_async_copy(sent_ref, sent_ref, tile_send).wait()


def fused_on_device(
    span_count,
    signal,
    gate_branch,
    write_proj,
    read_proj,
    step_logits,
    valid_mask,
    stretch_band,
    band_offset,
    decay_log,
    step_offset,
    skip_gain,
    norm_gain,
    out_weight,
):
    heads = decay_log.shape[0]
    inner = heads * HEAD_DIM
    width = out_weight.shape[1]
    pair_count = heads // 2
    tile_count = width // 2 // TILE
    vmem = pl.BlockSpec(memory_space=pltpu.VMEM)
    hbm = pl.BlockSpec(memory_space=pl.ANY)
    f32, bf16 = jnp.float32, jnp.bfloat16
    return pl.pallas_call(
        functools.partial(fused_kernel, heads, span_count),
        out_shape=pltpu.VMEM((STRETCH, width // 2), bf16),
        in_specs=[hbm] * 13,
        out_specs=vmem,
        scratch_shapes=[
            pltpu.VMEM((inner, width), bf16),
            pltpu.VMEM((STRETCH, inner), bf16),
            pltpu.VMEM((STRETCH, inner), bf16),
            pltpu.VMEM((STRETCH, STATE), bf16),
            pltpu.VMEM((STRETCH, STATE), bf16),
            pltpu.VMEM((heads, STRETCH), f32),
            pltpu.VMEM((1, STRETCH), jnp.int32),
            pltpu.VMEM((1, 1), jnp.int32),
            pltpu.VMEM((BANDS, heads), f32),
            pltpu.VMEM((1, heads), f32),
            pltpu.VMEM((1, heads), f32),
            pltpu.VMEM((1, heads), f32),
            pltpu.VMEM((pair_count, LANES), f32),
            pltpu.VMEM((LANES, STRETCH), f32),
            pltpu.VMEM((8, LANES), f32),
            pltpu.VMEM((heads, STRETCH), f32),
            pltpu.VMEM((STRETCH, LANES), f32),
            pltpu.VMEM((STRETCH, LANES), f32),
            pltpu.VMEM((heads, STRETCH), f32),
            pltpu.VMEM((16, LANES), bf16),
            pltpu.VMEM((STRETCH, STRETCH), f32),
            pltpu.VMEM((STATE, STRETCH), bf16),
            pltpu.VMEM((pair_count, STATE, LANES), f32),
            pltpu.VMEM((-(-pair_count // 16) * 16, LANES), f32),
            pltpu.VMEM((-(-pair_count // 16) * 16, LANES), f32),
            pltpu.VMEM((STRETCH, inner), f32),
            pltpu.VMEM((STRETCH, inner), bf16),
            pltpu.VMEM((STRETCH, LANES), f32),
            pltpu.VMEM((pair_count, STATE, LANES), bf16),
            pltpu.VMEM((pair_count, STATE, LANES), bf16),
            pltpu.VMEM((pair_count, STATE, LANES), bf16),
            pltpu.VMEM((pair_count, STATE, LANES), bf16),
            pltpu.VMEM((tile_count, STRETCH, TILE), bf16),
            pltpu.VMEM((tile_count, STRETCH, TILE), f32),
            pltpu.VMEM((tile_count, STRETCH, TILE), bf16),
            pltpu.VMEM((8, STRETCH), f32),
            pltpu.VMEM((8, STRETCH), f32),
            pltpu.SemaphoreType.DMA((3,)),
            pltpu.SemaphoreType.DMA((10,)),
            pltpu.SemaphoreType.DMA,
            pltpu.SemaphoreType.DMA,
            pltpu.SemaphoreType.DMA,
            pltpu.SemaphoreType.DMA((pair_count // STATE_PAIRS + 1,)),
            pltpu.SemaphoreType.DMA,
            pltpu.SemaphoreType.DMA((pair_count * PIECES,)),
            pltpu.SemaphoreType.DMA,
            pltpu.SemaphoreType.DMA((tile_count,)),
            pltpu.SemaphoreType.DMA,
            pltpu.SemaphoreType.DMA,
        ],
        compiler_params=pltpu.CompilerParams(
            collective_id=0, has_side_effects=True, vmem_limit_bytes=60 * 1024 * 1024
        ),
    )(
        signal,
        gate_branch,
        write_proj,
        read_proj,
        step_logits,
        valid_mask[None, :],
        stretch_band[None, :],
        band_offset,
        decay_log[None, :],
        step_offset[None, :],
        skip_gain[None, :],
        norm_gain.reshape(pair_count, LANES),
        out_weight,
    )


def solution(mesh):
    placed = (
        P(("group", "scan", "band"), "tensor"),
        P(("group", "scan", "band"), "tensor"),
        P(("group", "scan", "band"), None),
        P(("group", "scan", "band"), None),
        P("tensor", ("group", "scan", "band")),
        P(("group", "scan", "band")),
        P(("group", "scan", "band")),
        P(None, "tensor"),
        P("tensor"),
        P("tensor"),
        P("tensor"),
        P("tensor"),
        P("tensor", None),
    )
    shape = dict(mesh.shape)
    places = shape["scan"] * shape["band"]

    def layer(*arrays):
        rows = arrays[0].shape[0] // (shape["group"] * places)
        heads = arrays[8].shape[0] // shape["tensor"]
        width = arrays[12].shape[1]
        fits = (
            shape["tensor"] == 2
            and shape["band"] == 2
            and shape["scan"] >= 2
            and rows == STRETCH
            and heads % (2 * STATE_PAIRS) == 0
            and heads % (2 * MIX_PAIRS) == 0
            and heads % (2 * GATE_PAIRS) == 0
            and 3 * heads <= LANES
            and heads <= HEAD_DIM
            and width % (2 * TILE) == 0
        )
        member = on_device
        if fits:
            member = functools.partial(fused_on_device, shape["scan"])
        return mapped(member)(*arrays)

    def mapped(member):
        return jax.shard_map(
            member,
            mesh=mesh,
            in_specs=placed,
            out_specs=P(("group", "scan", "band"), "tensor"),
            check_vma=False,
        )

    return layer
```

```python
import functools

import jax
import jax.numpy as jnp
from jax import lax
from jax.experimental import pallas as pl
from jax.experimental.pallas import tpu as pltpu
from jax.sharding import PartitionSpec as P

HEAD_DIM = 64
STATE = 128
STRETCH = 256
BANDS = 12
INNER = 5120


EPSILON = 1e-05
HIGHEST = lax.Precision.HIGHEST


def step_sizes(step_logits, stretch_band, band_offset, step_offset):
    one_hot = (stretch_band[:, None] == jnp.arange(BANDS, dtype=jnp.int32)[None, :]).astype(
        jnp.float32
    )
    stretch_offset = jnp.dot(one_hot, band_offset, precision=HIGHEST)
    token_offset = jnp.repeat(stretch_offset, STRETCH, axis=0).T
    return jax.nn.softplus(step_logits + step_offset[:, None] + token_offset)


def combine(earlier, later_pair):
    return (
        earlier[0] + later_pair[0],
        jnp.exp(later_pair[0])[:, None, None] * earlier[1] + later_pair[1],
    )


def local_step(running_pair, member):
    return (combine(running_pair, member), running_pair)


def on_device(
    signal,
    gate_branch,
    write_proj,
    read_proj,
    step_logits,
    valid_mask,
    stretch_band,
    band_offset,
    decay_log,
    step_offset,
    skip_gain,
    norm_gain,
    out_weight,
):
    row_count = signal.shape[0]
    head_count = decay_log.shape[0]
    block_count = row_count // STRETCH
    step_size = step_sizes(step_logits, stretch_band, band_offset, step_offset)
    log_decay = step_size * (-jnp.exp(decay_log))[:, None]
    input_weight = step_size * valid_mask.astype(jnp.float32)[None, :]
    running = lax.associative_scan(
        jnp.add, log_decay.reshape(head_count, block_count, STRETCH), axis=2
    )
    weight_blocks = input_weight.reshape(head_count, block_count, STRETCH)
    signal_blocks = signal.reshape(block_count, STRETCH, head_count, HEAD_DIM)
    write_blocks = write_proj.reshape(block_count, STRETCH, STATE)
    read_blocks = read_proj.reshape(block_count, STRETCH, STATE)
    scores = jnp.einsum(
        "cin,cjn->cij", read_blocks, write_blocks, preferred_element_type=jnp.float32
    )
    lower_mask = jnp.arange(STRETCH)[:, None] >= jnp.arange(STRETCH)[None, :]
    span_logs = jnp.where(
        lower_mask[None, None], running[:, :, :, None] - running[:, :, None, :], -1e30
    )
    mixing = (jnp.exp(span_logs) * scores[None] * weight_blocks[:, :, None, :]).astype(jnp.bfloat16)
    local_out = jnp.einsum(
        "hcij,cjhp->cihp", mixing, signal_blocks, preferred_element_type=jnp.float32
    )
    tail_weight = jnp.exp(running[:, :, -1:] - running) * weight_blocks
    scaled = (
        signal_blocks.astype(jnp.float32) * jnp.transpose(tail_weight, (1, 2, 0))[:, :, :, None]
    ).astype(jnp.bfloat16)
    block_states = jnp.einsum(
        "cjhp,cjn->chpn", scaled, write_blocks, preferred_element_type=jnp.float32
    )
    block_decay = running[:, :, -1].T
    zero_state = jnp.zeros((head_count, HEAD_DIM, STATE), jnp.float32)
    zero_log = jnp.zeros((head_count,), jnp.float32)
    identity = (zero_log, zero_state)
    device_pair, segment_cumulative = lax.scan(local_step, identity, (block_decay, block_states))
    all_logs = lax.all_gather(device_pair[0][None], ("scan", "band"), axis=0, tiled=True)
    inclusive = lax.associative_scan(jnp.add, all_logs, axis=0)
    exclusive = inclusive - all_logs
    position = lax.axis_index(("scan", "band"))
    own_exclusive = lax.dynamic_index_in_dim(exclusive, position, 0, keepdims=False)
    shard_block = lax.all_gather(
        device_pair[1][None].astype(jnp.bfloat16), ("scan", "band"), axis=0, tiled=True
    ).astype(jnp.float32)
    how_many = shard_block.shape[0]
    sources = jnp.arange(how_many, dtype=jnp.int32)
    gap_logs = jnp.where((sources < position)[:, None], own_exclusive[None, :] - inclusive, -1e30)
    carry_state = zero_state + jnp.einsum(
        "kh,khpn->hpn", jnp.exp(gap_logs), shard_block, precision=HIGHEST
    )
    enter_state = (
        jnp.exp(segment_cumulative[0])[:, :, None, None] * carry_state[None] + segment_cumulative[1]
    )
    state_high = enter_state.astype(jnp.bfloat16)
    widened = lax.optimization_barrier(state_high).astype(jnp.float32)
    state_low = (enter_state - widened).astype(jnp.bfloat16)
    high_part = jnp.einsum(
        "cin,chpn->cihp", read_blocks, state_high, preferred_element_type=jnp.float32
    )
    low_part = jnp.einsum(
        "cin,chpn->cihp", read_blocks, state_low, preferred_element_type=jnp.float32
    )
    carried_out = jnp.transpose(jnp.exp(running), (1, 2, 0))[:, :, :, None] * (high_part + low_part)
    ssm_out = (local_out + carried_out).reshape(row_count, head_count, HEAD_DIM) + skip_gain[
        None, :, None
    ] * signal.reshape(row_count, head_count, HEAD_DIM).astype(jnp.float32)
    gated_out = ssm_out.reshape(row_count, head_count * HEAD_DIM) * jax.nn.silu(
        gate_branch.astype(jnp.float32)
    )
    square_total = lax.psum(jnp.sum(gated_out * gated_out, axis=1), "tensor")
    normed = (
        gated_out * lax.rsqrt(square_total / INNER + EPSILON)[:, None] * norm_gain[None, :]
    ).astype(jnp.bfloat16)
    own_columns = lax.psum_scatter(
        lax.dot_general(
            out_weight, normed, (((0,), (1,)), ((), ())), preferred_element_type=jnp.float32
        ).astype(jnp.bfloat16),
        "tensor",
        scatter_dimension=0,
        tiled=True,
    ).astype(jnp.float32)
    return own_columns.T.astype(jnp.bfloat16)


LOG2E = 1.4426950408889634
LANES = 128
STATE_PAIRS = 4
HEAD_START = 2
PIECES = 1
PIECE = STATE // PIECES
MIX_PAIRS = 2
GATE_PAIRS = 2
TILE = 256
MESH = pl.DeviceIdType.MESH


def fused_kernel(
    heads,
    span_count,
    signal_hbm,
    gate_hbm,
    write_hbm,
    read_hbm,
    logits_hbm,
    valid_hbm,
    band_hbm,
    offset_hbm,
    decay_hbm,
    bias_hbm,
    skip_hbm,
    gain_hbm,
    weight_hbm,
    out_ref,
    weight_ref,
    signal_ref,
    gate_ref,
    write_ref,
    read_ref,
    logits_ref,
    valid_ref,
    band_ref,
    offset_ref,
    decay_ref,
    bias_ref,
    skip_ref,
    gain_ref,
    padded_ref,
    params_ref,
    row_ref,
    run_ref,
    lead_ref,
    row_log_ref,
    skip_rows_ref,
    scores_ref,
    read_by_token_ref,
    state_ref,
    totals_ref,
    core_totals_ref,
    local_ref,
    normed_ref,
    square_ref,
    carry_ref,
    pass_ref,
    core_state_ref,
    entry_ref,
    sent_ref,
    own_ref,
    parts_ref,
    landed_ref,
    square_out_ref,
    square_in_ref,
    load_sem,
    small_sem,
    totals_send,
    totals_recv,
    core_send,
    core_recv,
    onward_send,
    arrival,
    tile_send,
    tile_recv,
    square_send,
    square_recv,
):
    pair_count = heads // 2
    scan_index = lax.axis_index("scan")
    band_index = lax.axis_index("band")
    tensor_index = lax.axis_index("tensor")
    first_core = band_index == 0
    second_core = band_index == 1
    first_chip = scan_index == 0
    has_previous = second_core & (scan_index > 0)
    has_next = second_core & (scan_index < span_count - 1)
    gets_entry = first_core & (scan_index > 0)
    peer = 1 - tensor_index
    other_core = {"band": 1 - band_index}
    following = {"scan": lax.rem(scan_index + 1, span_count)}
    previous = {"scan": lax.rem(scan_index + span_count - 1, span_count)}

    signal_load = pltpu.make_async_copy(signal_hbm, signal_ref, load_sem.at[2])
    gate_load = pltpu.make_async_copy(gate_hbm, gate_ref, load_sem.at[0])
    weight_load = pltpu.make_async_copy(weight_hbm, weight_ref, load_sem.at[1])
    small_loads = [
        pltpu.make_async_copy(source, target, small_sem.at[spot])
        for spot, (source, target) in enumerate(
            (
                (logits_hbm, logits_ref),
                (band_hbm, band_ref),
                (offset_hbm, offset_ref),
                (decay_hbm, decay_ref),
                (bias_hbm, bias_ref),
                (valid_hbm, valid_ref),
                (skip_hbm, skip_ref),
                (write_hbm, write_ref),
                (read_hbm, read_ref),
                (gain_hbm, gain_ref),
            )
        )
    ]
    for load in small_loads:
        load.start()
    signal_load.start()

    barrier = pltpu.get_barrier_semaphore()
    for target in (other_core, {"tensor": peer}):
        pl.semaphore_signal(barrier, inc=1, device_id=target, device_id_type=MESH)

    @pl.when(has_next)
    def _():
        pl.semaphore_signal(barrier, inc=1, device_id=following, device_id_type=MESH)

    @pl.when(has_previous)
    def _():
        pl.semaphore_signal(barrier, inc=1, device_id=previous, device_id_type=MESH)

    for load in small_loads:
        load.wait()

    params_ref[...] = jnp.zeros_like(params_ref)
    chosen = lax.broadcasted_iota(jnp.int32, (BANDS, heads), 0) == band_ref[...]
    params_ref[0:1, 0:heads] = bias_ref[...] + jnp.sum(
        jnp.where(chosen, offset_ref[...], 0.0), axis=0, keepdims=True
    )
    params_ref[1:2, 0:heads] = jnp.exp(decay_ref[...]) * -LOG2E
    params_ref[2:3, 0:heads] = skip_ref[...]
    head_columns = params_ref[...].T[0:heads]
    shifted = logits_ref[...] + head_columns[:, 0:1]
    step_size = jnp.maximum(shifted, 0.0) + jnp.log1p(jnp.exp(-jnp.abs(shifted)))
    lanes = lax.broadcasted_iota(jnp.int32, (STRETCH, LANES), 1)
    square_rows = lax.broadcasted_iota(jnp.int32, (STRETCH, STRETCH), 0)
    square_columns = lax.broadcasted_iota(jnp.int32, (STRETCH, STRETCH), 1)
    high = step_size.astype(jnp.bfloat16).astype(jnp.float32)
    middle = (step_size - high).astype(jnp.bfloat16).astype(jnp.float32)
    low = step_size - high - middle
    sums = jnp.dot(
        jnp.concatenate([high, middle, low], axis=0).astype(jnp.bfloat16),
        jnp.where(square_rows <= square_columns, 1.0, 0.0).astype(jnp.bfloat16),
        preferred_element_type=jnp.float32,
    )
    summed = sums[0:heads] + sums[heads : 2 * heads] + sums[2 * heads : 3 * heads]
    running = summed * head_columns[:, 1:2]
    in_weight = step_size * valid_ref[...].astype(jnp.float32)
    tail = jnp.exp2(running[:, STRETCH - 1 : STRETCH] - running) * in_weight
    row_ref[...] = running
    row_log_ref[...] = in_weight
    padded_ref[...] = jnp.zeros_like(padded_ref)
    padded_ref[0:heads, :] = tail
    padded_ref[HEAD_DIM : HEAD_DIM + heads, :] = running
    factors = padded_ref[...].T
    run_ref[...] = factors

    def three_parts(value):
        high = value.astype(jnp.bfloat16).astype(jnp.float32)
        rest = value - high
        middle = rest.astype(jnp.bfloat16).astype(jnp.float32)
        low = rest - middle
        packed = high + pltpu.roll(middle, heads, 1) + pltpu.roll(low, 2 * heads, 1)
        return packed.astype(jnp.bfloat16)

    last_running = pltpu.roll(factors[STRETCH - 16 : STRETCH], LANES - HEAD_DIM, 1)
    running_parts = three_parts(jnp.where(lanes[0:16] < heads, last_running, 0.0))
    part = lax.broadcasted_iota(jnp.int32, (LANES, 2 * LANES), 0)
    part = (
        part
        - jnp.where(part >= heads, heads, 0)
        - jnp.where(part >= 2 * heads, heads, 0)
    )
    head_of = lax.broadcasted_iota(jnp.int32, totals_ref.shape, 1)
    head_of = (
        head_of
        - jnp.where(head_of >= heads, heads, 0)
        - jnp.where(head_of >= 2 * heads, heads, 0)
    )
    own_pair = head_of // 2 == lax.broadcasted_iota(jnp.int32, totals_ref.shape, 0)
    last_parts = running_parts.astype(jnp.float32)[15:16, :]
    last_rows = (
        jnp.dot(
            jnp.where(own_pair, last_parts, 0.0).astype(jnp.bfloat16),
            jnp.where(
                part[:, 0:LANES] % 2
                == lax.broadcasted_iota(jnp.int32, (LANES, LANES), 1) // HEAD_DIM,
                1.0,
                0.0,
            ).astype(jnp.bfloat16),
            preferred_element_type=jnp.float32,
        )
    )
    totals_ref[...] = jnp.exp2(last_rows)
    write_turned = write_ref[...].astype(jnp.float32).T.astype(jnp.bfloat16)
    read_by_token_ref[...] = write_turned

    totals_copy = pltpu.make_async_remote_copy(
        src_ref=totals_ref,
        dst_ref=core_totals_ref,
        send_sem=totals_send,
        recv_sem=totals_recv,
        device_id=other_core,
        device_id_type=MESH,
    )

    def core_copy(start, count, group):
        members = pl.ds(start, count)
        return pltpu.make_async_remote_copy(
            src_ref=pass_ref.at[members],
            dst_ref=core_state_ref.at[members],
            send_sem=core_send,
            recv_sem=core_recv.at[group],
            device_id=other_core,
            device_id_type=MESH,
        )

    def onward_copy(pair, piece):
        rows = pl.ds(piece * PIECE, PIECE)
        return pltpu.make_async_remote_copy(
            src_ref=pass_ref.at[pair, rows],
            dst_ref=entry_ref.at[pair, rows],
            send_sem=onward_send,
            recv_sem=arrival.at[pair * PIECES + piece],
            device_id=following,
            device_id_type=MESH,
        )

    def entry_copy(pair):
        return pltpu.make_async_remote_copy(
            src_ref=entry_ref.at[pair],
            dst_ref=carry_ref.at[pair],
            send_sem=core_send,
            recv_sem=arrival.at[pair * PIECES],
            device_id=other_core,
            device_id_type=MESH,
        )

    def give_onward(pair, piece, carry):
        rows = slice(piece * PIECE, (piece + 1) * PIECE)
        onward = totals_ref[pl.ds(pair, 1), :] * carry + state_ref[pair, rows]
        pass_ref[pair, rows] = onward.astype(jnp.bfloat16)
        onward_copy(pair, piece).start()

    def first_chain_step(pair):
        own = core_state_ref[pair]
        carry_ref[pair] = own

        @pl.when(has_next)
        def _():
            for piece in range(PIECES):
                rows = slice(piece * PIECE, (piece + 1) * PIECE)
                give_onward(pair, piece, own[rows].astype(jnp.float32))

    def chain_step(pair):
        for piece in range(PIECES):
            rows = slice(piece * PIECE, (piece + 1) * PIECE)
            onward_copy(pair, piece).wait_recv()
            if piece == PIECES - 1:

                @pl.when(jnp.logical_not(has_next))
                def _():
                    entry_copy(pair).start()

            carry = core_totals_ref[pl.ds(pair, 1), :] * entry_ref[pair, rows].astype(
                jnp.float32
            ) + core_state_ref[pair, rows].astype(jnp.float32)
            carry_ref[pair, rows] = carry.astype(jnp.bfloat16)

            @pl.when(has_next)
            def _():
                give_onward(pair, piece, carry)
                if piece == PIECES - 1:
                    entry_copy(pair).start()

    def columns_of(pair):
        return pl.ds(pl.multiple_of(pair * LANES, LANES), LANES)

    narrow_side = lax.broadcasted_iota(jnp.int32, (LANES, LANES), 1) // HEAD_DIM
    narrow_index = part[:, 0:LANES] - narrow_side
    first_half = lanes < HEAD_DIM
    second_half = lanes >= HEAD_DIM

    def picker(index, pair):
        return jnp.where(index == 2 * pair, 1.0, 0.0).astype(jnp.bfloat16)

    def spread(values, index):
        return jnp.take_along_axis(values, index, axis=1, mode="promise_in_bounds")

    def pair_heads(pair):
        return 2 * pair + lanes // HEAD_DIM

    def state_pair(pair):
        columns = columns_of(pair)
        tail = spread(run_ref[...], pair_heads(pair))
        scaled = (signal_ref[:, columns].astype(jnp.float32) * tail).astype(jnp.bfloat16)
        state = jnp.dot(read_by_token_ref[...], scaled, preferred_element_type=jnp.float32)
        state_ref[pair] = state
        pass_ref[pair] = state.astype(jnp.bfloat16)


    def mix_pair(pair):
        columns = columns_of(pair)
        half = STRETCH // 2
        fed = signal_ref[:, columns]
        tops, bottoms, sides = [], [], []
        for side in range(2):
            row = row_ref[pl.ds(2 * pair + side, 1), :]
            most = row_log_ref[pl.ds(2 * pair + side, 1), :]
            run = spread(run_ref[...], jnp.full((STRETCH, LANES), HEAD_DIM + 2 * pair + side, jnp.int32))
            near = jnp.exp2(jnp.minimum(run[0:half] - row[:, 0:half], most[:, 0:half]))
            far = jnp.exp2(run[half:] - row[:, 0:half])
            late = jnp.exp2(jnp.minimum(run[half:] - row[:, half:], most[:, half:]))
            tops.append((near * scores_ref[0:half, 0:half]).astype(jnp.bfloat16))
            bottoms.append((far * scores_ref[half:, 0:half]).astype(jnp.bfloat16))
            bottoms.append((late * scores_ref[half:, half:]).astype(jnp.bfloat16))
            sides.append(jnp.where(first_half if side == 0 else second_half, fed, jnp.zeros_like(fed)))
        local_ref[0:half, columns] = jnp.dot(
            jnp.concatenate(tops, axis=1),
            jnp.concatenate([sides[0][0:half], sides[1][0:half]], axis=0),
            preferred_element_type=jnp.float32,
        )
        local_ref[half:, columns] = jnp.dot(
            jnp.concatenate(bottoms, axis=1),
            jnp.concatenate(sides, axis=0),
            preferred_element_type=jnp.float32,
        )

    def gate_parts(pair):
        columns = columns_of(pair)
        skip = jnp.dot(
            skip_rows_ref[...], picker(narrow_index, pair), preferred_element_type=jnp.float32
        )
        own = local_ref[:, columns] + skip[0:1, :] * signal_ref[:, columns].astype(jnp.float32)
        gate = gate_ref[:, columns].astype(jnp.float32)
        lead = spread(lead_ref[...], HEAD_DIM + pair_heads(pair))
        return own, lead, gate / (1.0 + jnp.exp(-gate))

    def gate_pair(pair, own, lead, gate):
        carried = jnp.dot(read_ref[...], carry_ref[pair], preferred_element_type=jnp.float32)
        gated = (own + lead * carried) * gate
        normed_ref[:, columns_of(pair)] = (gated * gain_ref[pl.ds(pair, 1), :]).astype(
            jnp.bfloat16
        )
        return gated * gated

    def state_pairs(start, count):
        for member in range(count):
            state_pair(start + member)

    def core_copies(start, count, group):
        @pl.when(first_core)
        def _():
            core_copy(start, count, group).start()

    def first_chain_steps(start, count, group):
        core_copy(start, count, group).wait_recv()
        for member in range(count):
            first_chain_step(start + member)

    group_count = pair_count // STATE_PAIRS
    signal_load.wait()
    state_pairs(0, HEAD_START)
    pl.semaphore_wait(barrier, 2 + jnp.where(has_next, 1, 0) + jnp.where(has_previous, 1, 0))
    core_copies(0, HEAD_START, 0)

    @pl.when(first_core)
    def _():
        totals_copy.start()

    gate_load.start()
    weight_load.start()
    state_pairs(HEAD_START, STATE_PAIRS - HEAD_START)
    core_copies(HEAD_START, STATE_PAIRS - HEAD_START, 1)

    @pl.when(second_core & first_chip)
    def _():
        first_chain_steps(0, HEAD_START, 0)

    @pl.loop(1, group_count)
    def _(group):
        start = group * STATE_PAIRS
        state_pairs(start, STATE_PAIRS)
        core_copies(start, STATE_PAIRS, group + 1)

        @pl.when(second_core & first_chip & (group == 1))
        def _():
            first_chain_steps(HEAD_START, STATE_PAIRS - HEAD_START, 1)

        @pl.when(second_core & first_chip & (group > 1))
        def _():
            first_chain_steps(start - STATE_PAIRS, STATE_PAIRS, group)

    @pl.when(second_core & first_chip)
    def _():
        first_chain_steps(pair_count - STATE_PAIRS, STATE_PAIRS, group_count)

    @pl.when(second_core)
    def _():
        totals_copy.wait_recv()

    skip_rows_ref[...] = three_parts(jnp.broadcast_to(params_ref[2:3, :], (16, LANES)))
    lead_ref[...] = jnp.exp2(run_ref[...])
    in_weights = row_log_ref[...]
    weight_log = jnp.where(in_weights > 0.0, jnp.log(in_weights) * LOG2E, -1e30)
    row_log_ref[...] = weight_log
    row_ref[...] = row_ref[...] - weight_log
    scores = jnp.dot(read_ref[...], read_by_token_ref[...], preferred_element_type=jnp.float32)
    scores_ref[...] = jnp.where(square_columns <= square_rows, scores, 0.0)
    square_ref[...] = jnp.zeros_like(square_ref)
    @pl.when(first_core & first_chip)
    def _():
        carry_ref[...] = jnp.zeros_like(carry_ref)

    @pl.loop(0, pair_count // MIX_PAIRS)
    def _(group):
        @pl.when(has_previous & has_next)
        def _():
            @pl.when(group == 0)
            def _():
                core_copy(0, HEAD_START, 0).wait_recv()

            @pl.when(group == 1)
            def _():
                core_copy(HEAD_START, STATE_PAIRS - HEAD_START, 1).wait_recv()

            @pl.when((group > 1) & (group % 2 == 0))
            def _():
                core_copy(group * MIX_PAIRS, STATE_PAIRS, group // 2 + 1).wait_recv()

            for member in range(MIX_PAIRS):
                chain_step(group * MIX_PAIRS + member)

        for member in range(MIX_PAIRS):
            mix_pair(group * MIX_PAIRS + member)

    gate_load.wait()
    last_step = has_previous & (scan_index == span_count - 1)

    @pl.when(last_step)
    def _():
        core_copy(0, HEAD_START, 0).wait_recv()
        core_copy(HEAD_START, STATE_PAIRS - HEAD_START, 1).wait_recv()

        @pl.loop(1, group_count)
        def _(group):
            core_copy(group * STATE_PAIRS, STATE_PAIRS, group + 1).wait_recv()

    def await_carry(start, count):
        @pl.when(last_step)
        def _():
            for member in range(count):
                chain_step(start + member)

        @pl.when(gets_entry)
        def _():
            for member in range(count):
                entry_copy(start + member).wait_recv()

    @pl.loop(0, pair_count // GATE_PAIRS - 1)
    def _(group):
        start = group * GATE_PAIRS
        await_carry(start, GATE_PAIRS)
        squares = square_ref[...]
        for member in range(GATE_PAIRS):
            squares = squares + gate_pair(start + member, *gate_parts(start + member))
        square_ref[...] = squares

    weight_load.wait()
    own_width = out_ref.shape[1]
    tile_count = own_width // TILE

    def tile_copy(tile):
        return pltpu.make_async_remote_copy(
            src_ref=sent_ref.at[tile],
            dst_ref=landed_ref.at[tile],
            send_sem=tile_send,
            recv_sem=tile_recv.at[tile],
            device_id={"tensor": peer},
            device_id_type=MESH,
        )

    def project(owner, tile, first=0, last=pair_count):
        start = pl.multiple_of(owner * own_width + tile * TILE, LANES)
        rows = slice(first * LANES, last * LANES)
        return jnp.dot(
            normed_ref[:, rows],
            weight_ref[rows, pl.ds(start, TILE)],
            preferred_element_type=jnp.float32,
        )

    early = pair_count - GATE_PAIRS
    for spot in range(GATE_PAIRS):
        for kind, value in enumerate(gate_parts(early + spot)):
            parts_ref[spot, kind] = value
    own_ref[0] = project(peer, 0, 0, early)
    for spot in range(GATE_PAIRS):
        pair = early + spot
        await_carry(pair, 1)
        square_ref[...] += gate_pair(
            pair, parts_ref[spot, 0], parts_ref[spot, 1], parts_ref[spot, 2]
        )
        if spot < GATE_PAIRS - 1:
            own_ref[0] += project(peer, 0, pair, pair + 1)
    sent_ref[0] = (own_ref[0] + project(peer, 0, pair_count - 1)).astype(jnp.bfloat16)
    tile_copy(0).start()
    square_sum = jnp.sum(square_ref[...].T, axis=0, keepdims=True)
    square_out_ref[...] = jnp.broadcast_to(square_sum, square_out_ref.shape)
    square_copy = pltpu.make_async_remote_copy(
        src_ref=square_out_ref,
        dst_ref=square_in_ref,
        send_sem=square_send,
        recv_sem=square_recv,
        device_id={"tensor": peer},
        device_id_type=MESH,
    )
    square_copy.start()

    @pl.loop(1, tile_count)
    def _(tile):
        sent_ref[tile] = project(peer, tile).astype(jnp.bfloat16)
        tile_copy(tile).start()

    @pl.loop(0, tile_count)
    def _(tile):
        own_ref[tile] = project(tensor_index, tile)

    @pl.when(first_core)
    def _():
        totals_copy.wait_send()

    @pl.when(first_core | has_previous)
    def _():
        pltpu.make_async_copy(pass_ref, pass_ref, core_send).wait()

    @pl.when(has_next)
    def _():
        pltpu.make_async_copy(pass_ref, pass_ref, onward_send).wait()

    square_copy.wait()
    inner = 2 * heads * HEAD_DIM
    scale = lax.rsqrt((square_out_ref[0:1, :] + square_in_ref[0:1, :]) / inner + EPSILON)
    square_ref[...] = jnp.broadcast_to(scale, (LANES, STRETCH)).T

    @pl.loop(0, tile_count)
    def _(tile):
        tile_copy(tile).wait_recv()
        scales = square_ref[...]
        for side in range(TILE // LANES):
            start = pl.multiple_of(tile * TILE + side * LANES, LANES)
            columns = slice(side * LANES, (side + 1) * LANES)
            both = own_ref[tile, :, columns] + landed_ref[tile, :, columns].astype(jnp.float32)
            out_ref[:, pl.ds(start, LANES)] = (both * scales).astype(jnp.bfloat16)

    pltpu.make_async_copy(sent_ref, sent_ref, tile_send).wait()


def fused_on_device(
    span_count,
    signal,
    gate_branch,
    write_proj,
    read_proj,
    step_logits,
    valid_mask,
    stretch_band,
    band_offset,
    decay_log,
    step_offset,
    skip_gain,
    norm_gain,
    out_weight,
):
    heads = decay_log.shape[0]
    inner = heads * HEAD_DIM
    width = out_weight.shape[1]
    pair_count = heads // 2
    tile_count = width // 2 // TILE
    vmem = pl.BlockSpec(memory_space=pltpu.VMEM)
    hbm = pl.BlockSpec(memory_space=pl.ANY)
    f32, bf16 = jnp.float32, jnp.bfloat16
    return pl.pallas_call(
        functools.partial(fused_kernel, heads, span_count),
        out_shape=pltpu.VMEM((STRETCH, width // 2), bf16),
        in_specs=[hbm] * 13,
        out_specs=vmem,
        scratch_shapes=[
            pltpu.VMEM((inner, width), bf16),
            pltpu.VMEM((STRETCH, inner), bf16),
            pltpu.VMEM((STRETCH, inner), bf16),
            pltpu.VMEM((STRETCH, STATE), bf16),
            pltpu.VMEM((STRETCH, STATE), bf16),
            pltpu.VMEM((heads, STRETCH), f32),
            pltpu.VMEM((1, STRETCH), jnp.int32),
            pltpu.VMEM((1, 1), jnp.int32),
            pltpu.VMEM((BANDS, heads), f32),
            pltpu.VMEM((1, heads), f32),
            pltpu.VMEM((1, heads), f32),
            pltpu.VMEM((1, heads), f32),
            pltpu.VMEM((pair_count, LANES), f32),
            pltpu.VMEM((LANES, STRETCH), f32),
            pltpu.VMEM((8, LANES), f32),
            pltpu.VMEM((heads, STRETCH), f32),
            pltpu.VMEM((STRETCH, LANES), f32),
            pltpu.VMEM((STRETCH, LANES), f32),
            pltpu.VMEM((heads, STRETCH), f32),
            pltpu.VMEM((16, LANES), bf16),
            pltpu.VMEM((STRETCH, STRETCH), f32),
            pltpu.VMEM((STATE, STRETCH), bf16),
            pltpu.VMEM((pair_count, STATE, LANES), f32),
            pltpu.VMEM((-(-pair_count // 16) * 16, LANES), f32),
            pltpu.VMEM((-(-pair_count // 16) * 16, LANES), f32),
            pltpu.VMEM((STRETCH, inner), f32),
            pltpu.VMEM((STRETCH, inner), bf16),
            pltpu.VMEM((STRETCH, LANES), f32),
            pltpu.VMEM((pair_count, STATE, LANES), bf16),
            pltpu.VMEM((pair_count, STATE, LANES), bf16),
            pltpu.VMEM((pair_count, STATE, LANES), bf16),
            pltpu.VMEM((pair_count, STATE, LANES), bf16),
            pltpu.VMEM((tile_count, STRETCH, TILE), bf16),
            pltpu.VMEM((tile_count, STRETCH, TILE), f32),
            pltpu.VMEM((GATE_PAIRS, 3, STRETCH, LANES), f32),
            pltpu.VMEM((tile_count, STRETCH, TILE), bf16),
            pltpu.VMEM((8, STRETCH), f32),
            pltpu.VMEM((8, STRETCH), f32),
            pltpu.SemaphoreType.DMA((3,)),
            pltpu.SemaphoreType.DMA((10,)),
            pltpu.SemaphoreType.DMA,
            pltpu.SemaphoreType.DMA,
            pltpu.SemaphoreType.DMA,
            pltpu.SemaphoreType.DMA((pair_count // STATE_PAIRS + 1,)),
            pltpu.SemaphoreType.DMA,
            pltpu.SemaphoreType.DMA((pair_count * PIECES,)),
            pltpu.SemaphoreType.DMA,
            pltpu.SemaphoreType.DMA((tile_count,)),
            pltpu.SemaphoreType.DMA,
            pltpu.SemaphoreType.DMA,
        ],
        compiler_params=pltpu.CompilerParams(
            collective_id=0, has_side_effects=True, vmem_limit_bytes=60 * 1024 * 1024
        ),
    )(
        signal,
        gate_branch,
        write_proj,
        read_proj,
        step_logits,
        valid_mask[None, :],
        stretch_band[None, :],
        band_offset,
        decay_log[None, :],
        step_offset[None, :],
        skip_gain[None, :],
        norm_gain.reshape(pair_count, LANES),
        out_weight,
    )


def solution(mesh):
    placed = (
        P(("group", "scan", "band"), "tensor"),
        P(("group", "scan", "band"), "tensor"),
        P(("group", "scan", "band"), None),
        P(("group", "scan", "band"), None),
        P("tensor", ("group", "scan", "band")),
        P(("group", "scan", "band")),
        P(("group", "scan", "band")),
        P(None, "tensor"),
        P("tensor"),
        P("tensor"),
        P("tensor"),
        P("tensor"),
        P("tensor", None),
    )
    shape = dict(mesh.shape)
    places = shape["scan"] * shape["band"]

    def layer(*arrays):
        rows = arrays[0].shape[0] // (shape["group"] * places)
        heads = arrays[8].shape[0] // shape["tensor"]
        width = arrays[12].shape[1]
        fits = (
            shape["tensor"] == 2
            and shape["band"] == 2
            and shape["scan"] >= 2
            and rows == STRETCH
            and heads % (2 * STATE_PAIRS) == 0
            and heads % (2 * MIX_PAIRS) == 0
            and heads % (2 * GATE_PAIRS) == 0
            and 3 * heads <= LANES
            and heads <= HEAD_DIM
            and width % (2 * TILE) == 0
        )
        member = on_device
        if fits:
            member = functools.partial(fused_on_device, shape["scan"])
        return mapped(member)(*arrays)

    def mapped(member):
        return jax.shard_map(
            member,
            mesh=mesh,
            in_specs=placed,
            out_specs=P(("group", "scan", "band"), "tensor"),
            check_vma=False,
        )

    return layer
```

```python
import functools

import jax
import jax.numpy as jnp
from jax import lax
from jax.experimental import pallas as pl
from jax.experimental.pallas import tpu as pltpu
from jax.sharding import PartitionSpec as P

HEAD_DIM = 64
STATE = 128
STRETCH = 256
BANDS = 12
INNER = 5120


EPSILON = 1e-05
HIGHEST = lax.Precision.HIGHEST


def step_sizes(step_logits, stretch_band, band_offset, step_offset):
    one_hot = (stretch_band[:, None] == jnp.arange(BANDS, dtype=jnp.int32)[None, :]).astype(
        jnp.float32
    )
    stretch_offset = jnp.dot(one_hot, band_offset, precision=HIGHEST)
    token_offset = jnp.repeat(stretch_offset, STRETCH, axis=0).T
    return jax.nn.softplus(step_logits + step_offset[:, None] + token_offset)


def combine(earlier, later_pair):
    return (
        earlier[0] + later_pair[0],
        jnp.exp(later_pair[0])[:, None, None] * earlier[1] + later_pair[1],
    )


def local_step(running_pair, member):
    return (combine(running_pair, member), running_pair)


def on_device(
    signal,
    gate_branch,
    write_proj,
    read_proj,
    step_logits,
    valid_mask,
    stretch_band,
    band_offset,
    decay_log,
    step_offset,
    skip_gain,
    norm_gain,
    out_weight,
):
    row_count = signal.shape[0]
    head_count = decay_log.shape[0]
    block_count = row_count // STRETCH
    step_size = step_sizes(step_logits, stretch_band, band_offset, step_offset)
    log_decay = step_size * (-jnp.exp(decay_log))[:, None]
    input_weight = step_size * valid_mask.astype(jnp.float32)[None, :]
    running = lax.associative_scan(
        jnp.add, log_decay.reshape(head_count, block_count, STRETCH), axis=2
    )
    weight_blocks = input_weight.reshape(head_count, block_count, STRETCH)
    signal_blocks = signal.reshape(block_count, STRETCH, head_count, HEAD_DIM)
    write_blocks = write_proj.reshape(block_count, STRETCH, STATE)
    read_blocks = read_proj.reshape(block_count, STRETCH, STATE)
    scores = jnp.einsum(
        "cin,cjn->cij", read_blocks, write_blocks, preferred_element_type=jnp.float32
    )
    lower_mask = jnp.arange(STRETCH)[:, None] >= jnp.arange(STRETCH)[None, :]
    span_logs = jnp.where(
        lower_mask[None, None], running[:, :, :, None] - running[:, :, None, :], -1e30
    )
    mixing = (jnp.exp(span_logs) * scores[None] * weight_blocks[:, :, None, :]).astype(jnp.bfloat16)
    local_out = jnp.einsum(
        "hcij,cjhp->cihp", mixing, signal_blocks, preferred_element_type=jnp.float32
    )
    tail_weight = jnp.exp(running[:, :, -1:] - running) * weight_blocks
    scaled = (
        signal_blocks.astype(jnp.float32) * jnp.transpose(tail_weight, (1, 2, 0))[:, :, :, None]
    ).astype(jnp.bfloat16)
    block_states = jnp.einsum(
        "cjhp,cjn->chpn", scaled, write_blocks, preferred_element_type=jnp.float32
    )
    block_decay = running[:, :, -1].T
    zero_state = jnp.zeros((head_count, HEAD_DIM, STATE), jnp.float32)
    zero_log = jnp.zeros((head_count,), jnp.float32)
    identity = (zero_log, zero_state)
    device_pair, segment_cumulative = lax.scan(local_step, identity, (block_decay, block_states))
    all_logs = lax.all_gather(device_pair[0][None], ("scan", "band"), axis=0, tiled=True)
    inclusive = lax.associative_scan(jnp.add, all_logs, axis=0)
    exclusive = inclusive - all_logs
    position = lax.axis_index(("scan", "band"))
    own_exclusive = lax.dynamic_index_in_dim(exclusive, position, 0, keepdims=False)
    shard_block = lax.all_gather(
        device_pair[1][None].astype(jnp.bfloat16), ("scan", "band"), axis=0, tiled=True
    ).astype(jnp.float32)
    how_many = shard_block.shape[0]
    sources = jnp.arange(how_many, dtype=jnp.int32)
    gap_logs = jnp.where((sources < position)[:, None], own_exclusive[None, :] - inclusive, -1e30)
    carry_state = zero_state + jnp.einsum(
        "kh,khpn->hpn", jnp.exp(gap_logs), shard_block, precision=HIGHEST
    )
    enter_state = (
        jnp.exp(segment_cumulative[0])[:, :, None, None] * carry_state[None] + segment_cumulative[1]
    )
    state_high = enter_state.astype(jnp.bfloat16)
    widened = lax.optimization_barrier(state_high).astype(jnp.float32)
    state_low = (enter_state - widened).astype(jnp.bfloat16)
    high_part = jnp.einsum(
        "cin,chpn->cihp", read_blocks, state_high, preferred_element_type=jnp.float32
    )
    low_part = jnp.einsum(
        "cin,chpn->cihp", read_blocks, state_low, preferred_element_type=jnp.float32
    )
    carried_out = jnp.transpose(jnp.exp(running), (1, 2, 0))[:, :, :, None] * (high_part + low_part)
    ssm_out = (local_out + carried_out).reshape(row_count, head_count, HEAD_DIM) + skip_gain[
        None, :, None
    ] * signal.reshape(row_count, head_count, HEAD_DIM).astype(jnp.float32)
    gated_out = ssm_out.reshape(row_count, head_count * HEAD_DIM) * jax.nn.silu(
        gate_branch.astype(jnp.float32)
    )
    square_total = lax.psum(jnp.sum(gated_out * gated_out, axis=1), "tensor")
    normed = (
        gated_out * lax.rsqrt(square_total / INNER + EPSILON)[:, None] * norm_gain[None, :]
    ).astype(jnp.bfloat16)
    own_columns = lax.psum_scatter(
        lax.dot_general(
            out_weight, normed, (((0,), (1,)), ((), ())), preferred_element_type=jnp.float32
        ).astype(jnp.bfloat16),
        "tensor",
        scatter_dimension=0,
        tiled=True,
    ).astype(jnp.float32)
    return own_columns.T.astype(jnp.bfloat16)


LOG2E = 1.4426950408889634
LANES = 128
STATE_PAIRS = 4
HEAD_START = 2
PIECES = 1
PIECE = STATE // PIECES
MIX_PAIRS = 2
GATE_PAIRS = 2
TILE = 256
MESH = pl.DeviceIdType.MESH


def fused_kernel(
    heads,
    span_count,
    signal_hbm,
    gate_hbm,
    write_hbm,
    read_hbm,
    logits_hbm,
    valid_hbm,
    band_hbm,
    offset_hbm,
    decay_hbm,
    bias_hbm,
    skip_hbm,
    gain_hbm,
    weight_hbm,
    out_ref,
    weight_ref,
    signal_ref,
    gate_ref,
    write_ref,
    read_ref,
    logits_ref,
    valid_ref,
    band_ref,
    offset_ref,
    decay_ref,
    bias_ref,
    skip_ref,
    gain_ref,
    padded_ref,
    params_ref,
    row_ref,
    run_ref,
    lead_ref,
    row_log_ref,
    skip_rows_ref,
    scores_ref,
    read_by_token_ref,
    state_ref,
    totals_ref,
    core_totals_ref,
    local_ref,
    normed_ref,
    square_ref,
    carry_ref,
    pass_ref,
    core_state_ref,
    entry_ref,
    sent_ref,
    own_ref,
    parts_ref,
    landed_ref,
    square_out_ref,
    square_in_ref,
    load_sem,
    small_sem,
    totals_send,
    totals_recv,
    core_send,
    core_recv,
    onward_send,
    arrival,
    tile_send,
    tile_recv,
    square_send,
    square_recv,
):
    pair_count = heads // 2
    scan_index = lax.axis_index("scan")
    band_index = lax.axis_index("band")
    tensor_index = lax.axis_index("tensor")
    first_core = band_index == 0
    second_core = band_index == 1
    first_chip = scan_index == 0
    has_previous = second_core & (scan_index > 0)
    has_next = second_core & (scan_index < span_count - 1)
    gets_entry = first_core & (scan_index > 0)
    peer = 1 - tensor_index
    other_core = {"band": 1 - band_index}
    following = {"scan": lax.rem(scan_index + 1, span_count)}
    previous = {"scan": lax.rem(scan_index + span_count - 1, span_count)}

    signal_load = pltpu.make_async_copy(signal_hbm, signal_ref, load_sem.at[2])
    gate_load = pltpu.make_async_copy(gate_hbm, gate_ref, load_sem.at[0])
    weight_load = pltpu.make_async_copy(weight_hbm, weight_ref, load_sem.at[1])
    small_loads = [
        pltpu.make_async_copy(source, target, small_sem.at[spot])
        for spot, (source, target) in enumerate(
            (
                (logits_hbm, logits_ref),
                (band_hbm, band_ref),
                (offset_hbm, offset_ref),
                (decay_hbm, decay_ref),
                (bias_hbm, bias_ref),
                (valid_hbm, valid_ref),
                (skip_hbm, skip_ref),
                (write_hbm, write_ref),
                (read_hbm, read_ref),
                (gain_hbm, gain_ref),
            )
        )
    ]
    for load in small_loads:
        load.start()
    signal_load.start()

    barrier = pltpu.get_barrier_semaphore()
    for target in (other_core, {"tensor": peer}):
        pl.semaphore_signal(barrier, inc=1, device_id=target, device_id_type=MESH)

    @pl.when(has_next)
    def _():
        pl.semaphore_signal(barrier, inc=1, device_id=following, device_id_type=MESH)

    @pl.when(has_previous)
    def _():
        pl.semaphore_signal(barrier, inc=1, device_id=previous, device_id_type=MESH)

    for load in small_loads:
        load.wait()

    params_ref[...] = jnp.zeros_like(params_ref)
    chosen = lax.broadcasted_iota(jnp.int32, (BANDS, heads), 0) == band_ref[...]
    params_ref[0:1, 0:heads] = bias_ref[...] + jnp.sum(
        jnp.where(chosen, offset_ref[...], 0.0), axis=0, keepdims=True
    )
    params_ref[1:2, 0:heads] = jnp.exp(decay_ref[...]) * -LOG2E
    params_ref[2:3, 0:heads] = skip_ref[...]
    head_columns = params_ref[...].T[0:heads]
    shifted = logits_ref[...] + head_columns[:, 0:1]
    step_size = jnp.maximum(shifted, 0.0) + jnp.log1p(jnp.exp(-jnp.abs(shifted)))
    lanes = lax.broadcasted_iota(jnp.int32, (STRETCH, LANES), 1)
    square_rows = lax.broadcasted_iota(jnp.int32, (STRETCH, STRETCH), 0)
    square_columns = lax.broadcasted_iota(jnp.int32, (STRETCH, STRETCH), 1)
    high = step_size.astype(jnp.bfloat16).astype(jnp.float32)
    middle = (step_size - high).astype(jnp.bfloat16).astype(jnp.float32)
    low = step_size - high - middle
    unused = jnp.zeros((LANES - 3 * heads, STRETCH), jnp.float32)
    sums = jnp.dot(
        jnp.concatenate([high, middle, low, unused], axis=0).astype(jnp.bfloat16),
        jnp.where(square_rows <= square_columns, 1.0, 0.0).astype(jnp.bfloat16),
        preferred_element_type=jnp.float32,
    )
    summed = sums[0:heads] + sums[heads : 2 * heads] + sums[2 * heads : 3 * heads]
    running = summed * head_columns[:, 1:2]
    in_weight = step_size * valid_ref[...].astype(jnp.float32)
    tail = jnp.exp2(running[:, STRETCH - 1 : STRETCH] - running) * in_weight
    row_ref[...] = running
    row_log_ref[...] = in_weight
    padded_ref[...] = jnp.zeros_like(padded_ref)
    padded_ref[0:heads, :] = tail
    padded_ref[HEAD_DIM : HEAD_DIM + heads, :] = running
    factors = padded_ref[...].T
    run_ref[...] = factors

    def three_parts(value):
        high = value.astype(jnp.bfloat16).astype(jnp.float32)
        rest = value - high
        middle = rest.astype(jnp.bfloat16).astype(jnp.float32)
        low = rest - middle
        packed = high + pltpu.roll(middle, heads, 1) + pltpu.roll(low, 2 * heads, 1)
        return packed.astype(jnp.bfloat16)

    last_running = pltpu.roll(factors[STRETCH - 16 : STRETCH], LANES - HEAD_DIM, 1)
    running_parts = three_parts(jnp.where(lanes[0:16] < heads, last_running, 0.0))
    part = lax.broadcasted_iota(jnp.int32, (LANES, 2 * LANES), 0)
    part = (
        part
        - jnp.where(part >= heads, heads, 0)
        - jnp.where(part >= 2 * heads, heads, 0)
    )
    head_of = lax.broadcasted_iota(jnp.int32, totals_ref.shape, 1)
    head_of = (
        head_of
        - jnp.where(head_of >= heads, heads, 0)
        - jnp.where(head_of >= 2 * heads, heads, 0)
    )
    own_pair = head_of // 2 == lax.broadcasted_iota(jnp.int32, totals_ref.shape, 0)
    last_parts = running_parts.astype(jnp.float32)[15:16, :]
    last_rows = (
        jnp.dot(
            jnp.where(own_pair, last_parts, 0.0).astype(jnp.bfloat16),
            jnp.where(
                part[:, 0:LANES] % 2
                == lax.broadcasted_iota(jnp.int32, (LANES, LANES), 1) // HEAD_DIM,
                1.0,
                0.0,
            ).astype(jnp.bfloat16),
            preferred_element_type=jnp.float32,
        )
    )
    totals_ref[...] = jnp.exp2(last_rows)
    write_turned = write_ref[...].astype(jnp.float32).T.astype(jnp.bfloat16)
    read_by_token_ref[...] = write_turned

    totals_copy = pltpu.make_async_remote_copy(
        src_ref=totals_ref,
        dst_ref=core_totals_ref,
        send_sem=totals_send,
        recv_sem=totals_recv,
        device_id=other_core,
        device_id_type=MESH,
    )

    def core_copy(start, count, group):
        members = pl.ds(start, count)
        return pltpu.make_async_remote_copy(
            src_ref=pass_ref.at[members],
            dst_ref=core_state_ref.at[members],
            send_sem=core_send,
            recv_sem=core_recv.at[group],
            device_id=other_core,
            device_id_type=MESH,
        )

    def onward_copy(pair, piece):
        rows = pl.ds(piece * PIECE, PIECE)
        return pltpu.make_async_remote_copy(
            src_ref=pass_ref.at[pair, rows],
            dst_ref=entry_ref.at[pair, rows],
            send_sem=onward_send,
            recv_sem=arrival.at[pair * PIECES + piece],
            device_id=following,
            device_id_type=MESH,
        )

    def entry_copy(pair):
        return pltpu.make_async_remote_copy(
            src_ref=entry_ref.at[pair],
            dst_ref=carry_ref.at[pair],
            send_sem=core_send,
            recv_sem=arrival.at[pair * PIECES],
            device_id=other_core,
            device_id_type=MESH,
        )

    def give_onward(pair, piece, carry):
        rows = slice(piece * PIECE, (piece + 1) * PIECE)
        onward = totals_ref[pl.ds(pair, 1), :] * carry + state_ref[pair, rows]
        pass_ref[pair, rows] = onward.astype(jnp.bfloat16)
        onward_copy(pair, piece).start()

    def first_chain_step(pair):
        own = core_state_ref[pair]
        carry_ref[pair] = own

        @pl.when(has_next)
        def _():
            for piece in range(PIECES):
                rows = slice(piece * PIECE, (piece + 1) * PIECE)
                give_onward(pair, piece, own[rows].astype(jnp.float32))

    def chain_step(pair):
        for piece in range(PIECES):
            rows = slice(piece * PIECE, (piece + 1) * PIECE)
            onward_copy(pair, piece).wait_recv()
            if piece == PIECES - 1:

                @pl.when(jnp.logical_not(has_next))
                def _():
                    entry_copy(pair).start()

            carry = core_totals_ref[pl.ds(pair, 1), :] * entry_ref[pair, rows].astype(
                jnp.float32
            ) + core_state_ref[pair, rows].astype(jnp.float32)
            carry_ref[pair, rows] = carry.astype(jnp.bfloat16)

            @pl.when(has_next)
            def _():
                give_onward(pair, piece, carry)
                if piece == PIECES - 1:
                    entry_copy(pair).start()

    def columns_of(pair):
        return pl.ds(pl.multiple_of(pair * LANES, LANES), LANES)

    narrow_side = lax.broadcasted_iota(jnp.int32, (LANES, LANES), 1) // HEAD_DIM
    narrow_index = part[:, 0:LANES] - narrow_side
    first_half = lanes < HEAD_DIM
    second_half = lanes >= HEAD_DIM

    def picker(index, pair):
        return jnp.where(index == 2 * pair, 1.0, 0.0).astype(jnp.bfloat16)

    def spread(values, index):
        return jnp.take_along_axis(values, index, axis=1, mode="promise_in_bounds")

    def pair_heads(pair):
        return 2 * pair + lanes // HEAD_DIM

    def state_pair(pair):
        columns = columns_of(pair)
        tail = spread(run_ref[...], pair_heads(pair))
        scaled = (signal_ref[:, columns].astype(jnp.float32) * tail).astype(jnp.bfloat16)
        state = jnp.dot(read_by_token_ref[...], scaled, preferred_element_type=jnp.float32)
        state_ref[pair] = state
        pass_ref[pair] = state.astype(jnp.bfloat16)


    def mix_pair(pair):
        columns = columns_of(pair)
        half = STRETCH // 2
        fed = signal_ref[:, columns]
        tops, bottoms, sides = [], [], []
        for side in range(2):
            row = row_ref[pl.ds(2 * pair + side, 1), :]
            most = row_log_ref[pl.ds(2 * pair + side, 1), :]
            run = spread(run_ref[...], jnp.full((STRETCH, LANES), HEAD_DIM + 2 * pair + side, jnp.int32))
            near = jnp.exp2(jnp.minimum(run[0:half] - row[:, 0:half], most[:, 0:half]))
            far = jnp.exp2(run[half:] - row[:, 0:half])
            late = jnp.exp2(jnp.minimum(run[half:] - row[:, half:], most[:, half:]))
            tops.append((near * scores_ref[0:half, 0:half]).astype(jnp.bfloat16))
            bottoms.append((far * scores_ref[half:, 0:half]).astype(jnp.bfloat16))
            bottoms.append((late * scores_ref[half:, half:]).astype(jnp.bfloat16))
            sides.append(jnp.where(first_half if side == 0 else second_half, fed, jnp.zeros_like(fed)))
        local_ref[0:half, columns] = jnp.dot(
            jnp.concatenate(tops, axis=1),
            jnp.concatenate([sides[0][0:half], sides[1][0:half]], axis=0),
            preferred_element_type=jnp.float32,
        )
        local_ref[half:, columns] = jnp.dot(
            jnp.concatenate(bottoms, axis=1),
            jnp.concatenate(sides, axis=0),
            preferred_element_type=jnp.float32,
        )

    def gate_parts(pair):
        columns = columns_of(pair)
        skip = jnp.dot(
            skip_rows_ref[...], picker(narrow_index, pair), preferred_element_type=jnp.float32
        )
        own = local_ref[:, columns] + skip[0:1, :] * signal_ref[:, columns].astype(jnp.float32)
        gate = gate_ref[:, columns].astype(jnp.float32)
        lead = spread(lead_ref[...], HEAD_DIM + pair_heads(pair))
        return own, lead, gate / (1.0 + jnp.exp(-gate))

    def gate_pair(pair, own, lead, gate):
        carried = jnp.dot(read_ref[...], carry_ref[pair], preferred_element_type=jnp.float32)
        gated = (own + lead * carried) * gate
        normed_ref[:, columns_of(pair)] = (gated * gain_ref[pl.ds(pair, 1), :]).astype(
            jnp.bfloat16
        )
        return gated * gated

    def state_pairs(start, count):
        for member in range(count):
            state_pair(start + member)

    def core_copies(start, count, group):
        @pl.when(first_core)
        def _():
            core_copy(start, count, group).start()

    def first_chain_steps(start, count, group):
        core_copy(start, count, group).wait_recv()
        for member in range(count):
            first_chain_step(start + member)

    group_count = pair_count // STATE_PAIRS
    signal_load.wait()
    state_pairs(0, HEAD_START)
    pl.semaphore_wait(barrier, 2 + jnp.where(has_next, 1, 0) + jnp.where(has_previous, 1, 0))
    core_copies(0, HEAD_START, 0)

    @pl.when(first_core)
    def _():
        totals_copy.start()

    gate_load.start()
    weight_load.start()
    state_pairs(HEAD_START, STATE_PAIRS - HEAD_START)
    core_copies(HEAD_START, STATE_PAIRS - HEAD_START, 1)

    @pl.when(second_core & first_chip)
    def _():
        first_chain_steps(0, HEAD_START, 0)

    @pl.loop(1, group_count)
    def _(group):
        start = group * STATE_PAIRS
        state_pairs(start, STATE_PAIRS)
        core_copies(start, STATE_PAIRS, group + 1)

        @pl.when(second_core & first_chip & (group == 1))
        def _():
            first_chain_steps(HEAD_START, STATE_PAIRS - HEAD_START, 1)

        @pl.when(second_core & first_chip & (group > 1))
        def _():
            first_chain_steps(start - STATE_PAIRS, STATE_PAIRS, group)

    @pl.when(second_core & first_chip)
    def _():
        first_chain_steps(pair_count - STATE_PAIRS, STATE_PAIRS, group_count)

    @pl.when(second_core)
    def _():
        totals_copy.wait_recv()

    skip_rows_ref[...] = three_parts(jnp.broadcast_to(params_ref[2:3, :], (16, LANES)))
    lead_ref[...] = jnp.exp2(run_ref[...])
    in_weights = row_log_ref[...]
    weight_log = jnp.where(in_weights > 0.0, jnp.log(in_weights) * LOG2E, -1e30)
    row_log_ref[...] = weight_log
    row_ref[...] = row_ref[...] - weight_log
    scores = jnp.dot(read_ref[...], read_by_token_ref[...], preferred_element_type=jnp.float32)
    scores_ref[...] = jnp.where(square_columns <= square_rows, scores, 0.0)
    square_ref[...] = jnp.zeros_like(square_ref)
    @pl.when(first_core & first_chip)
    def _():
        carry_ref[...] = jnp.zeros_like(carry_ref)

    @pl.loop(0, pair_count // MIX_PAIRS)
    def _(group):
        @pl.when(has_previous & has_next)
        def _():
            @pl.when(group == 0)
            def _():
                core_copy(0, HEAD_START, 0).wait_recv()

            @pl.when(group == 1)
            def _():
                core_copy(HEAD_START, STATE_PAIRS - HEAD_START, 1).wait_recv()

            @pl.when((group > 1) & (group % 2 == 0))
            def _():
                core_copy(group * MIX_PAIRS, STATE_PAIRS, group // 2 + 1).wait_recv()

            for member in range(MIX_PAIRS):
                chain_step(group * MIX_PAIRS + member)

        for member in range(MIX_PAIRS):
            mix_pair(group * MIX_PAIRS + member)

    gate_load.wait()
    last_step = has_previous & (scan_index == span_count - 1)

    @pl.when(last_step)
    def _():
        core_copy(0, HEAD_START, 0).wait_recv()
        core_copy(HEAD_START, STATE_PAIRS - HEAD_START, 1).wait_recv()

        @pl.loop(1, group_count)
        def _(group):
            core_copy(group * STATE_PAIRS, STATE_PAIRS, group + 1).wait_recv()

    def await_carry(start, count):
        @pl.when(last_step)
        def _():
            for member in range(count):
                chain_step(start + member)

        @pl.when(gets_entry)
        def _():
            for member in range(count):
                entry_copy(start + member).wait_recv()

    @pl.loop(0, pair_count // GATE_PAIRS - 1)
    def _(group):
        start = group * GATE_PAIRS
        await_carry(start, GATE_PAIRS)
        squares = square_ref[...]
        for member in range(GATE_PAIRS):
            squares = squares + gate_pair(start + member, *gate_parts(start + member))
        square_ref[...] = squares

    weight_load.wait()
    own_width = out_ref.shape[1]
    tile_count = own_width // TILE

    def tile_copy(tile):
        return pltpu.make_async_remote_copy(
            src_ref=sent_ref.at[tile],
            dst_ref=landed_ref.at[tile],
            send_sem=tile_send,
            recv_sem=tile_recv.at[tile],
            device_id={"tensor": peer},
            device_id_type=MESH,
        )

    def project(owner, tile, first=0, last=pair_count):
        start = pl.multiple_of(owner * own_width + tile * TILE, LANES)
        rows = slice(first * LANES, last * LANES)
        return jnp.dot(
            normed_ref[:, rows],
            weight_ref[rows, pl.ds(start, TILE)],
            preferred_element_type=jnp.float32,
        )

    early = pair_count - GATE_PAIRS
    for spot in range(GATE_PAIRS):
        for kind, value in enumerate(gate_parts(early + spot)):
            parts_ref[spot, kind] = value
    own_ref[0] = project(peer, 0, 0, early)
    for spot in range(GATE_PAIRS):
        pair = early + spot
        await_carry(pair, 1)
        square_ref[...] += gate_pair(
            pair, parts_ref[spot, 0], parts_ref[spot, 1], parts_ref[spot, 2]
        )
        if spot < GATE_PAIRS - 1:
            own_ref[0] += project(peer, 0, pair, pair + 1)
    sent_ref[0] = (own_ref[0] + project(peer, 0, pair_count - 1)).astype(jnp.bfloat16)
    tile_copy(0).start()
    square_sum = jnp.sum(square_ref[...].T, axis=0, keepdims=True)
    square_out_ref[...] = jnp.broadcast_to(square_sum, square_out_ref.shape)
    square_copy = pltpu.make_async_remote_copy(
        src_ref=square_out_ref,
        dst_ref=square_in_ref,
        send_sem=square_send,
        recv_sem=square_recv,
        device_id={"tensor": peer},
        device_id_type=MESH,
    )
    square_copy.start()

    @pl.loop(1, tile_count)
    def _(tile):
        sent_ref[tile] = project(peer, tile).astype(jnp.bfloat16)
        tile_copy(tile).start()

    @pl.loop(0, tile_count)
    def _(tile):
        own_ref[tile] = project(tensor_index, tile)

    @pl.when(first_core)
    def _():
        totals_copy.wait_send()

    @pl.when(first_core | has_previous)
    def _():
        pltpu.make_async_copy(pass_ref, pass_ref, core_send).wait()

    @pl.when(has_next)
    def _():
        pltpu.make_async_copy(pass_ref, pass_ref, onward_send).wait()

    square_copy.wait()
    inner = 2 * heads * HEAD_DIM
    scale = lax.rsqrt((square_out_ref[0:1, :] + square_in_ref[0:1, :]) / inner + EPSILON)
    square_ref[...] = jnp.broadcast_to(scale, (LANES, STRETCH)).T

    @pl.loop(0, tile_count)
    def _(tile):
        tile_copy(tile).wait_recv()
        scales = square_ref[...]
        for side in range(TILE // LANES):
            start = pl.multiple_of(tile * TILE + side * LANES, LANES)
            columns = slice(side * LANES, (side + 1) * LANES)
            both = own_ref[tile, :, columns] + landed_ref[tile, :, columns].astype(jnp.float32)
            out_ref[:, pl.ds(start, LANES)] = (both * scales).astype(jnp.bfloat16)

    pltpu.make_async_copy(sent_ref, sent_ref, tile_send).wait()


def fused_on_device(
    span_count,
    signal,
    gate_branch,
    write_proj,
    read_proj,
    step_logits,
    valid_mask,
    stretch_band,
    band_offset,
    decay_log,
    step_offset,
    skip_gain,
    norm_gain,
    out_weight,
):
    heads = decay_log.shape[0]
    inner = heads * HEAD_DIM
    width = out_weight.shape[1]
    pair_count = heads // 2
    tile_count = width // 2 // TILE
    vmem = pl.BlockSpec(memory_space=pltpu.VMEM)
    hbm = pl.BlockSpec(memory_space=pl.ANY)
    f32, bf16 = jnp.float32, jnp.bfloat16
    return pl.pallas_call(
        functools.partial(fused_kernel, heads, span_count),
        out_shape=pltpu.VMEM((STRETCH, width // 2), bf16),
        in_specs=[hbm] * 13,
        out_specs=vmem,
        scratch_shapes=[
            pltpu.VMEM((inner, width), bf16),
            pltpu.VMEM((STRETCH, inner), bf16),
            pltpu.VMEM((STRETCH, inner), bf16),
            pltpu.VMEM((STRETCH, STATE), bf16),
            pltpu.VMEM((STRETCH, STATE), bf16),
            pltpu.VMEM((heads, STRETCH), f32),
            pltpu.VMEM((1, STRETCH), jnp.int32),
            pltpu.VMEM((1, 1), jnp.int32),
            pltpu.VMEM((BANDS, heads), f32),
            pltpu.VMEM((1, heads), f32),
            pltpu.VMEM((1, heads), f32),
            pltpu.VMEM((1, heads), f32),
            pltpu.VMEM((pair_count, LANES), f32),
            pltpu.VMEM((LANES, STRETCH), f32),
            pltpu.VMEM((8, LANES), f32),
            pltpu.VMEM((heads, STRETCH), f32),
            pltpu.VMEM((STRETCH, LANES), f32),
            pltpu.VMEM((STRETCH, LANES), f32),
            pltpu.VMEM((heads, STRETCH), f32),
            pltpu.VMEM((16, LANES), bf16),
            pltpu.VMEM((STRETCH, STRETCH), f32),
            pltpu.VMEM((STATE, STRETCH), bf16),
            pltpu.VMEM((pair_count, STATE, LANES), f32),
            pltpu.VMEM((-(-pair_count // 16) * 16, LANES), f32),
            pltpu.VMEM((-(-pair_count // 16) * 16, LANES), f32),
            pltpu.VMEM((STRETCH, inner), f32),
            pltpu.VMEM((STRETCH, inner), bf16),
            pltpu.VMEM((STRETCH, LANES), f32),
            pltpu.VMEM((pair_count, STATE, LANES), bf16),
            pltpu.VMEM((pair_count, STATE, LANES), bf16),
            pltpu.VMEM((pair_count, STATE, LANES), bf16),
            pltpu.VMEM((pair_count, STATE, LANES), bf16),
            pltpu.VMEM((tile_count, STRETCH, TILE), bf16),
            pltpu.VMEM((tile_count, STRETCH, TILE), f32),
            pltpu.VMEM((GATE_PAIRS, 3, STRETCH, LANES), f32),
            pltpu.VMEM((tile_count, STRETCH, TILE), bf16),
            pltpu.VMEM((8, STRETCH), f32),
            pltpu.VMEM((8, STRETCH), f32),
            pltpu.SemaphoreType.DMA((3,)),
            pltpu.SemaphoreType.DMA((10,)),
            pltpu.SemaphoreType.DMA,
            pltpu.SemaphoreType.DMA,
            pltpu.SemaphoreType.DMA,
            pltpu.SemaphoreType.DMA((pair_count // STATE_PAIRS + 1,)),
            pltpu.SemaphoreType.DMA,
            pltpu.SemaphoreType.DMA((pair_count * PIECES,)),
            pltpu.SemaphoreType.DMA,
            pltpu.SemaphoreType.DMA((tile_count,)),
            pltpu.SemaphoreType.DMA,
            pltpu.SemaphoreType.DMA,
        ],
        compiler_params=pltpu.CompilerParams(
            collective_id=0, has_side_effects=True, vmem_limit_bytes=60 * 1024 * 1024
        ),
    )(
        signal,
        gate_branch,
        write_proj,
        read_proj,
        step_logits,
        valid_mask[None, :],
        stretch_band[None, :],
        band_offset,
        decay_log[None, :],
        step_offset[None, :],
        skip_gain[None, :],
        norm_gain.reshape(pair_count, LANES),
        out_weight,
    )


def solution(mesh):
    placed = (
        P(("group", "scan", "band"), "tensor"),
        P(("group", "scan", "band"), "tensor"),
        P(("group", "scan", "band"), None),
        P(("group", "scan", "band"), None),
        P("tensor", ("group", "scan", "band")),
        P(("group", "scan", "band")),
        P(("group", "scan", "band")),
        P(None, "tensor"),
        P("tensor"),
        P("tensor"),
        P("tensor"),
        P("tensor"),
        P("tensor", None),
    )
    shape = dict(mesh.shape)
    places = shape["scan"] * shape["band"]

    def layer(*arrays):
        rows = arrays[0].shape[0] // (shape["group"] * places)
        heads = arrays[8].shape[0] // shape["tensor"]
        width = arrays[12].shape[1]
        fits = (
            shape["tensor"] == 2
            and shape["band"] == 2
            and shape["scan"] >= 2
            and rows == STRETCH
            and heads % (2 * STATE_PAIRS) == 0
            and heads % (2 * MIX_PAIRS) == 0
            and heads % (2 * GATE_PAIRS) == 0
            and 3 * heads < LANES
            and heads <= HEAD_DIM
            and width % (2 * TILE) == 0
        )
        member = on_device
        if fits:
            member = functools.partial(fused_on_device, shape["scan"])
        return mapped(member)(*arrays)

    def mapped(member):
        return jax.shard_map(
            member,
            mesh=mesh,
            in_specs=placed,
            out_specs=P(("group", "scan", "band"), "tensor"),
            check_vma=False,
        )

    return layer
```

```python
import functools

import jax
import jax.numpy as jnp
from jax import lax
from jax.experimental import pallas as pl
from jax.experimental.pallas import tpu as pltpu
from jax.sharding import PartitionSpec as P

HEAD_DIM = 64
STATE = 128
STRETCH = 256
BANDS = 12
INNER = 5120


EPSILON = 1e-05
HIGHEST = lax.Precision.HIGHEST


def step_sizes(step_logits, stretch_band, band_offset, step_offset):
    one_hot = (stretch_band[:, None] == jnp.arange(BANDS, dtype=jnp.int32)[None, :]).astype(
        jnp.float32
    )
    stretch_offset = jnp.dot(one_hot, band_offset, precision=HIGHEST)
    token_offset = jnp.repeat(stretch_offset, STRETCH, axis=0).T
    return jax.nn.softplus(step_logits + step_offset[:, None] + token_offset)


def combine(earlier, later_pair):
    return (
        earlier[0] + later_pair[0],
        jnp.exp(later_pair[0])[:, None, None] * earlier[1] + later_pair[1],
    )


def local_step(running_pair, member):
    return (combine(running_pair, member), running_pair)


def on_device(
    signal,
    gate_branch,
    write_proj,
    read_proj,
    step_logits,
    valid_mask,
    stretch_band,
    band_offset,
    decay_log,
    step_offset,
    skip_gain,
    norm_gain,
    out_weight,
):
    row_count = signal.shape[0]
    head_count = decay_log.shape[0]
    block_count = row_count // STRETCH
    step_size = step_sizes(step_logits, stretch_band, band_offset, step_offset)
    log_decay = step_size * (-jnp.exp(decay_log))[:, None]
    input_weight = step_size * valid_mask.astype(jnp.float32)[None, :]
    running = lax.associative_scan(
        jnp.add, log_decay.reshape(head_count, block_count, STRETCH), axis=2
    )
    weight_blocks = input_weight.reshape(head_count, block_count, STRETCH)
    signal_blocks = signal.reshape(block_count, STRETCH, head_count, HEAD_DIM)
    write_blocks = write_proj.reshape(block_count, STRETCH, STATE)
    read_blocks = read_proj.reshape(block_count, STRETCH, STATE)
    scores = jnp.einsum(
        "cin,cjn->cij", read_blocks, write_blocks, preferred_element_type=jnp.float32
    )
    lower_mask = jnp.arange(STRETCH)[:, None] >= jnp.arange(STRETCH)[None, :]
    span_logs = jnp.where(
        lower_mask[None, None], running[:, :, :, None] - running[:, :, None, :], -1e30
    )
    mixing = (jnp.exp(span_logs) * scores[None] * weight_blocks[:, :, None, :]).astype(jnp.bfloat16)
    local_out = jnp.einsum(
        "hcij,cjhp->cihp", mixing, signal_blocks, preferred_element_type=jnp.float32
    )
    tail_weight = jnp.exp(running[:, :, -1:] - running) * weight_blocks
    scaled = (
        signal_blocks.astype(jnp.float32) * jnp.transpose(tail_weight, (1, 2, 0))[:, :, :, None]
    ).astype(jnp.bfloat16)
    block_states = jnp.einsum(
        "cjhp,cjn->chpn", scaled, write_blocks, preferred_element_type=jnp.float32
    )
    block_decay = running[:, :, -1].T
    zero_state = jnp.zeros((head_count, HEAD_DIM, STATE), jnp.float32)
    zero_log = jnp.zeros((head_count,), jnp.float32)
    identity = (zero_log, zero_state)
    device_pair, segment_cumulative = lax.scan(local_step, identity, (block_decay, block_states))
    all_logs = lax.all_gather(device_pair[0][None], ("scan", "band"), axis=0, tiled=True)
    inclusive = lax.associative_scan(jnp.add, all_logs, axis=0)
    exclusive = inclusive - all_logs
    position = lax.axis_index(("scan", "band"))
    own_exclusive = lax.dynamic_index_in_dim(exclusive, position, 0, keepdims=False)
    shard_block = lax.all_gather(
        device_pair[1][None].astype(jnp.bfloat16), ("scan", "band"), axis=0, tiled=True
    ).astype(jnp.float32)
    how_many = shard_block.shape[0]
    sources = jnp.arange(how_many, dtype=jnp.int32)
    gap_logs = jnp.where((sources < position)[:, None], own_exclusive[None, :] - inclusive, -1e30)
    carry_state = zero_state + jnp.einsum(
        "kh,khpn->hpn", jnp.exp(gap_logs), shard_block, precision=HIGHEST
    )
    enter_state = (
        jnp.exp(segment_cumulative[0])[:, :, None, None] * carry_state[None] + segment_cumulative[1]
    )
    state_high = enter_state.astype(jnp.bfloat16)
    widened = lax.optimization_barrier(state_high).astype(jnp.float32)
    state_low = (enter_state - widened).astype(jnp.bfloat16)
    high_part = jnp.einsum(
        "cin,chpn->cihp", read_blocks, state_high, preferred_element_type=jnp.float32
    )
    low_part = jnp.einsum(
        "cin,chpn->cihp", read_blocks, state_low, preferred_element_type=jnp.float32
    )
    carried_out = jnp.transpose(jnp.exp(running), (1, 2, 0))[:, :, :, None] * (high_part + low_part)
    ssm_out = (local_out + carried_out).reshape(row_count, head_count, HEAD_DIM) + skip_gain[
        None, :, None
    ] * signal.reshape(row_count, head_count, HEAD_DIM).astype(jnp.float32)
    gated_out = ssm_out.reshape(row_count, head_count * HEAD_DIM) * jax.nn.silu(
        gate_branch.astype(jnp.float32)
    )
    square_total = lax.psum(jnp.sum(gated_out * gated_out, axis=1), "tensor")
    normed = (
        gated_out * lax.rsqrt(square_total / INNER + EPSILON)[:, None] * norm_gain[None, :]
    ).astype(jnp.bfloat16)
    own_columns = lax.psum_scatter(
        lax.dot_general(
            out_weight, normed, (((0,), (1,)), ((), ())), preferred_element_type=jnp.float32
        ).astype(jnp.bfloat16),
        "tensor",
        scatter_dimension=0,
        tiled=True,
    ).astype(jnp.float32)
    return own_columns.T.astype(jnp.bfloat16)


LOG2E = 1.4426950408889634
LANES = 128
STATE_PAIRS = 4
HEAD_START = 2
PIECES = 1
PIECE = STATE // PIECES
MIX_PAIRS = 2
GATE_PAIRS = 2
TILE = 256
MESH = pl.DeviceIdType.MESH


def fused_kernel(
    heads,
    span_count,
    signal_hbm,
    gate_hbm,
    write_hbm,
    read_hbm,
    logits_hbm,
    valid_hbm,
    band_hbm,
    offset_hbm,
    decay_hbm,
    bias_hbm,
    skip_hbm,
    gain_hbm,
    weight_hbm,
    out_ref,
    weight_ref,
    signal_ref,
    gate_ref,
    write_ref,
    read_ref,
    logits_ref,
    valid_ref,
    band_ref,
    offset_ref,
    decay_ref,
    bias_ref,
    skip_ref,
    gain_ref,
    padded_ref,
    params_ref,
    row_ref,
    run_ref,
    lead_ref,
    row_log_ref,
    skip_rows_ref,
    scores_ref,
    read_by_token_ref,
    state_ref,
    totals_ref,
    core_totals_ref,
    local_ref,
    normed_ref,
    square_ref,
    carry_ref,
    pass_ref,
    core_state_ref,
    entry_ref,
    sent_ref,
    own_ref,
    parts_ref,
    landed_ref,
    square_out_ref,
    square_in_ref,
    load_sem,
    small_sem,
    totals_send,
    totals_recv,
    core_send,
    core_recv,
    onward_send,
    arrival,
    tile_send,
    tile_recv,
    square_send,
    square_recv,
):
    pair_count = heads // 2
    scan_index = lax.axis_index("scan")
    band_index = lax.axis_index("band")
    tensor_index = lax.axis_index("tensor")
    first_core = band_index == 0
    second_core = band_index == 1
    first_chip = scan_index == 0
    has_previous = second_core & (scan_index > 0)
    has_next = second_core & (scan_index < span_count - 1)
    gets_entry = first_core & (scan_index > 0)
    peer = 1 - tensor_index
    other_core = {"band": 1 - band_index}
    following = {"scan": lax.rem(scan_index + 1, span_count)}
    previous = {"scan": lax.rem(scan_index + span_count - 1, span_count)}

    signal_load = pltpu.make_async_copy(signal_hbm, signal_ref, load_sem.at[2])
    gate_load = pltpu.make_async_copy(gate_hbm, gate_ref, load_sem.at[0])
    weight_load = pltpu.make_async_copy(weight_hbm, weight_ref, load_sem.at[1])
    small_loads = [
        pltpu.make_async_copy(source, target, small_sem.at[spot])
        for spot, (source, target) in enumerate(
            (
                (logits_hbm, logits_ref),
                (band_hbm, band_ref),
                (offset_hbm, offset_ref),
                (decay_hbm, decay_ref),
                (bias_hbm, bias_ref),
                (valid_hbm, valid_ref),
                (skip_hbm, skip_ref),
                (write_hbm, write_ref),
                (read_hbm, read_ref),
                (gain_hbm, gain_ref),
            )
        )
    ]
    for load in small_loads:
        load.start()
    signal_load.start()

    barrier = pltpu.get_barrier_semaphore()
    for target in (other_core, {"tensor": peer}):
        pl.semaphore_signal(barrier, inc=1, device_id=target, device_id_type=MESH)

    @pl.when(has_next)
    def _():
        pl.semaphore_signal(barrier, inc=1, device_id=following, device_id_type=MESH)

    @pl.when(has_previous)
    def _():
        pl.semaphore_signal(barrier, inc=1, device_id=previous, device_id_type=MESH)

    for load in small_loads[:7]:
        load.wait()

    params_ref[...] = jnp.zeros_like(params_ref)
    chosen = lax.broadcasted_iota(jnp.int32, (BANDS, heads), 0) == band_ref[...]
    params_ref[0:1, 0:heads] = bias_ref[...] + jnp.sum(
        jnp.where(chosen, offset_ref[...], 0.0), axis=0, keepdims=True
    )
    params_ref[1:2, 0:heads] = jnp.exp(decay_ref[...]) * -LOG2E
    params_ref[2:3, 0:heads] = skip_ref[...]
    head_columns = params_ref[...].T[0:heads]
    shifted = logits_ref[...] + head_columns[:, 0:1]
    step_size = jnp.maximum(shifted, 0.0) + jnp.log1p(jnp.exp(-jnp.abs(shifted)))
    lanes = lax.broadcasted_iota(jnp.int32, (STRETCH, LANES), 1)
    square_rows = lax.broadcasted_iota(jnp.int32, (STRETCH, STRETCH), 0)
    square_columns = lax.broadcasted_iota(jnp.int32, (STRETCH, STRETCH), 1)
    high = step_size.astype(jnp.bfloat16).astype(jnp.float32)
    middle = (step_size - high).astype(jnp.bfloat16).astype(jnp.float32)
    low = step_size - high - middle
    unused = jnp.zeros((LANES - 3 * heads, STRETCH), jnp.float32)
    sums = jnp.dot(
        jnp.concatenate([high, middle, low, unused], axis=0).astype(jnp.bfloat16),
        jnp.where(square_rows <= square_columns, 1.0, 0.0).astype(jnp.bfloat16),
        preferred_element_type=jnp.float32,
    )
    summed = sums[0:heads] + sums[heads : 2 * heads] + sums[2 * heads : 3 * heads]
    running = summed * head_columns[:, 1:2]
    in_weight = step_size * valid_ref[...].astype(jnp.float32)
    tail = jnp.exp2(running[:, STRETCH - 1 : STRETCH] - running) * in_weight
    row_ref[...] = running
    row_log_ref[...] = in_weight
    padded_ref[...] = jnp.zeros_like(padded_ref)
    padded_ref[0:heads, :] = tail
    padded_ref[HEAD_DIM : HEAD_DIM + heads, :] = running
    factors = padded_ref[...].T
    run_ref[...] = factors

    def three_parts(value):
        high = value.astype(jnp.bfloat16).astype(jnp.float32)
        rest = value - high
        middle = rest.astype(jnp.bfloat16).astype(jnp.float32)
        low = rest - middle
        packed = high + pltpu.roll(middle, heads, 1) + pltpu.roll(low, 2 * heads, 1)
        return packed.astype(jnp.bfloat16)

    last_running = pltpu.roll(factors[STRETCH - 16 : STRETCH], LANES - HEAD_DIM, 1)
    running_parts = three_parts(jnp.where(lanes[0:16] < heads, last_running, 0.0))
    part = lax.broadcasted_iota(jnp.int32, (LANES, 2 * LANES), 0)
    part = (
        part
        - jnp.where(part >= heads, heads, 0)
        - jnp.where(part >= 2 * heads, heads, 0)
    )
    head_of = lax.broadcasted_iota(jnp.int32, totals_ref.shape, 1)
    head_of = (
        head_of
        - jnp.where(head_of >= heads, heads, 0)
        - jnp.where(head_of >= 2 * heads, heads, 0)
    )
    own_pair = head_of // 2 == lax.broadcasted_iota(jnp.int32, totals_ref.shape, 0)
    last_parts = running_parts.astype(jnp.float32)[15:16, :]
    last_rows = (
        jnp.dot(
            jnp.where(own_pair, last_parts, 0.0).astype(jnp.bfloat16),
            jnp.where(
                part[:, 0:LANES] % 2
                == lax.broadcasted_iota(jnp.int32, (LANES, LANES), 1) // HEAD_DIM,
                1.0,
                0.0,
            ).astype(jnp.bfloat16),
            preferred_element_type=jnp.float32,
        )
    )
    totals_ref[...] = jnp.exp2(last_rows)
    small_loads[7].wait()
    write_turned = write_ref[...].astype(jnp.float32).T.astype(jnp.bfloat16)
    read_by_token_ref[...] = write_turned

    totals_copy = pltpu.make_async_remote_copy(
        src_ref=totals_ref,
        dst_ref=core_totals_ref,
        send_sem=totals_send,
        recv_sem=totals_recv,
        device_id=other_core,
        device_id_type=MESH,
    )

    def core_copy(start, count, group):
        members = pl.ds(start, count)
        return pltpu.make_async_remote_copy(
            src_ref=pass_ref.at[members],
            dst_ref=core_state_ref.at[members],
            send_sem=core_send,
            recv_sem=core_recv.at[group],
            device_id=other_core,
            device_id_type=MESH,
        )

    def onward_copy(pair, piece):
        rows = pl.ds(piece * PIECE, PIECE)
        return pltpu.make_async_remote_copy(
            src_ref=pass_ref.at[pair, rows],
            dst_ref=entry_ref.at[pair, rows],
            send_sem=onward_send,
            recv_sem=arrival.at[pair * PIECES + piece],
            device_id=following,
            device_id_type=MESH,
        )

    def entry_copy(pair):
        return pltpu.make_async_remote_copy(
            src_ref=entry_ref.at[pair],
            dst_ref=carry_ref.at[pair],
            send_sem=core_send,
            recv_sem=arrival.at[pair * PIECES],
            device_id=other_core,
            device_id_type=MESH,
        )

    def give_onward(pair, piece, carry):
        rows = slice(piece * PIECE, (piece + 1) * PIECE)
        onward = totals_ref[pl.ds(pair, 1), :] * carry + state_ref[pair, rows]
        pass_ref[pair, rows] = onward.astype(jnp.bfloat16)
        onward_copy(pair, piece).start()

    def first_chain_step(pair):
        own = core_state_ref[pair]
        carry_ref[pair] = own

        @pl.when(has_next)
        def _():
            for piece in range(PIECES):
                rows = slice(piece * PIECE, (piece + 1) * PIECE)
                give_onward(pair, piece, own[rows].astype(jnp.float32))

    def chain_step(pair):
        for piece in range(PIECES):
            rows = slice(piece * PIECE, (piece + 1) * PIECE)
            onward_copy(pair, piece).wait_recv()
            if piece == PIECES - 1:

                @pl.when(jnp.logical_not(has_next))
                def _():
                    entry_copy(pair).start()

            carry = core_totals_ref[pl.ds(pair, 1), :] * entry_ref[pair, rows].astype(
                jnp.float32
            ) + core_state_ref[pair, rows].astype(jnp.float32)
            carry_ref[pair, rows] = carry.astype(jnp.bfloat16)

            @pl.when(has_next)
            def _():
                give_onward(pair, piece, carry)
                if piece == PIECES - 1:
                    entry_copy(pair).start()

    def columns_of(pair):
        return pl.ds(pl.multiple_of(pair * LANES, LANES), LANES)

    narrow_side = lax.broadcasted_iota(jnp.int32, (LANES, LANES), 1) // HEAD_DIM
    narrow_index = part[:, 0:LANES] - narrow_side
    first_half = lanes < HEAD_DIM
    second_half = lanes >= HEAD_DIM

    def picker(index, pair):
        return jnp.where(index == 2 * pair, 1.0, 0.0).astype(jnp.bfloat16)

    def spread(values, index):
        return jnp.take_along_axis(values, index, axis=1, mode="promise_in_bounds")

    def pair_heads(pair):
        return 2 * pair + lanes // HEAD_DIM

    def state_pair(pair):
        columns = columns_of(pair)
        tail = spread(run_ref[...], pair_heads(pair))
        scaled = (signal_ref[:, columns].astype(jnp.float32) * tail).astype(jnp.bfloat16)
        state = jnp.dot(read_by_token_ref[...], scaled, preferred_element_type=jnp.float32)
        state_ref[pair] = state
        pass_ref[pair] = state.astype(jnp.bfloat16)


    def mix_pair(pair):
        columns = columns_of(pair)
        half = STRETCH // 2
        fed = signal_ref[:, columns]
        tops, bottoms, sides = [], [], []
        for side in range(2):
            row = row_ref[pl.ds(2 * pair + side, 1), :]
            most = row_log_ref[pl.ds(2 * pair + side, 1), :]
            run = spread(run_ref[...], jnp.full((STRETCH, LANES), HEAD_DIM + 2 * pair + side, jnp.int32))
            near = jnp.exp2(jnp.minimum(run[0:half] - row[:, 0:half], most[:, 0:half]))
            far = jnp.exp2(run[half:] - row[:, 0:half])
            late = jnp.exp2(jnp.minimum(run[half:] - row[:, half:], most[:, half:]))
            tops.append((near * scores_ref[0:half, 0:half]).astype(jnp.bfloat16))
            bottoms.append((far * scores_ref[half:, 0:half]).astype(jnp.bfloat16))
            bottoms.append((late * scores_ref[half:, half:]).astype(jnp.bfloat16))
            sides.append(jnp.where(first_half if side == 0 else second_half, fed, jnp.zeros_like(fed)))
        local_ref[0:half, columns] = jnp.dot(
            jnp.concatenate(tops, axis=1),
            jnp.concatenate([sides[0][0:half], sides[1][0:half]], axis=0),
            preferred_element_type=jnp.float32,
        )
        local_ref[half:, columns] = jnp.dot(
            jnp.concatenate(bottoms, axis=1),
            jnp.concatenate(sides, axis=0),
            preferred_element_type=jnp.float32,
        )

    def gate_parts(pair):
        columns = columns_of(pair)
        skip = jnp.dot(
            skip_rows_ref[...], picker(narrow_index, pair), preferred_element_type=jnp.float32
        )
        own = local_ref[:, columns] + skip[0:1, :] * signal_ref[:, columns].astype(jnp.float32)
        gate = gate_ref[:, columns].astype(jnp.float32)
        lead = spread(lead_ref[...], HEAD_DIM + pair_heads(pair))
        return own, lead, gate / (1.0 + jnp.exp(-gate))

    def gate_pair(pair, own, lead, gate):
        carried = jnp.dot(read_ref[...], carry_ref[pair], preferred_element_type=jnp.float32)
        gated = (own + lead * carried) * gate
        normed_ref[:, columns_of(pair)] = (gated * gain_ref[pl.ds(pair, 1), :]).astype(
            jnp.bfloat16
        )
        return gated * gated

    def state_pairs(start, count):
        for member in range(count):
            state_pair(start + member)

    def core_copies(start, count, group):
        @pl.when(first_core)
        def _():
            core_copy(start, count, group).start()

    def first_chain_steps(start, count, group):
        core_copy(start, count, group).wait_recv()
        for member in range(count):
            first_chain_step(start + member)

    group_count = pair_count // STATE_PAIRS
    signal_load.wait()
    state_pairs(0, HEAD_START)
    pl.semaphore_wait(barrier, 2 + jnp.where(has_next, 1, 0) + jnp.where(has_previous, 1, 0))
    core_copies(0, HEAD_START, 0)

    @pl.when(first_core)
    def _():
        totals_copy.start()

    gate_load.start()
    weight_load.start()
    state_pairs(HEAD_START, STATE_PAIRS - HEAD_START)
    core_copies(HEAD_START, STATE_PAIRS - HEAD_START, 1)

    @pl.when(second_core & first_chip)
    def _():
        first_chain_steps(0, HEAD_START, 0)

    @pl.loop(1, group_count)
    def _(group):
        start = group * STATE_PAIRS
        state_pairs(start, STATE_PAIRS)
        core_copies(start, STATE_PAIRS, group + 1)

        @pl.when(second_core & first_chip & (group == 1))
        def _():
            first_chain_steps(HEAD_START, STATE_PAIRS - HEAD_START, 1)

        @pl.when(second_core & first_chip & (group > 1))
        def _():
            first_chain_steps(start - STATE_PAIRS, STATE_PAIRS, group)

    @pl.when(second_core & first_chip)
    def _():
        first_chain_steps(pair_count - STATE_PAIRS, STATE_PAIRS, group_count)

    @pl.when(second_core)
    def _():
        totals_copy.wait_recv()

    skip_rows_ref[...] = three_parts(jnp.broadcast_to(params_ref[2:3, :], (16, LANES)))
    lead_ref[...] = jnp.exp2(run_ref[...])
    in_weights = row_log_ref[...]
    weight_log = jnp.where(in_weights > 0.0, jnp.log(in_weights) * LOG2E, -1e30)
    row_log_ref[...] = weight_log
    row_ref[...] = row_ref[...] - weight_log
    for load in small_loads[8:]:
        load.wait()
    scores = jnp.dot(read_ref[...], read_by_token_ref[...], preferred_element_type=jnp.float32)
    scores_ref[...] = jnp.where(square_columns <= square_rows, scores, 0.0)
    square_ref[...] = jnp.zeros_like(square_ref)
    @pl.when(first_core & first_chip)
    def _():
        carry_ref[...] = jnp.zeros_like(carry_ref)

    @pl.loop(0, pair_count // MIX_PAIRS)
    def _(group):
        @pl.when(has_previous & has_next)
        def _():
            @pl.when(group == 0)
            def _():
                core_copy(0, HEAD_START, 0).wait_recv()

            @pl.when(group == 1)
            def _():
                core_copy(HEAD_START, STATE_PAIRS - HEAD_START, 1).wait_recv()

            @pl.when((group > 1) & (group % 2 == 0))
            def _():
                core_copy(group * MIX_PAIRS, STATE_PAIRS, group // 2 + 1).wait_recv()

            for member in range(MIX_PAIRS):
                chain_step(group * MIX_PAIRS + member)

        for member in range(MIX_PAIRS):
            mix_pair(group * MIX_PAIRS + member)

    gate_load.wait()
    last_step = has_previous & (scan_index == span_count - 1)

    @pl.when(last_step)
    def _():
        core_copy(0, HEAD_START, 0).wait_recv()
        core_copy(HEAD_START, STATE_PAIRS - HEAD_START, 1).wait_recv()

        @pl.loop(1, group_count)
        def _(group):
            core_copy(group * STATE_PAIRS, STATE_PAIRS, group + 1).wait_recv()

    def await_carry(start, count):
        @pl.when(last_step)
        def _():
            for member in range(count):
                chain_step(start + member)

        @pl.when(gets_entry)
        def _():
            for member in range(count):
                entry_copy(start + member).wait_recv()

    @pl.loop(0, pair_count // GATE_PAIRS - 1)
    def _(group):
        start = group * GATE_PAIRS
        await_carry(start, GATE_PAIRS)
        squares = square_ref[...]
        for member in range(GATE_PAIRS):
            squares = squares + gate_pair(start + member, *gate_parts(start + member))
        square_ref[...] = squares

    weight_load.wait()
    own_width = out_ref.shape[1]
    tile_count = own_width // TILE

    def tile_copy(tile):
        return pltpu.make_async_remote_copy(
            src_ref=sent_ref.at[tile],
            dst_ref=landed_ref.at[tile],
            send_sem=tile_send,
            recv_sem=tile_recv.at[tile],
            device_id={"tensor": peer},
            device_id_type=MESH,
        )

    def project(owner, tile, first=0, last=pair_count):
        start = pl.multiple_of(owner * own_width + tile * TILE, LANES)
        rows = slice(first * LANES, last * LANES)
        return jnp.dot(
            normed_ref[:, rows],
            weight_ref[rows, pl.ds(start, TILE)],
            preferred_element_type=jnp.float32,
        )

    early = pair_count - GATE_PAIRS
    for spot in range(GATE_PAIRS):
        for kind, value in enumerate(gate_parts(early + spot)):
            parts_ref[spot, kind] = value
    own_ref[0] = project(peer, 0, 0, early)
    for spot in range(GATE_PAIRS):
        pair = early + spot
        await_carry(pair, 1)
        square_ref[...] += gate_pair(
            pair, parts_ref[spot, 0], parts_ref[spot, 1], parts_ref[spot, 2]
        )
        if spot < GATE_PAIRS - 1:
            own_ref[0] += project(peer, 0, pair, pair + 1)
    sent_ref[0] = (own_ref[0] + project(peer, 0, pair_count - 1)).astype(jnp.bfloat16)
    tile_copy(0).start()
    square_sum = jnp.sum(square_ref[...].T, axis=0, keepdims=True)
    square_out_ref[...] = jnp.broadcast_to(square_sum, square_out_ref.shape)
    square_copy = pltpu.make_async_remote_copy(
        src_ref=square_out_ref,
        dst_ref=square_in_ref,
        send_sem=square_send,
        recv_sem=square_recv,
        device_id={"tensor": peer},
        device_id_type=MESH,
    )
    square_copy.start()

    @pl.loop(1, tile_count)
    def _(tile):
        sent_ref[tile] = project(peer, tile).astype(jnp.bfloat16)
        tile_copy(tile).start()

    @pl.loop(0, tile_count)
    def _(tile):
        own_ref[tile] = project(tensor_index, tile)

    @pl.when(first_core)
    def _():
        totals_copy.wait_send()

    @pl.when(first_core | has_previous)
    def _():
        pltpu.make_async_copy(pass_ref, pass_ref, core_send).wait()

    @pl.when(has_next)
    def _():
        pltpu.make_async_copy(pass_ref, pass_ref, onward_send).wait()

    square_copy.wait()
    inner = 2 * heads * HEAD_DIM
    scale = lax.rsqrt((square_out_ref[0:1, :] + square_in_ref[0:1, :]) / inner + EPSILON)
    square_ref[...] = jnp.broadcast_to(scale, (LANES, STRETCH)).T

    @pl.loop(0, tile_count)
    def _(tile):
        tile_copy(tile).wait_recv()
        scales = square_ref[...]
        for side in range(TILE // LANES):
            start = pl.multiple_of(tile * TILE + side * LANES, LANES)
            columns = slice(side * LANES, (side + 1) * LANES)
            both = own_ref[tile, :, columns] + landed_ref[tile, :, columns].astype(jnp.float32)
            out_ref[:, pl.ds(start, LANES)] = (both * scales).astype(jnp.bfloat16)

    pltpu.make_async_copy(sent_ref, sent_ref, tile_send).wait()


def fused_on_device(
    span_count,
    signal,
    gate_branch,
    write_proj,
    read_proj,
    step_logits,
    valid_mask,
    stretch_band,
    band_offset,
    decay_log,
    step_offset,
    skip_gain,
    norm_gain,
    out_weight,
):
    heads = decay_log.shape[0]
    inner = heads * HEAD_DIM
    width = out_weight.shape[1]
    pair_count = heads // 2
    tile_count = width // 2 // TILE
    vmem = pl.BlockSpec(memory_space=pltpu.VMEM)
    hbm = pl.BlockSpec(memory_space=pl.ANY)
    f32, bf16 = jnp.float32, jnp.bfloat16
    return pl.pallas_call(
        functools.partial(fused_kernel, heads, span_count),
        out_shape=pltpu.VMEM((STRETCH, width // 2), bf16),
        in_specs=[hbm] * 13,
        out_specs=vmem,
        scratch_shapes=[
            pltpu.VMEM((inner, width), bf16),
            pltpu.VMEM((STRETCH, inner), bf16),
            pltpu.VMEM((STRETCH, inner), bf16),
            pltpu.VMEM((STRETCH, STATE), bf16),
            pltpu.VMEM((STRETCH, STATE), bf16),
            pltpu.VMEM((heads, STRETCH), f32),
            pltpu.VMEM((1, STRETCH), jnp.int32),
            pltpu.VMEM((1, 1), jnp.int32),
            pltpu.VMEM((BANDS, heads), f32),
            pltpu.VMEM((1, heads), f32),
            pltpu.VMEM((1, heads), f32),
            pltpu.VMEM((1, heads), f32),
            pltpu.VMEM((pair_count, LANES), f32),
            pltpu.VMEM((LANES, STRETCH), f32),
            pltpu.VMEM((8, LANES), f32),
            pltpu.VMEM((heads, STRETCH), f32),
            pltpu.VMEM((STRETCH, LANES), f32),
            pltpu.VMEM((STRETCH, LANES), f32),
            pltpu.VMEM((heads, STRETCH), f32),
            pltpu.VMEM((16, LANES), bf16),
            pltpu.VMEM((STRETCH, STRETCH), f32),
            pltpu.VMEM((STATE, STRETCH), bf16),
            pltpu.VMEM((pair_count, STATE, LANES), f32),
            pltpu.VMEM((-(-pair_count // 16) * 16, LANES), f32),
            pltpu.VMEM((-(-pair_count // 16) * 16, LANES), f32),
            pltpu.VMEM((STRETCH, inner), f32),
            pltpu.VMEM((STRETCH, inner), bf16),
            pltpu.VMEM((STRETCH, LANES), f32),
            pltpu.VMEM((pair_count, STATE, LANES), bf16),
            pltpu.VMEM((pair_count, STATE, LANES), bf16),
            pltpu.VMEM((pair_count, STATE, LANES), bf16),
            pltpu.VMEM((pair_count, STATE, LANES), bf16),
            pltpu.VMEM((tile_count, STRETCH, TILE), bf16),
            pltpu.VMEM((tile_count, STRETCH, TILE), f32),
            pltpu.VMEM((GATE_PAIRS, 3, STRETCH, LANES), f32),
            pltpu.VMEM((tile_count, STRETCH, TILE), bf16),
            pltpu.VMEM((8, STRETCH), f32),
            pltpu.VMEM((8, STRETCH), f32),
            pltpu.SemaphoreType.DMA((3,)),
            pltpu.SemaphoreType.DMA((10,)),
            pltpu.SemaphoreType.DMA,
            pltpu.SemaphoreType.DMA,
            pltpu.SemaphoreType.DMA,
            pltpu.SemaphoreType.DMA((pair_count // STATE_PAIRS + 1,)),
            pltpu.SemaphoreType.DMA,
            pltpu.SemaphoreType.DMA((pair_count * PIECES,)),
            pltpu.SemaphoreType.DMA,
            pltpu.SemaphoreType.DMA((tile_count,)),
            pltpu.SemaphoreType.DMA,
            pltpu.SemaphoreType.DMA,
        ],
        compiler_params=pltpu.CompilerParams(
            collective_id=0, has_side_effects=True, vmem_limit_bytes=60 * 1024 * 1024
        ),
    )(
        signal,
        gate_branch,
        write_proj,
        read_proj,
        step_logits,
        valid_mask[None, :],
        stretch_band[None, :],
        band_offset,
        decay_log[None, :],
        step_offset[None, :],
        skip_gain[None, :],
        norm_gain.reshape(pair_count, LANES),
        out_weight,
    )


def solution(mesh):
    placed = (
        P(("group", "scan", "band"), "tensor"),
        P(("group", "scan", "band"), "tensor"),
        P(("group", "scan", "band"), None),
        P(("group", "scan", "band"), None),
        P("tensor", ("group", "scan", "band")),
        P(("group", "scan", "band")),
        P(("group", "scan", "band")),
        P(None, "tensor"),
        P("tensor"),
        P("tensor"),
        P("tensor"),
        P("tensor"),
        P("tensor", None),
    )
    shape = dict(mesh.shape)
    places = shape["scan"] * shape["band"]

    def layer(*arrays):
        rows = arrays[0].shape[0] // (shape["group"] * places)
        heads = arrays[8].shape[0] // shape["tensor"]
        width = arrays[12].shape[1]
        fits = (
            shape["tensor"] == 2
            and shape["band"] == 2
            and shape["scan"] >= 2
            and rows == STRETCH
            and heads % (2 * STATE_PAIRS) == 0
            and heads % (2 * MIX_PAIRS) == 0
            and heads % (2 * GATE_PAIRS) == 0
            and 3 * heads < LANES
            and heads <= HEAD_DIM
            and width % (2 * TILE) == 0
        )
        member = on_device
        if fits:
            member = functools.partial(fused_on_device, shape["scan"])
        return mapped(member)(*arrays)

    def mapped(member):
        return jax.shard_map(
            member,
            mesh=mesh,
            in_specs=placed,
            out_specs=P(("group", "scan", "band"), "tensor"),
            check_vma=False,
        )

    return layer
```

```python
import functools

import jax
import jax.numpy as jnp
from jax import lax
from jax.experimental import pallas as pl
from jax.experimental.pallas import tpu as pltpu
from jax.sharding import PartitionSpec as P

HEAD_DIM = 64
STATE = 128
STRETCH = 256
BANDS = 12
INNER = 5120


EPSILON = 1e-05
HIGHEST = lax.Precision.HIGHEST


def step_sizes(step_logits, stretch_band, band_offset, step_offset):
    one_hot = (stretch_band[:, None] == jnp.arange(BANDS, dtype=jnp.int32)[None, :]).astype(
        jnp.float32
    )
    stretch_offset = jnp.dot(one_hot, band_offset, precision=HIGHEST)
    token_offset = jnp.repeat(stretch_offset, STRETCH, axis=0).T
    return jax.nn.softplus(step_logits + step_offset[:, None] + token_offset)


def combine(earlier, later_pair):
    return (
        earlier[0] + later_pair[0],
        jnp.exp(later_pair[0])[:, None, None] * earlier[1] + later_pair[1],
    )


def local_step(running_pair, member):
    return (combine(running_pair, member), running_pair)


def on_device(
    signal,
    gate_branch,
    write_proj,
    read_proj,
    step_logits,
    valid_mask,
    stretch_band,
    band_offset,
    decay_log,
    step_offset,
    skip_gain,
    norm_gain,
    out_weight,
):
    row_count = signal.shape[0]
    head_count = decay_log.shape[0]
    block_count = row_count // STRETCH
    step_size = step_sizes(step_logits, stretch_band, band_offset, step_offset)
    log_decay = step_size * (-jnp.exp(decay_log))[:, None]
    input_weight = step_size * valid_mask.astype(jnp.float32)[None, :]
    running = lax.associative_scan(
        jnp.add, log_decay.reshape(head_count, block_count, STRETCH), axis=2
    )
    weight_blocks = input_weight.reshape(head_count, block_count, STRETCH)
    signal_blocks = signal.reshape(block_count, STRETCH, head_count, HEAD_DIM)
    write_blocks = write_proj.reshape(block_count, STRETCH, STATE)
    read_blocks = read_proj.reshape(block_count, STRETCH, STATE)
    scores = jnp.einsum(
        "cin,cjn->cij", read_blocks, write_blocks, preferred_element_type=jnp.float32
    )
    lower_mask = jnp.arange(STRETCH)[:, None] >= jnp.arange(STRETCH)[None, :]
    span_logs = jnp.where(
        lower_mask[None, None], running[:, :, :, None] - running[:, :, None, :], -1e30
    )
    mixing = (jnp.exp(span_logs) * scores[None] * weight_blocks[:, :, None, :]).astype(jnp.bfloat16)
    local_out = jnp.einsum(
        "hcij,cjhp->cihp", mixing, signal_blocks, preferred_element_type=jnp.float32
    )
    tail_weight = jnp.exp(running[:, :, -1:] - running) * weight_blocks
    scaled = (
        signal_blocks.astype(jnp.float32) * jnp.transpose(tail_weight, (1, 2, 0))[:, :, :, None]
    ).astype(jnp.bfloat16)
    block_states = jnp.einsum(
        "cjhp,cjn->chpn", scaled, write_blocks, preferred_element_type=jnp.float32
    )
    block_decay = running[:, :, -1].T
    zero_state = jnp.zeros((head_count, HEAD_DIM, STATE), jnp.float32)
    zero_log = jnp.zeros((head_count,), jnp.float32)
    identity = (zero_log, zero_state)
    device_pair, segment_cumulative = lax.scan(local_step, identity, (block_decay, block_states))
    all_logs = lax.all_gather(device_pair[0][None], ("scan", "band"), axis=0, tiled=True)
    inclusive = lax.associative_scan(jnp.add, all_logs, axis=0)
    exclusive = inclusive - all_logs
    position = lax.axis_index(("scan", "band"))
    own_exclusive = lax.dynamic_index_in_dim(exclusive, position, 0, keepdims=False)
    shard_block = lax.all_gather(
        device_pair[1][None].astype(jnp.bfloat16), ("scan", "band"), axis=0, tiled=True
    ).astype(jnp.float32)
    how_many = shard_block.shape[0]
    sources = jnp.arange(how_many, dtype=jnp.int32)
    gap_logs = jnp.where((sources < position)[:, None], own_exclusive[None, :] - inclusive, -1e30)
    carry_state = zero_state + jnp.einsum(
        "kh,khpn->hpn", jnp.exp(gap_logs), shard_block, precision=HIGHEST
    )
    enter_state = (
        jnp.exp(segment_cumulative[0])[:, :, None, None] * carry_state[None] + segment_cumulative[1]
    )
    state_high = enter_state.astype(jnp.bfloat16)
    widened = lax.optimization_barrier(state_high).astype(jnp.float32)
    state_low = (enter_state - widened).astype(jnp.bfloat16)
    high_part = jnp.einsum(
        "cin,chpn->cihp", read_blocks, state_high, preferred_element_type=jnp.float32
    )
    low_part = jnp.einsum(
        "cin,chpn->cihp", read_blocks, state_low, preferred_element_type=jnp.float32
    )
    carried_out = jnp.transpose(jnp.exp(running), (1, 2, 0))[:, :, :, None] * (high_part + low_part)
    ssm_out = (local_out + carried_out).reshape(row_count, head_count, HEAD_DIM) + skip_gain[
        None, :, None
    ] * signal.reshape(row_count, head_count, HEAD_DIM).astype(jnp.float32)
    gated_out = ssm_out.reshape(row_count, head_count * HEAD_DIM) * jax.nn.silu(
        gate_branch.astype(jnp.float32)
    )
    square_total = lax.psum(jnp.sum(gated_out * gated_out, axis=1), "tensor")
    normed = (
        gated_out * lax.rsqrt(square_total / INNER + EPSILON)[:, None] * norm_gain[None, :]
    ).astype(jnp.bfloat16)
    own_columns = lax.psum_scatter(
        lax.dot_general(
            out_weight, normed, (((0,), (1,)), ((), ())), preferred_element_type=jnp.float32
        ).astype(jnp.bfloat16),
        "tensor",
        scatter_dimension=0,
        tiled=True,
    ).astype(jnp.float32)
    return own_columns.T.astype(jnp.bfloat16)


LOG2E = 1.4426950408889634
LANES = 128
STATE_PAIRS = 4
HEAD_START = 2
PIECES = 1
PIECE = STATE // PIECES
MIX_PAIRS = 2
GATE_PAIRS = 2
TILE = 128
MESH = pl.DeviceIdType.MESH


def fused_kernel(
    heads,
    span_count,
    signal_hbm,
    gate_hbm,
    write_hbm,
    read_hbm,
    logits_hbm,
    valid_hbm,
    band_hbm,
    offset_hbm,
    decay_hbm,
    bias_hbm,
    skip_hbm,
    gain_hbm,
    weight_hbm,
    out_ref,
    weight_ref,
    signal_ref,
    gate_ref,
    write_ref,
    read_ref,
    logits_ref,
    valid_ref,
    band_ref,
    offset_ref,
    decay_ref,
    bias_ref,
    skip_ref,
    gain_ref,
    padded_ref,
    params_ref,
    row_ref,
    run_ref,
    lead_ref,
    row_log_ref,
    skip_rows_ref,
    scores_ref,
    read_by_token_ref,
    state_ref,
    totals_ref,
    core_totals_ref,
    local_ref,
    normed_ref,
    square_ref,
    carry_ref,
    pass_ref,
    core_state_ref,
    entry_ref,
    sent_ref,
    own_ref,
    parts_ref,
    landed_ref,
    square_out_ref,
    square_in_ref,
    load_sem,
    small_sem,
    totals_send,
    totals_recv,
    core_send,
    core_recv,
    onward_send,
    arrival,
    tile_send,
    tile_recv,
    square_send,
    square_recv,
):
    pair_count = heads // 2
    scan_index = lax.axis_index("scan")
    band_index = lax.axis_index("band")
    tensor_index = lax.axis_index("tensor")
    first_core = band_index == 0
    second_core = band_index == 1
    first_chip = scan_index == 0
    has_previous = second_core & (scan_index > 0)
    has_next = second_core & (scan_index < span_count - 1)
    gets_entry = first_core & (scan_index > 0)
    peer = 1 - tensor_index
    other_core = {"band": 1 - band_index}
    following = {"scan": lax.rem(scan_index + 1, span_count)}
    previous = {"scan": lax.rem(scan_index + span_count - 1, span_count)}

    signal_load = pltpu.make_async_copy(signal_hbm, signal_ref, load_sem.at[2])
    gate_load = pltpu.make_async_copy(gate_hbm, gate_ref, load_sem.at[0])
    weight_load = pltpu.make_async_copy(weight_hbm, weight_ref, load_sem.at[1])
    small_loads = [
        pltpu.make_async_copy(source, target, small_sem.at[spot])
        for spot, (source, target) in enumerate(
            (
                (logits_hbm, logits_ref),
                (band_hbm, band_ref),
                (offset_hbm, offset_ref),
                (decay_hbm, decay_ref),
                (bias_hbm, bias_ref),
                (valid_hbm, valid_ref),
                (skip_hbm, skip_ref),
                (write_hbm, write_ref),
                (read_hbm, read_ref),
                (gain_hbm, gain_ref),
            )
        )
    ]
    for load in small_loads:
        load.start()
    signal_load.start()

    barrier = pltpu.get_barrier_semaphore()
    for target in (other_core, {"tensor": peer}):
        pl.semaphore_signal(barrier, inc=1, device_id=target, device_id_type=MESH)

    @pl.when(has_next)
    def _():
        pl.semaphore_signal(barrier, inc=1, device_id=following, device_id_type=MESH)

    @pl.when(has_previous)
    def _():
        pl.semaphore_signal(barrier, inc=1, device_id=previous, device_id_type=MESH)

    for load in small_loads[:7]:
        load.wait()

    params_ref[...] = jnp.zeros_like(params_ref)
    chosen = lax.broadcasted_iota(jnp.int32, (BANDS, heads), 0) == band_ref[...]
    params_ref[0:1, 0:heads] = bias_ref[...] + jnp.sum(
        jnp.where(chosen, offset_ref[...], 0.0), axis=0, keepdims=True
    )
    params_ref[1:2, 0:heads] = jnp.exp(decay_ref[...]) * -LOG2E
    params_ref[2:3, 0:heads] = skip_ref[...]
    head_columns = params_ref[...].T[0:heads]
    shifted = logits_ref[...] + head_columns[:, 0:1]
    step_size = jnp.maximum(shifted, 0.0) + jnp.log1p(jnp.exp(-jnp.abs(shifted)))
    lanes = lax.broadcasted_iota(jnp.int32, (STRETCH, LANES), 1)
    square_rows = lax.broadcasted_iota(jnp.int32, (STRETCH, STRETCH), 0)
    square_columns = lax.broadcasted_iota(jnp.int32, (STRETCH, STRETCH), 1)
    high = step_size.astype(jnp.bfloat16).astype(jnp.float32)
    middle = (step_size - high).astype(jnp.bfloat16).astype(jnp.float32)
    low = step_size - high - middle
    unused = jnp.zeros((LANES - 3 * heads, STRETCH), jnp.float32)
    sums = jnp.dot(
        jnp.concatenate([high, middle, low, unused], axis=0).astype(jnp.bfloat16),
        jnp.where(square_rows <= square_columns, 1.0, 0.0).astype(jnp.bfloat16),
        preferred_element_type=jnp.float32,
    )
    summed = sums[0:heads] + sums[heads : 2 * heads] + sums[2 * heads : 3 * heads]
    running = summed * head_columns[:, 1:2]
    in_weight = step_size * valid_ref[...].astype(jnp.float32)
    tail = jnp.exp2(running[:, STRETCH - 1 : STRETCH] - running) * in_weight
    row_ref[...] = running
    row_log_ref[...] = in_weight
    padded_ref[...] = jnp.zeros_like(padded_ref)
    padded_ref[0:heads, :] = tail
    padded_ref[HEAD_DIM : HEAD_DIM + heads, :] = running
    factors = padded_ref[...].T
    run_ref[...] = factors

    def three_parts(value):
        high = value.astype(jnp.bfloat16).astype(jnp.float32)
        rest = value - high
        middle = rest.astype(jnp.bfloat16).astype(jnp.float32)
        low = rest - middle
        packed = high + pltpu.roll(middle, heads, 1) + pltpu.roll(low, 2 * heads, 1)
        return packed.astype(jnp.bfloat16)

    last_running = pltpu.roll(factors[STRETCH - 16 : STRETCH], LANES - HEAD_DIM, 1)
    running_parts = three_parts(jnp.where(lanes[0:16] < heads, last_running, 0.0))
    part = lax.broadcasted_iota(jnp.int32, (LANES, 2 * LANES), 0)
    part = (
        part
        - jnp.where(part >= heads, heads, 0)
        - jnp.where(part >= 2 * heads, heads, 0)
    )
    head_of = lax.broadcasted_iota(jnp.int32, totals_ref.shape, 1)
    head_of = (
        head_of
        - jnp.where(head_of >= heads, heads, 0)
        - jnp.where(head_of >= 2 * heads, heads, 0)
    )
    own_pair = head_of // 2 == lax.broadcasted_iota(jnp.int32, totals_ref.shape, 0)
    last_parts = running_parts.astype(jnp.float32)[15:16, :]
    last_rows = (
        jnp.dot(
            jnp.where(own_pair, last_parts, 0.0).astype(jnp.bfloat16),
            jnp.where(
                part[:, 0:LANES] % 2
                == lax.broadcasted_iota(jnp.int32, (LANES, LANES), 1) // HEAD_DIM,
                1.0,
                0.0,
            ).astype(jnp.bfloat16),
            preferred_element_type=jnp.float32,
        )
    )
    totals_ref[...] = jnp.exp2(last_rows)
    small_loads[7].wait()
    write_turned = write_ref[...].astype(jnp.float32).T.astype(jnp.bfloat16)
    read_by_token_ref[...] = write_turned

    totals_copy = pltpu.make_async_remote_copy(
        src_ref=totals_ref,
        dst_ref=core_totals_ref,
        send_sem=totals_send,
        recv_sem=totals_recv,
        device_id=other_core,
        device_id_type=MESH,
    )

    def core_copy(start, count, group):
        members = pl.ds(start, count)
        return pltpu.make_async_remote_copy(
            src_ref=pass_ref.at[members],
            dst_ref=core_state_ref.at[members],
            send_sem=core_send,
            recv_sem=core_recv.at[group],
            device_id=other_core,
            device_id_type=MESH,
        )

    def onward_copy(pair, piece):
        rows = pl.ds(piece * PIECE, PIECE)
        return pltpu.make_async_remote_copy(
            src_ref=pass_ref.at[pair, rows],
            dst_ref=entry_ref.at[pair, rows],
            send_sem=onward_send,
            recv_sem=arrival.at[pair * PIECES + piece],
            device_id=following,
            device_id_type=MESH,
        )

    def entry_copy(pair):
        return pltpu.make_async_remote_copy(
            src_ref=entry_ref.at[pair],
            dst_ref=carry_ref.at[pair],
            send_sem=core_send,
            recv_sem=arrival.at[pair * PIECES],
            device_id=other_core,
            device_id_type=MESH,
        )

    def give_onward(pair, piece, carry):
        rows = slice(piece * PIECE, (piece + 1) * PIECE)
        onward = totals_ref[pl.ds(pair, 1), :] * carry + state_ref[pair, rows]
        pass_ref[pair, rows] = onward.astype(jnp.bfloat16)
        onward_copy(pair, piece).start()

    def first_chain_step(pair):
        own = core_state_ref[pair]
        carry_ref[pair] = own

        @pl.when(has_next)
        def _():
            for piece in range(PIECES):
                rows = slice(piece * PIECE, (piece + 1) * PIECE)
                give_onward(pair, piece, own[rows].astype(jnp.float32))

    def chain_step(pair):
        for piece in range(PIECES):
            rows = slice(piece * PIECE, (piece + 1) * PIECE)
            onward_copy(pair, piece).wait_recv()
            if piece == PIECES - 1:

                @pl.when(jnp.logical_not(has_next))
                def _():
                    entry_copy(pair).start()

            carry = core_totals_ref[pl.ds(pair, 1), :] * entry_ref[pair, rows].astype(
                jnp.float32
            ) + core_state_ref[pair, rows].astype(jnp.float32)
            carry_ref[pair, rows] = carry.astype(jnp.bfloat16)

            @pl.when(has_next)
            def _():
                give_onward(pair, piece, carry)
                if piece == PIECES - 1:
                    entry_copy(pair).start()

    def columns_of(pair):
        return pl.ds(pl.multiple_of(pair * LANES, LANES), LANES)

    narrow_side = lax.broadcasted_iota(jnp.int32, (LANES, LANES), 1) // HEAD_DIM
    narrow_index = part[:, 0:LANES] - narrow_side
    first_half = lanes < HEAD_DIM
    second_half = lanes >= HEAD_DIM

    def picker(index, pair):
        return jnp.where(index == 2 * pair, 1.0, 0.0).astype(jnp.bfloat16)

    def spread(values, index):
        return jnp.take_along_axis(values, index, axis=1, mode="promise_in_bounds")

    def pair_heads(pair):
        return 2 * pair + lanes // HEAD_DIM

    def state_pair(pair):
        columns = columns_of(pair)
        tail = spread(run_ref[...], pair_heads(pair))
        scaled = (signal_ref[:, columns].astype(jnp.float32) * tail).astype(jnp.bfloat16)
        state = jnp.dot(read_by_token_ref[...], scaled, preferred_element_type=jnp.float32)
        state_ref[pair] = state
        pass_ref[pair] = state.astype(jnp.bfloat16)


    def mix_pair(pair):
        columns = columns_of(pair)
        half = STRETCH // 2
        fed = signal_ref[:, columns]
        tops, bottoms, sides = [], [], []
        for side in range(2):
            row = row_ref[pl.ds(2 * pair + side, 1), :]
            most = row_log_ref[pl.ds(2 * pair + side, 1), :]
            run = spread(run_ref[...], jnp.full((STRETCH, LANES), HEAD_DIM + 2 * pair + side, jnp.int32))
            near = jnp.exp2(jnp.minimum(run[0:half] - row[:, 0:half], most[:, 0:half]))
            far = jnp.exp2(run[half:] - row[:, 0:half])
            late = jnp.exp2(jnp.minimum(run[half:] - row[:, half:], most[:, half:]))
            tops.append((near * scores_ref[0:half, 0:half]).astype(jnp.bfloat16))
            bottoms.append((far * scores_ref[half:, 0:half]).astype(jnp.bfloat16))
            bottoms.append((late * scores_ref[half:, half:]).astype(jnp.bfloat16))
            sides.append(jnp.where(first_half if side == 0 else second_half, fed, jnp.zeros_like(fed)))
        local_ref[0:half, columns] = jnp.dot(
            jnp.concatenate(tops, axis=1),
            jnp.concatenate([sides[0][0:half], sides[1][0:half]], axis=0),
            preferred_element_type=jnp.float32,
        )
        local_ref[half:, columns] = jnp.dot(
            jnp.concatenate(bottoms, axis=1),
            jnp.concatenate(sides, axis=0),
            preferred_element_type=jnp.float32,
        )

    def gate_parts(pair):
        columns = columns_of(pair)
        skip = jnp.dot(
            skip_rows_ref[...], picker(narrow_index, pair), preferred_element_type=jnp.float32
        )
        own = local_ref[:, columns] + skip[0:1, :] * signal_ref[:, columns].astype(jnp.float32)
        gate = gate_ref[:, columns].astype(jnp.float32)
        lead = spread(lead_ref[...], HEAD_DIM + pair_heads(pair))
        return own, lead, gate / (1.0 + jnp.exp(-gate))

    def gate_pair(pair, own, lead, gate):
        carried = jnp.dot(read_ref[...], carry_ref[pair], preferred_element_type=jnp.float32)
        gated = (own + lead * carried) * gate
        normed_ref[:, columns_of(pair)] = (gated * gain_ref[pl.ds(pair, 1), :]).astype(
            jnp.bfloat16
        )
        return gated * gated

    def state_pairs(start, count):
        for member in range(count):
            state_pair(start + member)

    def core_copies(start, count, group):
        @pl.when(first_core)
        def _():
            core_copy(start, count, group).start()

    def first_chain_steps(start, count, group):
        core_copy(start, count, group).wait_recv()
        for member in range(count):
            first_chain_step(start + member)

    group_count = pair_count // STATE_PAIRS
    signal_load.wait()
    state_pairs(0, HEAD_START)
    pl.semaphore_wait(barrier, 2 + jnp.where(has_next, 1, 0) + jnp.where(has_previous, 1, 0))
    core_copies(0, HEAD_START, 0)

    @pl.when(first_core)
    def _():
        totals_copy.start()

    gate_load.start()
    weight_load.start()
    state_pairs(HEAD_START, STATE_PAIRS - HEAD_START)
    core_copies(HEAD_START, STATE_PAIRS - HEAD_START, 1)

    @pl.when(second_core & first_chip)
    def _():
        first_chain_steps(0, HEAD_START, 0)

    @pl.loop(1, group_count)
    def _(group):
        start = group * STATE_PAIRS
        state_pairs(start, STATE_PAIRS)
        core_copies(start, STATE_PAIRS, group + 1)

        @pl.when(second_core & first_chip & (group == 1))
        def _():
            first_chain_steps(HEAD_START, STATE_PAIRS - HEAD_START, 1)

        @pl.when(second_core & first_chip & (group > 1))
        def _():
            first_chain_steps(start - STATE_PAIRS, STATE_PAIRS, group)

    @pl.when(second_core & first_chip)
    def _():
        first_chain_steps(pair_count - STATE_PAIRS, STATE_PAIRS, group_count)

    @pl.when(second_core)
    def _():
        totals_copy.wait_recv()

    skip_rows_ref[...] = three_parts(jnp.broadcast_to(params_ref[2:3, :], (16, LANES)))
    lead_ref[...] = jnp.exp2(run_ref[...])
    in_weights = row_log_ref[...]
    weight_log = jnp.where(in_weights > 0.0, jnp.log(in_weights) * LOG2E, -1e30)
    row_log_ref[...] = weight_log
    row_ref[...] = row_ref[...] - weight_log
    for load in small_loads[8:]:
        load.wait()
    scores = jnp.dot(read_ref[...], read_by_token_ref[...], preferred_element_type=jnp.float32)
    scores_ref[...] = jnp.where(square_columns <= square_rows, scores, 0.0)
    square_ref[...] = jnp.zeros_like(square_ref)
    @pl.when(first_core & first_chip)
    def _():
        carry_ref[...] = jnp.zeros_like(carry_ref)

    @pl.loop(0, pair_count // MIX_PAIRS)
    def _(group):
        @pl.when(has_previous & has_next)
        def _():
            @pl.when(group == 0)
            def _():
                core_copy(0, HEAD_START, 0).wait_recv()

            @pl.when(group == 1)
            def _():
                core_copy(HEAD_START, STATE_PAIRS - HEAD_START, 1).wait_recv()

            @pl.when((group > 1) & (group % 2 == 0))
            def _():
                core_copy(group * MIX_PAIRS, STATE_PAIRS, group // 2 + 1).wait_recv()

            for member in range(MIX_PAIRS):
                chain_step(group * MIX_PAIRS + member)

        for member in range(MIX_PAIRS):
            mix_pair(group * MIX_PAIRS + member)

    gate_load.wait()
    last_step = has_previous & (scan_index == span_count - 1)

    @pl.when(last_step)
    def _():
        core_copy(0, HEAD_START, 0).wait_recv()
        core_copy(HEAD_START, STATE_PAIRS - HEAD_START, 1).wait_recv()

        @pl.loop(1, group_count)
        def _(group):
            core_copy(group * STATE_PAIRS, STATE_PAIRS, group + 1).wait_recv()

    def await_carry(start, count):
        @pl.when(last_step)
        def _():
            for member in range(count):
                chain_step(start + member)

        @pl.when(gets_entry)
        def _():
            for member in range(count):
                entry_copy(start + member).wait_recv()

    @pl.loop(0, pair_count // GATE_PAIRS - 1)
    def _(group):
        start = group * GATE_PAIRS
        await_carry(start, GATE_PAIRS)
        squares = square_ref[...]
        for member in range(GATE_PAIRS):
            squares = squares + gate_pair(start + member, *gate_parts(start + member))
        square_ref[...] = squares

    weight_load.wait()
    own_width = out_ref.shape[1]
    tile_count = own_width // TILE

    def tile_copy(tile):
        return pltpu.make_async_remote_copy(
            src_ref=sent_ref.at[tile],
            dst_ref=landed_ref.at[tile],
            send_sem=tile_send,
            recv_sem=tile_recv.at[tile],
            device_id={"tensor": peer},
            device_id_type=MESH,
        )

    def project(owner, tile, first=0, last=pair_count):
        start = pl.multiple_of(owner * own_width + tile * TILE, LANES)
        rows = slice(first * LANES, last * LANES)
        return jnp.dot(
            normed_ref[:, rows],
            weight_ref[rows, pl.ds(start, TILE)],
            preferred_element_type=jnp.float32,
        )

    early = pair_count - GATE_PAIRS
    for spot in range(GATE_PAIRS):
        for kind, value in enumerate(gate_parts(early + spot)):
            parts_ref[spot, kind] = value
    own_ref[0] = project(peer, 0, 0, early)
    for spot in range(GATE_PAIRS):
        pair = early + spot
        await_carry(pair, 1)
        square_ref[...] += gate_pair(
            pair, parts_ref[spot, 0], parts_ref[spot, 1], parts_ref[spot, 2]
        )
        if spot < GATE_PAIRS - 1:
            own_ref[0] += project(peer, 0, pair, pair + 1)
    sent_ref[0] = (own_ref[0] + project(peer, 0, pair_count - 1)).astype(jnp.bfloat16)
    tile_copy(0).start()
    square_sum = jnp.sum(square_ref[...].T, axis=0, keepdims=True)
    square_out_ref[...] = jnp.broadcast_to(square_sum, square_out_ref.shape)
    square_copy = pltpu.make_async_remote_copy(
        src_ref=square_out_ref,
        dst_ref=square_in_ref,
        send_sem=square_send,
        recv_sem=square_recv,
        device_id={"tensor": peer},
        device_id_type=MESH,
    )
    square_copy.start()

    @pl.loop(1, tile_count)
    def _(tile):
        sent_ref[tile] = project(peer, tile).astype(jnp.bfloat16)
        tile_copy(tile).start()

    @pl.loop(0, tile_count)
    def _(tile):
        own_ref[tile] = project(tensor_index, tile)

    @pl.when(first_core)
    def _():
        totals_copy.wait_send()

    @pl.when(first_core | has_previous)
    def _():
        pltpu.make_async_copy(pass_ref, pass_ref, core_send).wait()

    @pl.when(has_next)
    def _():
        pltpu.make_async_copy(pass_ref, pass_ref, onward_send).wait()

    square_copy.wait()
    inner = 2 * heads * HEAD_DIM
    scale = lax.rsqrt((square_out_ref[0:1, :] + square_in_ref[0:1, :]) / inner + EPSILON)
    square_ref[...] = jnp.broadcast_to(scale, (LANES, STRETCH)).T

    @pl.loop(0, tile_count)
    def _(tile):
        tile_copy(tile).wait_recv()
        scales = square_ref[...]
        for side in range(TILE // LANES):
            start = pl.multiple_of(tile * TILE + side * LANES, LANES)
            columns = slice(side * LANES, (side + 1) * LANES)
            both = own_ref[tile, :, columns] + landed_ref[tile, :, columns].astype(jnp.float32)
            out_ref[:, pl.ds(start, LANES)] = (both * scales).astype(jnp.bfloat16)

    pltpu.make_async_copy(sent_ref, sent_ref, tile_send).wait()


def fused_on_device(
    span_count,
    signal,
    gate_branch,
    write_proj,
    read_proj,
    step_logits,
    valid_mask,
    stretch_band,
    band_offset,
    decay_log,
    step_offset,
    skip_gain,
    norm_gain,
    out_weight,
):
    heads = decay_log.shape[0]
    inner = heads * HEAD_DIM
    width = out_weight.shape[1]
    pair_count = heads // 2
    tile_count = width // 2 // TILE
    vmem = pl.BlockSpec(memory_space=pltpu.VMEM)
    hbm = pl.BlockSpec(memory_space=pl.ANY)
    f32, bf16 = jnp.float32, jnp.bfloat16
    return pl.pallas_call(
        functools.partial(fused_kernel, heads, span_count),
        out_shape=pltpu.VMEM((STRETCH, width // 2), bf16),
        in_specs=[hbm] * 13,
        out_specs=vmem,
        scratch_shapes=[
            pltpu.VMEM((inner, width), bf16),
            pltpu.VMEM((STRETCH, inner), bf16),
            pltpu.VMEM((STRETCH, inner), bf16),
            pltpu.VMEM((STRETCH, STATE), bf16),
            pltpu.VMEM((STRETCH, STATE), bf16),
            pltpu.VMEM((heads, STRETCH), f32),
            pltpu.VMEM((1, STRETCH), jnp.int32),
            pltpu.VMEM((1, 1), jnp.int32),
            pltpu.VMEM((BANDS, heads), f32),
            pltpu.VMEM((1, heads), f32),
            pltpu.VMEM((1, heads), f32),
            pltpu.VMEM((1, heads), f32),
            pltpu.VMEM((pair_count, LANES), f32),
            pltpu.VMEM((LANES, STRETCH), f32),
            pltpu.VMEM((8, LANES), f32),
            pltpu.VMEM((heads, STRETCH), f32),
            pltpu.VMEM((STRETCH, LANES), f32),
            pltpu.VMEM((STRETCH, LANES), f32),
            pltpu.VMEM((heads, STRETCH), f32),
            pltpu.VMEM((16, LANES), bf16),
            pltpu.VMEM((STRETCH, STRETCH), f32),
            pltpu.VMEM((STATE, STRETCH), bf16),
            pltpu.VMEM((pair_count, STATE, LANES), f32),
            pltpu.VMEM((-(-pair_count // 16) * 16, LANES), f32),
            pltpu.VMEM((-(-pair_count // 16) * 16, LANES), f32),
            pltpu.VMEM((STRETCH, inner), f32),
            pltpu.VMEM((STRETCH, inner), bf16),
            pltpu.VMEM((STRETCH, LANES), f32),
            pltpu.VMEM((pair_count, STATE, LANES), bf16),
            pltpu.VMEM((pair_count, STATE, LANES), bf16),
            pltpu.VMEM((pair_count, STATE, LANES), bf16),
            pltpu.VMEM((pair_count, STATE, LANES), bf16),
            pltpu.VMEM((tile_count, STRETCH, TILE), bf16),
            pltpu.VMEM((tile_count, STRETCH, TILE), f32),
            pltpu.VMEM((GATE_PAIRS, 3, STRETCH, LANES), f32),
            pltpu.VMEM((tile_count, STRETCH, TILE), bf16),
            pltpu.VMEM((8, STRETCH), f32),
            pltpu.VMEM((8, STRETCH), f32),
            pltpu.SemaphoreType.DMA((3,)),
            pltpu.SemaphoreType.DMA((10,)),
            pltpu.SemaphoreType.DMA,
            pltpu.SemaphoreType.DMA,
            pltpu.SemaphoreType.DMA,
            pltpu.SemaphoreType.DMA((pair_count // STATE_PAIRS + 1,)),
            pltpu.SemaphoreType.DMA,
            pltpu.SemaphoreType.DMA((pair_count * PIECES,)),
            pltpu.SemaphoreType.DMA,
            pltpu.SemaphoreType.DMA((tile_count,)),
            pltpu.SemaphoreType.DMA,
            pltpu.SemaphoreType.DMA,
        ],
        compiler_params=pltpu.CompilerParams(
            collective_id=0, has_side_effects=True, vmem_limit_bytes=60 * 1024 * 1024
        ),
    )(
        signal,
        gate_branch,
        write_proj,
        read_proj,
        step_logits,
        valid_mask[None, :],
        stretch_band[None, :],
        band_offset,
        decay_log[None, :],
        step_offset[None, :],
        skip_gain[None, :],
        norm_gain.reshape(pair_count, LANES),
        out_weight,
    )


def solution(mesh):
    placed = (
        P(("group", "scan", "band"), "tensor"),
        P(("group", "scan", "band"), "tensor"),
        P(("group", "scan", "band"), None),
        P(("group", "scan", "band"), None),
        P("tensor", ("group", "scan", "band")),
        P(("group", "scan", "band")),
        P(("group", "scan", "band")),
        P(None, "tensor"),
        P("tensor"),
        P("tensor"),
        P("tensor"),
        P("tensor"),
        P("tensor", None),
    )
    shape = dict(mesh.shape)
    places = shape["scan"] * shape["band"]

    def layer(*arrays):
        rows = arrays[0].shape[0] // (shape["group"] * places)
        heads = arrays[8].shape[0] // shape["tensor"]
        width = arrays[12].shape[1]
        fits = (
            shape["tensor"] == 2
            and shape["band"] == 2
            and shape["scan"] >= 2
            and rows == STRETCH
            and heads % (2 * STATE_PAIRS) == 0
            and heads % (2 * MIX_PAIRS) == 0
            and heads % (2 * GATE_PAIRS) == 0
            and 3 * heads < LANES
            and heads <= HEAD_DIM
            and width % (2 * TILE) == 0
        )
        member = on_device
        if fits:
            member = functools.partial(fused_on_device, shape["scan"])
        return mapped(member)(*arrays)

    def mapped(member):
        return jax.shard_map(
            member,
            mesh=mesh,
            in_specs=placed,
            out_specs=P(("group", "scan", "band"), "tensor"),
            check_vma=False,
        )

    return layer
```
